32 devices in a mesh: gz: 8 (over z, y), gy: 4 (over x, core).
Axes of the slice: x: 2, y: 2, z: 4, core: 2. Of those that a mesh axis runs over, the one named last changes fastest.
Arguments:
- noisy_field: bfloat16 [32, 16, 256, 256], P(None, 'gz', 'gy'), may hold values from -6 to 6
- spectral_weights: bfloat16 [2, 2, 6912, 32, 32], P(None, None, 'gz', None, 'gy'), may hold values from -0.75 to 0.75
- skip_weights: bfloat16 [2, 32, 32], replicated, may hold values from -1 to 1
- in_weights: bfloat16 [2, 256, 32], replicated, may hold values from -1 to 1
- in_bias: float32 [2, 256], replicated, may hold values from -3 to 3
- out_weights: bfloat16 [2, 32, 256], replicated, may hold values from -0.375 to 0.375
Outputs:
- refined: bfloat16 [32, 16, 256, 256], P(None, 'gz', 'gy')
The draws below stay inside these ranges and needn't reach their ends.
All inputs are finite; a program needn't handle non-finite values.
Results may differ from the reference program's by a relative error of at most 0.023.
Values may be sent and summed in bfloat16 or wider, within the bound.
A program may use at most 128 MiB of HBM per device.

```python
import math
import jax
import jax.numpy as jnp
from jax import lax

W = 32
HID = 256
NX = 256
MX = 12
KY = 24
KZ = 24
LAYERS = 2
NY = 256
NZ = 16
KMODES = 6912


def block_scale(own_key, shape, shards, smallest, largest):
    def one(axis_at, parts):
        heights = jax.random.uniform(jax.random.fold_in(jax.random.fold_in(own_key, 6), axis_at), (parts,), jnp.float32, smallest / len(shards), largest / len(shards))
        return jnp.repeat(jnp.exp(heights), shape[axis_at] // parts).reshape((-1,) + (1,) * (len(shape) - axis_at - 1))

    gain = one(*shards[0])
    for cut in shards[1:]:
        gain = gain * one(*cut)
    return gain


def gaussian(rng, dims, deviation, bound, shards=(), kind=jnp.bfloat16):
    array = jax.random.normal(rng, dims, jnp.float32) * deviation
    if len(shards) > 0:
        array = block_scale(rng, dims, shards, -0.22, 0.18) * array
    return jnp.clip(array, min=-bound, max=bound).astype(kind)


def setup_inputs(seed: int = 0) -> dict:
    keys = jax.random.split(jax.random.key(seed), 7)
    return {
        "noisy_field": gaussian(keys[0], (W, NZ, NY, NX), 1.0, 6.0, ((1, 8), (2, 4))),
        "spectral_weights": gaussian(keys[1], (LAYERS, 2, KMODES, W, W), (2 * W) ** -0.5, 0.75, ((2, 8), (4, 4))),
        "skip_weights": gaussian(keys[2], (LAYERS, W, W), W ** -0.5, 1.0),
        "in_weights": gaussian(keys[3], (LAYERS, HID, W), W ** -0.5, 1.0),
        "in_bias": gaussian(keys[4], (LAYERS, HID), 0.5, 3.0, (), jnp.float32),
        "out_weights": gaussian(keys[5], (LAYERS, W, HID), HID ** -0.5, 0.375),
    }


def angles(number, positions, length, signed):
    kept = jnp.arange(number, dtype=jnp.int32)
    if signed:
        kept = jnp.where(kept < number // 2, kept, kept - number)
    phases = jnp.mod(kept[:, None] * positions[None, :], length)
    radians = 2.0 * math.pi / length * phases.astype(jnp.float32)
    return (jnp.cos(radians), jnp.sin(radians))

def forward_table(x_positions, length):
    x_cosine, x_sine = angles(MX, x_positions, length, False)
    return jnp.concatenate([x_cosine, -x_sine], 0).T.astype(jnp.bfloat16)

def inverse_table(x_positions, length):
    x_cosine, x_sine = angles(MX, x_positions, length, False)
    factor = jnp.where(jnp.arange(MX) == 0, jnp.float32(1.0), jnp.float32(2.0))
    inverse_scale = 1.0 / math.sqrt(2.0 * KMODES)
    return jnp.concatenate([x_cosine * factor[:, None], -x_sine * factor[:, None]], 0) * inverse_scale

def reference(noisy_field, spectral_weights, skip_weights, in_weights, in_bias, out_weights):
    highest = lax.Precision.HIGHEST
    z_positions = jnp.arange(NZ, dtype=jnp.int32)
    y_positions = jnp.arange(NY, dtype=jnp.int32)
    x_positions = jnp.arange(NX, dtype=jnp.int32)
    z_cosine, z_sine = angles(KZ, z_positions, NZ, True)
    y_cosine, y_sine = angles(KY, y_positions, NY, True)
    table_fwd = forward_table(x_positions, NX)
    table_inv = inverse_table(x_positions, NX)
    forward_scale = 1.0 / math.sqrt(NX * NY * NZ)
    current = noisy_field
    for layer_idx in range(LAYERS):

        def accumulate(running, zindex):
            zplane = lax.dynamic_index_in_dim(current, zindex, 1, keepdims=False)
            xtransform = jnp.dot(zplane.reshape(W * NY, NX), table_fwd, preferred_element_type=jnp.float32).reshape(W, NY, 2, MX)
            along_real = xtransform[:, :, 0]
            along_imag = xtransform[:, :, 1]
            ypass_real = (jnp.einsum('wym,ky->wkm', along_real, y_cosine, precision=highest) + jnp.einsum('wym,ky->wkm', along_imag, y_sine, precision=highest)) * forward_scale
            ypass_imag = (jnp.einsum('wym,ky->wkm', along_imag, y_cosine, precision=highest) - jnp.einsum('wym,ky->wkm', along_real, y_sine, precision=highest)) * forward_scale
            zc_column = lax.dynamic_index_in_dim(z_cosine, zindex, 1, keepdims=False)[None, :, None, None]
            zs_column = lax.dynamic_index_in_dim(z_sine, zindex, 1, keepdims=False)[None, :, None, None]
            sum_real, sum_imag = running
            sum_real = sum_real + ypass_real[:, None] * zc_column + ypass_imag[:, None] * zs_column
            sum_imag = sum_imag + ypass_imag[:, None] * zc_column - ypass_real[:, None] * zs_column
            return ((sum_real, sum_imag), None)
        zeros_init = jnp.zeros((W, KZ, KY, MX), jnp.float32)
        (sum_real, sum_imag), _ = lax.scan(accumulate, (zeros_init, zeros_init), z_positions)
        spec_real = lax.optimization_barrier(sum_real.reshape(W, KMODES).astype(jnp.bfloat16)).astype(jnp.float32)
        spec_imag = lax.optimization_barrier(sum_imag.reshape(W, KMODES).astype(jnp.bfloat16)).astype(jnp.float32)
        coefficients = spectral_weights[layer_idx].astype(jnp.float32)
        modal_real = jnp.einsum('ik,kio->ok', spec_real, coefficients[0], precision=highest) - jnp.einsum('ik,kio->ok', spec_imag, coefficients[1], precision=highest)
        modal_imag = jnp.einsum('ik,kio->ok', spec_real, coefficients[1], precision=highest) + jnp.einsum('ik,kio->ok', spec_imag, coefficients[0], precision=highest)
        modal_real = lax.optimization_barrier(modal_real.astype(jnp.bfloat16)).astype(jnp.float32).reshape(W, KZ, KY * MX)
        modal_imag = lax.optimization_barrier(modal_imag.astype(jnp.bfloat16)).astype(jnp.float32).reshape(W, KZ, KY * MX)
        skip_matrix = skip_weights[layer_idx]
        lift_matrix = in_weights[layer_idx]
        bias_column = in_bias[layer_idx][:, None]
        down_matrix = out_weights[layer_idx]
        layer_input = current

        def plane_output(zindex):
            zc_column = lax.dynamic_index_in_dim(z_cosine, zindex, 1, keepdims=False)
            zs_column = lax.dynamic_index_in_dim(z_sine, zindex, 1, keepdims=False)
            plane_real = jnp.einsum('wkq,k->wq', modal_real, zc_column, precision=highest) - jnp.einsum('wkq,k->wq', modal_imag, zs_column, precision=highest)
            plane_imag = jnp.einsum('wkq,k->wq', modal_real, zs_column, precision=highest) + jnp.einsum('wkq,k->wq', modal_imag, zc_column, precision=highest)
            plane_real = plane_real.reshape(W, KY, MX)
            plane_imag = plane_imag.reshape(W, KY, MX)
            rows_real = jnp.einsum('wkm,ky->wym', plane_real, y_cosine, precision=highest) - jnp.einsum('wkm,ky->wym', plane_imag, y_sine, precision=highest)
            rows_imag = jnp.einsum('wkm,ky->wym', plane_real, y_sine, precision=highest) + jnp.einsum('wkm,ky->wym', plane_imag, y_cosine, precision=highest)
            stacked = jnp.stack([rows_real, rows_imag], axis=2).reshape(W * NY, 2 * MX)
            spatial = jnp.dot(stacked, table_inv, precision=highest).reshape(W, NY * NX)
            zplane = lax.dynamic_index_in_dim(layer_input, zindex, 1, keepdims=False).reshape(W, NY * NX)
            mixed_sum = spatial + jnp.dot(skip_matrix, zplane, preferred_element_type=jnp.float32)
            before = jnp.dot(lift_matrix, mixed_sum.astype(jnp.bfloat16), preferred_element_type=jnp.float32) + bias_column
            hidden = jax.nn.gelu(before, approximate=False).astype(jnp.bfloat16)
            result = mixed_sum + jnp.dot(down_matrix, hidden, preferred_element_type=jnp.float32)
            return result.astype(jnp.bfloat16).reshape(W, NY, NX)
        planes_out = lax.map(plane_output, z_positions)
        current = jnp.moveaxis(planes_out, 0, 1)
    return current
```

```python
import functools
import math

import jax
import jax.numpy as jnp
from jax import lax
from jax.experimental import pallas as pl
from jax.experimental.pallas import tpu as pltpu
from jax.sharding import PartitionSpec as P
import ml_dtypes
import numpy as np

MX = 12
KY = 24
KZ = 24
KP = KY // 2
LANES = 128
ROWS = 32
F32 = jnp.float32
BF16 = jnp.bfloat16


def angles(number, positions, length, signed):
    kept = jnp.arange(number, dtype=jnp.int32)
    if signed:
        kept = jnp.where(kept < number // 2, kept, kept - number)
    phases = jnp.mod(kept[:, None] * positions[None, :], length)
    radians = 2.0 * math.pi / length * phases.astype(jnp.float32)
    return (jnp.cos(radians), jnp.sin(radians))


def forward_table(length):
    cosine, sine = angles(MX, jnp.arange(length, dtype=jnp.int32), length, False)
    part = jnp.concatenate([cosine, -sine, -sine, -cosine], 0)
    table = jnp.concatenate([part, part], 0).T.astype(BF16)
    return jnp.pad(table, ((0, 0), (0, LANES - 8 * MX)))


def inverse_table(length):
    cosine, sine = angles(MX, jnp.arange(length, dtype=jnp.int32), length, False)
    factor = jnp.where(jnp.arange(MX) == 0, F32(1.0), F32(2.0))[:, None]
    scale = 1.0 / math.sqrt(2.0 * KZ * KY * MX)
    half = jnp.concatenate([cosine * factor, -sine * factor], 0) * scale
    table = jnp.concatenate([half] * 4, 0).astype(BF16)
    return jnp.pad(table, ((0, LANES - 8 * MX), (0, 0)))


def y_weights(positions, length):
    cosine, sine = angles(KY, positions, length, True)
    both = jnp.stack([cosine, sine], -1).transpose(1, 0, 2)
    lanes = jnp.repeat(both.reshape(positions.shape[0], KP, 4), 2 * MX, axis=2)
    return jnp.pad(lanes, ((0, 0), (0, 0), (0, LANES - 8 * MX)))


def gelu(value):
    return 0.5 * value * (1.0 + lax.erf(value * F32(math.sqrt(0.5))))


def accumulate_modes(along, weight_ref, modes_ref):
    rows, channels = along.shape[0], along.shape[1]

    @pl.when(pl.program_id(1) == 0)
    def _():
        modes_ref[...] = jnp.zeros_like(modes_ref)

    for kp in range(KP):
        total = along[0] * weight_ref[0, kp : kp + 1, :]
        for y in range(1, rows):
            total = total + along[y] * weight_ref[y, kp : kp + 1, :]
        modes_ref[0, kp] += total


def forward_kernel(field_ref, weight_ref, table_ref, modes_ref):
    rows, channels, length = field_ref.shape
    flat = field_ref[...].reshape(rows * channels, length)
    along = jnp.dot(flat, table_ref[...], preferred_element_type=F32)
    accumulate_modes(along.reshape(rows, channels, LANES), weight_ref, modes_ref)


def layer_body(
    field_ref, planes_ref, weight_ref, inverse_ref, skip_ref, lift_ref, bias_ref, down_ref, out_ref
):
    rows, channels, length = field_ref.shape
    parts = []
    for y in range(rows):
        total = planes_ref[0, 0] * weight_ref[y, 0:1, :]
        for kp in range(1, KP):
            total = total + planes_ref[0, kp] * weight_ref[y, kp : kp + 1, :]
        parts.append(total.astype(BF16))
    stacked = jnp.concatenate(parts, 0)
    spatial = jnp.dot(stacked, inverse_ref[...], preferred_element_type=F32)
    wide_spatial = jnp.concatenate(
        [spatial[y * channels : (y + 1) * channels] for y in range(rows)], 1
    )
    wide_field = jnp.concatenate([field_ref[y] for y in range(rows)], 1)
    mixed = wide_spatial + jnp.dot(skip_ref[...], wide_field, preferred_element_type=F32)
    before = jnp.dot(lift_ref[...], mixed.astype(BF16), preferred_element_type=F32)
    hidden = gelu(before + bias_ref[...]).astype(BF16)
    result = mixed + jnp.dot(down_ref[...], hidden, preferred_element_type=F32)
    result = result.astype(BF16)
    for y in range(rows):
        out_ref[y] = result[:, y * length : (y + 1) * length]


def middle_kernel(
    field_ref, planes_ref, weight_ref, inverse_ref, skip_ref, lift_ref, bias_ref, down_ref,
    table_ref, out_ref, modes_ref,
):
    layer_body(
        field_ref, planes_ref, weight_ref, inverse_ref, skip_ref, lift_ref, bias_ref, down_ref,
        out_ref,
    )
    forward_kernel(out_ref, weight_ref, table_ref, modes_ref)


def whole(shape):
    return pl.BlockSpec(shape, lambda z, y: (0,) * len(shape))


def run_forward(field, weights_y, table, planes):
    total, channels, length = field.shape
    steps = total // planes // ROWS
    return pl.pallas_call(
        forward_kernel,
        grid=(planes, steps),
        in_specs=[
            pl.BlockSpec((ROWS, channels, length), lambda z, y: (z * steps + y, 0, 0)),
            pl.BlockSpec((ROWS, KP, LANES), lambda z, y: (y, 0, 0)),
            whole(table.shape),
        ],
        out_specs=pl.BlockSpec((1, KP, channels, LANES), lambda z, y: (z, 0, 0, 0)),
        out_shape=jax.ShapeDtypeStruct((planes, KP, channels, LANES), F32),
        name="forward_modes",
    )(field, weights_y, table)


def run_layer(field, plane_modes, weights_y, inverse, skip, lift, bias, down, table):
    total, channels, length = field.shape
    planes = plane_modes.shape[0]
    steps = total // planes // ROWS
    field_spec = pl.BlockSpec((ROWS, channels, length), lambda z, y: (z * steps + y, 0, 0))
    modes_spec = pl.BlockSpec((1, KP, channels, LANES), lambda z, y: (z, 0, 0, 0))
    field_shape = jax.ShapeDtypeStruct(field.shape, BF16)
    modes_shape = jax.ShapeDtypeStruct(plane_modes.shape, F32)
    args = [field, plane_modes, weights_y, inverse, skip, lift, bias, down]
    specs = [
        field_spec,
        modes_spec,
        pl.BlockSpec((ROWS, KP, LANES), lambda z, y: (y, 0, 0)),
        whole(inverse.shape),
        whole(skip.shape),
        whole(lift.shape),
        whole(bias.shape),
        whole(down.shape),
    ]
    if table is None:
        return pl.pallas_call(
            layer_body,
            grid=(planes, steps),
            in_specs=specs,
            out_specs=field_spec,
            out_shape=field_shape,
            name="last_layer",
        )(*args)
    return pl.pallas_call(
        middle_kernel,
        grid=(planes, steps),
        in_specs=specs + [whole(table.shape)],
        out_specs=[field_spec, modes_spec],
        out_shape=[field_shape, modes_shape],
        name="middle_layer",
    )(*args, table)


def fold_modes(modes, scale):
    planes, _, channels, _ = modes.shape
    split = modes[..., : 8 * MX].reshape(planes, KP, channels, 2, 2, 2, MX)
    folded = (split[:, :, :, :, 0] + split[:, :, :, :, 1]) * scale
    ordered = folded.transpose(0, 4, 2, 1, 3, 5)
    return ordered.reshape(planes * 2, channels, KY * MX)


def unfold_modes(rows, planes):
    channels = rows.shape[1]
    real, imag = (
        rows.astype(F32).reshape(planes, 2, channels, KP, 2, MX)[:, part] for part in range(2)
    )
    lanes = jnp.stack([real, imag, -imag, real], axis=4)
    lanes = lanes.transpose(0, 2, 1, 3, 4, 5).reshape(planes, KP, channels, 8 * MX)
    return jnp.pad(lanes, ((0, 0), (0, 0), (0, 0), (0, LANES - 8 * MX)))


def greet(axes):
    barrier = pltpu.get_barrier_semaphore()
    total = 0
    for axis, count in axes:
        me = lax.axis_index(axis)
        for step in range(1, count):
            pl.semaphore_signal(
                barrier,
                inc=1,
                device_id={axis: lax.rem(me + step, count)},
                device_id_type=pl.DeviceIdType.MESH,
            )
        total += count - 1
    pl.semaphore_wait(barrier, total)


def spread(axis, count, source, held, send_sem, recv_sem):
    me = lax.axis_index(axis)
    copies = []
    for step in range(1, count):
        peer = lax.rem(me + step, count)
        copy = pltpu.make_async_remote_copy(
            src_ref=source(peer),
            dst_ref=held.at[step],
            send_sem=send_sem.at[step],
            recv_sem=recv_sem.at[step],
            device_id={axis: peer},
            device_id_type=pl.DeviceIdType.MESH,
        )
        copy.start()
        copies.append(copy)
    return copies


def collect(axis, count, own, held, copies, out_ref):
    me = lax.axis_index(axis)
    out_ref[me] = own
    for step, copy in enumerate(copies, 1):
        copy.wait_recv()
        out_ref[lax.rem(me - step + count, count)] = held[step]


def z_and_y(groups, quarters, own_ref, matrix_ref, out_ref, held_z, all_z, stage, held_y, sems):
    send_z, recv_z, send_y, recv_y = sems
    first = spread("gz", groups, lambda peer: own_ref, held_z, send_z, recv_z)
    collect("gz", groups, own_ref[...], held_z, first, all_z)
    rows = all_z[...].reshape(-1, all_z.shape[-1]).astype(F32)
    stage[...] = jnp.dot(
        matrix_ref[...], rows, precision=lax.Precision.HIGHEST, preferred_element_type=F32
    ).astype(BF16)
    second = spread("gy", quarters, lambda peer: stage, held_y, send_y, recv_y)
    collect("gy", quarters, stage[...], held_y, second, out_ref)
    return first + second


def sum_kernel(
    groups, quarters, own_ref, matrix_ref, out_ref, held_sum, summed, held_z, all_z, stage, held_y,
    send_sum, recv_sum, *sems,
):
    greet((("gz", groups), ("gy", quarters)))
    copies = spread("gy", quarters, lambda peer: own_ref.at[peer], held_sum, send_sum, recv_sum)
    total = own_ref[lax.axis_index("gy")]
    for step, copy in enumerate(copies, 1):
        copy.wait_recv()
        total = total + held_sum[step]
    summed[...] = total.astype(BF16)
    copies += z_and_y(
        groups, quarters, summed, matrix_ref, out_ref, held_z, all_z, stage, held_y, sems
    )
    for copy in copies:
        copy.wait_send()


def spread_kernel(
    groups, quarters, own_ref, matrix_ref, out_ref, held_z, all_z, stage, held_y, *sems
):
    greet((("gz", groups), ("gy", quarters)))
    copies = z_and_y(
        groups, quarters, own_ref, matrix_ref, out_ref, held_z, all_z, stage, held_y, sems
    )
    for copy in copies:
        copy.wait_send()


def communicate(value, matrix, summing, number):
    groups, quarters = lax.axis_size("gz"), lax.axis_size("gy")
    block = value.shape[-2:]
    result = (matrix.shape[0], block[1])
    vmem = pl.BlockSpec(memory_space=pltpu.VMEM)
    scratch = [
        pltpu.VMEM((groups,) + block, BF16),
        pltpu.VMEM((groups,) + block, BF16),
        pltpu.VMEM(result, BF16),
        pltpu.VMEM((quarters,) + result, BF16),
    ]
    sems = [pltpu.SemaphoreType.DMA((count,)) for count in (groups, groups, quarters, quarters)]
    if summing:
        scratch = [pltpu.VMEM((quarters,) + block, F32), pltpu.VMEM(block, BF16)] + scratch
        sems = [pltpu.SemaphoreType.DMA((quarters,))] * 2 + sems
    return pl.pallas_call(
        functools.partial(sum_kernel if summing else spread_kernel, groups, quarters),
        out_shape=jax.ShapeDtypeStruct((quarters,) + result, BF16),
        in_specs=[vmem, vmem],
        out_specs=vmem,
        scratch_shapes=scratch + sems,
        compiler_params=pltpu.CompilerParams(collective_id=number, has_side_effects=True),
        name="exchange",
    )(value, matrix)


def z_matrix(cosine, sine, inverse):
    sign = -1.0 if inverse else 1.0
    return jnp.stack(
        [jnp.stack([cosine, sign * sine]), jnp.stack([-sign * sine, cosine])]
    )


def weigh(spectrum, coefficients):
    real, imag = spectrum[0], spectrum[1]

    def product(left, right):
        return jnp.einsum("zcq,zqco->zoq", left, right, preferred_element_type=F32)

    modal_real = product(real, coefficients[0]) - product(imag, coefficients[1])
    modal_imag = product(real, coefficients[1]) + product(imag, coefficients[0])
    return jnp.stack([modal_real, modal_imag]).astype(BF16)


def exchange(partial, local_weights, planes, full_z, number):
    highest = lax.Precision.HIGHEST
    channels = partial.shape[1]
    modes = KY * MX
    here_z = lax.axis_index("gz") * planes + jnp.arange(planes, dtype=jnp.int32)
    all_z = jnp.arange(full_z, dtype=jnp.int32)
    own_modes = local_weights.shape[1]
    groups = lax.axis_size("gz")
    if own_modes % modes == 0:
        own_kz = own_modes // modes
        cosine, sine = angles(KZ, all_z, full_z, True)
        first = lax.axis_index("gz") * own_kz
        cosine = lax.dynamic_slice_in_dim(cosine, first, own_kz, 0)
        sine = lax.dynamic_slice_in_dim(sine, first, own_kz, 0)
        forward = z_matrix(cosine, sine, False).transpose(0, 2, 3, 1)
        forward = forward.reshape(2 * own_kz, 2 * full_z)
        quarters = lax.axis_size("gy")
        share = channels // quarters
        split = partial.reshape(planes * 2, quarters, share, modes).transpose(1, 0, 2, 3)
        spectrum = communicate(
            split.reshape(quarters, planes * 2 * share, modes),
            jnp.kron(forward, jnp.eye(share, dtype=F32)),
            True,
            number,
        )
        spectrum = spectrum.reshape(quarters, 2, own_kz, share, modes).transpose(1, 2, 0, 3, 4)
        spectrum = spectrum.reshape(2, own_kz, channels, modes)
        coefficients = local_weights.reshape(2, own_kz, modes, channels, -1)
        modal = weigh(spectrum, coefficients)
        outputs = modal.shape[2]
        cosine, sine = angles(KZ, here_z, full_z, True)
        inverse = z_matrix(cosine, sine, True).reshape(2, 2, groups, own_kz, planes)
        inverse = inverse.transpose(4, 0, 2, 1, 3).reshape(planes * 2, groups * 2 * own_kz)
        rows = communicate(
            modal.reshape(2 * own_kz * outputs, modes),
            jnp.kron(inverse, jnp.eye(outputs, dtype=F32)),
            False,
            number + 1,
        )
        rows = rows.reshape(quarters, planes * 2, outputs, modes).transpose(1, 0, 2, 3)
        return rows.reshape(planes * 2, channels, modes)
    cosine, sine = angles(KZ, here_z, full_z, True)
    forward = z_matrix(cosine, sine, False).transpose(0, 2, 3, 1)
    sums = jnp.einsum(
        "akr,rcq->ackq", forward.reshape(2, KZ, planes * 2), partial, precision=highest
    ).reshape(2, channels, KZ * modes)
    sums = lax.psum_scatter(sums, "gz", scatter_dimension=2, tiled=True)
    spectrum = lax.psum(sums, "gy").astype(BF16)[:, None]
    coefficients = lax.all_gather(local_weights, "gy", axis=3, tiled=True)[:, None]
    modal = weigh(spectrum, coefficients)[:, 0]
    modal = lax.all_gather(modal, "gz", axis=2, tiled=True)
    modal = modal.astype(F32).reshape(2, channels, KZ, modes)
    inverse = z_matrix(cosine, sine, True)
    rows = jnp.einsum("abkz,bckq->zacq", inverse, modal, precision=highest)
    return rows.reshape(planes * 2, channels, modes)


def per_device(noisy_field, spectral_weights, skip_weights, in_weights, in_bias, out_weights):
    channels, planes, quarter, length_x = noisy_field.shape
    layer_count = spectral_weights.shape[0]
    full_y = quarter * lax.axis_size("gy")
    full_z = planes * lax.axis_size("gz")
    y_positions = lax.axis_index("gy") * quarter + jnp.arange(quarter, dtype=jnp.int32)
    weights_y = y_weights(y_positions, full_y)
    table = forward_table(length_x)
    inverse = inverse_table(length_x)
    scale = 1.0 / math.sqrt(length_x * full_y * full_z)
    field = noisy_field.transpose(1, 2, 0, 3).reshape(planes * quarter, channels, length_x)
    modes = run_forward(field, weights_y, table, planes)
    for layer in range(layer_count):
        rows = exchange(
            fold_modes(modes, scale), spectral_weights[layer], planes, full_z, 2 * layer
        )
        last = layer == layer_count - 1
        result = run_layer(
            field,
            unfold_modes(rows, planes),
            weights_y,
            inverse,
            skip_weights[layer],
            in_weights[layer],
            in_bias[layer][:, None],
            out_weights[layer],
            None if last else table,
        )
        if last:
            field = result
        else:
            field, modes = result
    return field.reshape(planes, quarter, channels, length_x).transpose(2, 0, 1, 3)


HALF = math.sqrt(0.5)
WIDE = 384
SUB = 32
YB = 8
VMEM_LIMIT = 52 * 2**20


def np_angles(number, positions, length, signed):
    kept = np.arange(number)
    if signed:
        kept = np.where(kept < number // 2, kept, kept - number)
    phases = np.mod(kept[:, None] * np.asarray(positions)[None, :], length)
    radians = 2.0 * math.pi / length * phases
    return np.cos(radians), np.sin(radians)


def np_tables(groups, quarters, planes, quarter, length_x, channels):
    full_y, full_z = quarter * quarters, planes * groups
    share = channels // quarters
    own_kz = KZ // groups
    modes = KY * MX
    x_cos, x_sin = np_angles(MX, range(length_x), length_x, False)
    to_x = np.zeros((YB, length_x, YB, SUB))
    from_x = np.zeros((YB, SUB, YB, length_x))
    factor = np.where(np.arange(MX) == 0, 1.0, 2.0)[:, None] / math.sqrt(2.0 * KZ * KY * MX)
    for j in range(YB):
        to_x[j, :, j, :MX] = x_cos.T
        to_x[j, :, j, MX : 2 * MX] = -x_sin.T
        from_x[j, :MX, j, :] = x_cos * factor
        from_x[j, MX : 2 * MX, j, :] = -x_sin * factor
    y_cos, y_sin = np_angles(KY, range(quarter), full_y, True)
    to_y = np.zeros((quarter, SUB, 2, WIDE))
    from_y = np.zeros((2, WIDE, quarter, SUB))
    scale = 1.0 / math.sqrt(length_x * full_y * full_z)
    for ky in range(KY):
        for kx in range(MX):
            at = ky * MX + kx
            cosine, sine = y_cos[ky], y_sin[ky]
            to_y[:, kx, 0, at] = cosine * scale
            to_y[:, MX + kx, 0, at] = sine * scale
            to_y[:, kx, 1, at] = -sine * scale
            to_y[:, MX + kx, 1, at] = cosine * scale
            from_y[0, at, :, kx] = cosine
            from_y[1, at, :, kx] = -sine
            from_y[0, at, :, MX + kx] = sine
            from_y[1, at, :, MX + kx] = cosine
    turn_cos, turn_sin = np_angles(KY, np.arange(quarters) * quarter, full_y, True)
    turn = np.zeros((quarters, 2, WIDE))
    turn[:, 0, :modes] = np.repeat(turn_cos.T, MX, axis=1)
    turn[:, 1, :modes] = np.repeat(turn_sin.T, MX, axis=1)
    z_cos, z_sin = np_angles(KZ, range(full_z), full_z, True)
    z_cos = z_cos.reshape(groups, own_kz, groups, planes)
    z_sin = z_sin.reshape(groups, own_kz, groups, planes)
    forward = np.zeros((groups, 2, own_kz, groups, planes, 2))
    forward[:, 0, :, :, :, 0] = z_cos
    forward[:, 0, :, :, :, 1] = z_sin
    forward[:, 1, :, :, :, 0] = -z_sin
    forward[:, 1, :, :, :, 1] = z_cos
    forward = forward.reshape(groups, 2 * own_kz, groups * planes * 2)
    back_cos = z_cos.transpose(0, 2, 3, 1)
    back_sin = z_sin.transpose(0, 2, 3, 1)
    inverse = np.zeros((groups, groups, planes, 2, own_kz, 2))
    inverse[:, :, :, 0, :, 0] = back_cos
    inverse[:, :, :, 0, :, 1] = -back_sin
    inverse[:, :, :, 1, :, 0] = back_sin
    inverse[:, :, :, 1, :, 1] = back_cos
    inverse = inverse.reshape(groups, groups * planes * 2, own_kz * 2)
    eye = np.eye(share)[None]

    def low(array):
        return array.astype(np.float32).astype(ml_dtypes.bfloat16)

    return dict(
        to_x=low(to_x.reshape(YB * length_x, YB * SUB)),
        from_x=low(from_x.reshape(YB * SUB, YB * length_x)),
        to_y=low(to_y.reshape(quarter * SUB, 2 * WIDE)),
        from_y=low(from_y.reshape(2 * WIDE, quarter * SUB)),
        turn=turn.astype(np.float32),
        to_z=low(np.kron(forward, eye)),
        from_z=low(np.kron(inverse, eye)),
    )


def send(axis, count, source, target, send_sem, recv_sem):
    me = lax.axis_index(axis)
    copies = []
    for step in range(1, count):
        peer = lax.rem(me + step, count)
        copy = pltpu.make_async_remote_copy(
            src_ref=source(peer),
            dst_ref=target(me, step),
            send_sem=send_sem.at[step],
            recv_sem=recv_sem.at[step],
            device_id={axis: peer},
            device_id_type=pl.DeviceIdType.MESH,
        )
        copy.start()
        copies.append(copy)
    return copies


def spectra(field, to_x, to_y):
    blocks, rows, _ = field.shape
    along = jnp.dot(
        field[...].reshape(blocks * rows, -1), to_x[...], preferred_element_type=F32
    ).astype(BF16)
    along = jnp.concatenate([along[b * rows : (b + 1) * rows] for b in range(blocks)], 1)
    return jnp.dot(along, to_y[...], preferred_element_type=F32)


def weigh_modes(spec, weights, modal):
    share = 8
    length = weights.shape[-1]
    for start in range(0, length, 256):
        width = min(256, length - start)
        cols = slice(start, start + width)

        def group(cg, total, cols=cols, width=width):
            real, imag = total
            lines = spec[pl.ds(pl.multiple_of(cg * 16, 16), 16), cols]
            for t in range(share // 2):
                at = pl.ds(pl.multiple_of(cg * share * share + 16 * t, 16), 16)
                w_real = weights[0, at, cols].astype(F32)
                w_imag = weights[1, at, cols].astype(F32)
                parts = []
                for part in range(2):
                    rows = [
                        jnp.broadcast_to(lines[at_row : at_row + 1], (share, width))
                        for at_row in (part * share + 2 * t, part * share + 2 * t + 1)
                    ]
                    parts.append(jnp.concatenate(rows, 0))
                real = real + parts[0] * w_real - parts[1] * w_imag
                imag = imag + parts[0] * w_imag + parts[1] * w_real
            return real, imag

        zero = jnp.zeros((16, width), F32)
        real, imag = lax.fori_loop(0, spec.shape[0] // 16, group, (zero, zero))
        modal[:share, cols] = real[:share] + real[share:]
        modal[share:, cols] = imag[:share] + imag[share:]


def exchange_modes(spectrum, tables, weights, buffers, sems, ready):
    turn_ref, to_z, from_z, from_y = tables
    part, held_sum, all_z, all_c, spec, modal, out_z, held_z, all_o = buffers
    groups, quarters = all_z.shape[0], part.shape[0]
    share = 8
    planes = all_z.shape[1] // (2 * share)
    channels = quarters * share
    own_kz = to_z.shape[1] // (2 * share)
    g, q = lax.axis_index("gz"), lax.axis_index("gy")
    turn = turn_ref[q]
    cosine, sine = turn[0:1], turn[1:2]
    real, imag = spectrum[:, :WIDE], spectrum[:, WIDE:]
    real, imag = cosine * real + sine * imag, cosine * imag - sine * real
    for quarter in range(quarters):
        rows = []
        for z in range(planes):
            at = z * channels + quarter * share
            rows += [real[at : at + share], imag[at : at + share]]
        part[quarter] = jnp.concatenate(rows, 0).astype(BF16)
    ready["greet"]()
    copies = send(
        "gy", quarters, lambda peer: part.at[peer], lambda me, step: held_sum.at[step], *sems[0]
    )
    total = part[q].astype(F32)
    for step, copy in enumerate(copies, 1):
        copy.wait_recv()
        total = total + held_sum[step].astype(F32)
    all_z[g] = total.astype(BF16)
    more = send("gz", groups, lambda peer: all_z.at[g], lambda me, step: all_z.at[me], *sems[1])
    for copy in more:
        copy.wait_recv()
    copies += more
    rows = all_z[...].reshape(-1, WIDE)
    bins = jnp.dot(to_z[g], rows, preferred_element_type=F32)
    modes = KY * MX
    length = 8 * 128
    zero = jnp.zeros((share, length - WIDE), F32)
    halves = []
    for half in range(2):
        for kz in range(own_kz):
            at = (half * own_kz + kz) * share
            wide = jnp.concatenate([bins[at : at + share], zero], 1)
            if kz == 0:
                line = wide
            else:
                line = line + pltpu.roll(wide, kz * modes, 1)
        halves.append(line)
    all_c[q] = jnp.concatenate(halves, 0)[:, : all_c.shape[-1]].astype(BF16)
    more = send("gy", quarters, lambda peer: all_c.at[q], lambda me, step: all_c.at[me], *sems[2])
    for copy in more:
        copy.wait_recv()
    copies += more
    spec[...] = all_c[...].reshape(spec.shape).astype(F32)
    modal[...] = jnp.zeros_like(modal)
    ready["weights"]()
    weigh_modes(spec, weights, modal)
    line = modal[...]
    rows = []
    for kz in range(own_kz):
        moved = line if kz == 0 else pltpu.roll(line, length - kz * modes, 1)
        rows.append(moved[:, :WIDE])
    rows = jnp.concatenate(rows, 0).astype(BF16)
    back = jnp.dot(from_z[g], rows, preferred_element_type=F32)
    out_z[...] = back.astype(BF16).reshape(out_z.shape)
    more = send(
        "gz", groups, lambda peer: out_z.at[peer], lambda me, step: held_z.at[step], *sems[3]
    )
    total = out_z[g].astype(F32)
    for step, copy in enumerate(more, 1):
        copy.wait_recv()
        total = total + held_z[step].astype(F32)
    copies += more
    all_o[q] = total.astype(BF16)
    more = send("gy", quarters, lambda peer: all_o.at[q], lambda me, step: all_o.at[me], *sems[4])
    for copy in more:
        copy.wait_recv()
    copies += more
    ready["from_y"]()
    real, imag = [], []
    pieces = [all_o[quarter].astype(F32) for quarter in range(quarters)]
    for z in range(planes):
        for piece in pieces:
            at = z * 2 * share
            real.append(piece[at : at + share])
            imag.append(piece[at + share : at + 2 * share])
    real, imag = jnp.concatenate(real, 0), jnp.concatenate(imag, 0)
    real, imag = cosine * real - sine * imag, sine * real + cosine * imag
    rows = jnp.concatenate([real, imag], 1).astype(BF16)
    result = jnp.dot(rows, from_y[...], preferred_element_type=F32).astype(BF16)
    for copy in copies:
        copy.wait_send()
    return result


def pointwise(field, rows_y, from_x, skip, lift_t, bias, down, lift, out):
    blocks, rows, length = field.shape
    channels = skip.shape[-1]
    planes = rows // channels
    hidden = down.shape[-1]
    scaled = bias * F32(HALF)
    high = scaled.astype(BF16).astype(F32)
    middle = (scaled - high).astype(BF16).astype(F32)
    low = scaled - high - middle
    tail = jnp.zeros((128 - channels - 3, hidden), F32)
    tall = jnp.concatenate([lift_t.astype(F32), high, middle, low, tail], 0)
    lift[...] = tall.T.astype(BF16)
    blank = jnp.zeros((channels, channels), F32)
    skip = skip.astype(F32)
    block_rows = []
    for z in range(planes):
        block_rows.append(
            jnp.concatenate([skip if z == other else blank for other in range(planes)], 1)
        )
    skip_all = jnp.concatenate(block_rows, 0).astype(BF16)
    ones = (lax.broadcasted_iota(jnp.int32, (16, planes * length), 0) < 3).astype(F32).astype(BF16)
    wide_k = channels + 16

    def step(b, carry):
        current = field[b]
        spatial = jnp.dot(
            rows_y[:, pl.ds(pl.multiple_of(b * YB * SUB, YB * SUB), YB * SUB)],
            from_x[...],
            preferred_element_type=F32,
        )
        mixed = spatial + jnp.dot(skip_all, current, preferred_element_type=F32)
        lower = (mixed * F32(HALF)).astype(BF16)
        wide = jnp.concatenate(
            [lower[z * channels : (z + 1) * channels] for z in range(planes)], 1
        )
        wide = jnp.concatenate([wide, ones], 0)
        value = jnp.dot(lift[:, :wide_k], wide, preferred_element_type=F32)
        value = (value + value * lax.erf(value)).astype(BF16)
        change = jnp.dot(down, value, preferred_element_type=F32) * F32(HALF)
        for z in range(planes):
            at = z * channels
            result = mixed[at : at + channels] + change[:, z * length : (z + 1) * length]
            out[b, at : at + channels, :] = result.astype(BF16)
        return carry

    lax.fori_loop(0, blocks, step, 0)


def meet(groups, quarters):
    barrier = pltpu.get_barrier_semaphore()
    for axis, count in (("gz", groups), ("gy", quarters)):
        me = lax.axis_index(axis)
        for step in range(1, count):
            pl.semaphore_signal(
                barrier,
                inc=1,
                device_id={axis: lax.rem(me + step, count)},
                device_id_type=pl.DeviceIdType.MESH,
            )
    return lambda: pl.semaphore_wait(barrier, groups + quarters - 2)


def loads(pairs, sem):
    copies = [
        pltpu.make_async_copy(source, target, sem.at[at])
        for at, (source, target) in enumerate(pairs)
    ]
    for copy in copies:
        copy.start()
    return copies


def first_kernel(
    layer, sizes, field_hbm, to_x_hbm, to_y_hbm, from_y_hbm, weights_hbm, turn, to_z, from_z,
    rows_out, field, to_x, to_y, from_y, weights, local_sem, *rest,
):
    groups, quarters = sizes
    greeting = meet(groups, quarters)
    copies = loads(
        [
            (field_hbm, field),
            (to_x_hbm, to_x),
            (to_y_hbm, to_y),
            (weights_hbm.at[layer], weights),
            (from_y_hbm, from_y),
        ],
        local_sem,
    )
    buffers, sems = rest[:9], rest[9:]
    sems = [(sems[2 * at], sems[2 * at + 1]) for at in range(5)]
    for copy in copies[:3]:
        copy.wait()
    spectrum = spectra(field, to_x, to_y)
    ready = {"greet": greeting, "weights": copies[3].wait, "from_y": copies[4].wait}
    rows_out[...] = exchange_modes(
        spectrum, (turn, to_z, from_z, from_y), weights, buffers, sems, ready
    )


def middle_fused(
    layer, sizes, field_hbm, rows_y, from_x_hbm, to_x_hbm, to_y_hbm, from_y_hbm, weights_hbm,
    turn, to_z, from_z, skip, lift_t, bias, down,
    rows_out, field_out, field, from_x, to_x, to_y, from_y, weights, lift, local_sem, *rest,
):
    groups, quarters = sizes
    greeting = meet(groups, quarters)
    copies = loads(
        [
            (field_hbm, field),
            (from_x_hbm, from_x),
            (to_x_hbm, to_x),
            (to_y_hbm, to_y),
            (weights_hbm.at[layer], weights),
            (from_y_hbm, from_y),
        ],
        local_sem,
    )
    buffers, sems = rest[:9], rest[9:]
    sems = [(sems[2 * at], sems[2 * at + 1]) for at in range(5)]
    for copy in copies[:2]:
        copy.wait()
    before = layer - 1
    pointwise(
        field, rows_y, from_x, skip[before], lift_t[before], bias[before : before + 1],
        down[before], lift, field_out,
    )
    for copy in copies[2:4]:
        copy.wait()
    spectrum = spectra(field_out, to_x, to_y)
    ready = {"greet": greeting, "weights": copies[4].wait, "from_y": copies[5].wait}
    rows_out[...] = exchange_modes(
        spectrum, (turn, to_z, from_z, from_y), weights, buffers, sems, ready
    )


def last_kernel(
    layer, field_hbm, rows_y, from_x_hbm, skip, lift_t, bias, down, field_out,
    field, from_x, lift, local_sem,
):
    copies = loads([(field_hbm, field), (from_x_hbm, from_x)], local_sem)
    for copy in copies:
        copy.wait()
    pointwise(
        field, rows_y, from_x, skip[layer], lift_t[layer], bias[layer : layer + 1],
        down[layer], lift, field_out,
    )


def fast_device(noisy_field, spectral_weights, skip_weights, in_weights, in_bias, out_weights):
    channels, planes, quarter, length_x = noisy_field.shape
    layer_count = spectral_weights.shape[0]
    groups, quarters = lax.axis_size("gz"), lax.axis_size("gy")
    own_kz = KZ // groups
    own_modes = spectral_weights.shape[2]
    share = channels // quarters
    blocks = quarter // YB
    hidden = in_weights.shape[1]
    tables = np_tables(groups, quarters, planes, quarter, length_x, channels)
    tables = {name: jnp.asarray(value) for name, value in tables.items()}
    field = noisy_field.reshape(channels, planes, blocks, YB, length_x)
    field = field.transpose(2, 1, 0, 3, 4).reshape(blocks, planes * channels, YB * length_x)
    weights = spectral_weights.transpose(0, 1, 3, 4, 2)
    weights = weights.reshape(layer_count, 2, channels * share, own_modes)
    lift_t = in_weights.transpose(0, 2, 1)
    rows_shape = jax.ShapeDtypeStruct((planes * channels, quarter * SUB), BF16)
    field_shape = jax.ShapeDtypeStruct(field.shape, BF16)
    anywhere = pl.BlockSpec(memory_space=pl.ANY)
    vmem = pl.BlockSpec(memory_space=pltpu.VMEM)

    def held(name):
        return pltpu.VMEM(tables[name].shape, tables[name].dtype)

    full = length_wide = -(-own_modes // 128) * 128
    block = (planes * 2 * share, WIDE)
    traffic = [
        pltpu.VMEM((quarters,) + block, BF16),
        pltpu.VMEM((quarters,) + block, BF16),
        pltpu.VMEM((groups,) + block, BF16),
        pltpu.VMEM((quarters, 2 * share, full), BF16),
        pltpu.VMEM((quarters * 2 * share, full), F32),
        pltpu.VMEM((2 * share, 8 * 128), F32),
        pltpu.VMEM((groups,) + block, BF16),
        pltpu.VMEM((groups,) + block, BF16),
        pltpu.VMEM((quarters,) + block, BF16),
    ]
    for count in (quarters, groups, quarters, groups, quarters):
        traffic += [pltpu.SemaphoreType.DMA((count,))] * 2
    weights_held = pltpu.VMEM(weights.shape[1:], BF16)
    lift_held = pltpu.VMEM((hidden, 128), BF16)
    field_held = pltpu.VMEM(field.shape, BF16)
    maps = (skip_weights, lift_t, in_bias, out_weights)
    rows = pl.pallas_call(
        functools.partial(first_kernel, 0, (groups, quarters)),
        out_shape=rows_shape,
        in_specs=[anywhere] * 5 + [vmem] * 3,
        out_specs=vmem,
        scratch_shapes=[
            field_held, held("to_x"), held("to_y"), held("from_y"), weights_held,
            pltpu.SemaphoreType.DMA((5,)),
        ] + traffic,
        compiler_params=pltpu.CompilerParams(
            collective_id=0, has_side_effects=True, vmem_limit_bytes=VMEM_LIMIT
        ),
        name="first_modes",
    )(
        field, tables["to_x"], tables["to_y"], tables["from_y"], weights, tables["turn"],
        tables["to_z"], tables["from_z"],
    )
    for layer in range(1, layer_count):
        rows, field = pl.pallas_call(
            functools.partial(middle_fused, layer, (groups, quarters)),
            out_shape=[rows_shape, field_shape],
            in_specs=[anywhere, vmem] + [anywhere] * 5 + [vmem] * 7,
            out_specs=[vmem, vmem],
            scratch_shapes=[
                field_held, held("from_x"), held("to_x"), held("to_y"), held("from_y"),
                weights_held, lift_held, pltpu.SemaphoreType.DMA((6,)),
            ] + traffic,
            compiler_params=pltpu.CompilerParams(
                collective_id=layer, has_side_effects=True, vmem_limit_bytes=VMEM_LIMIT
            ),
            name="middle_modes",
        )(
            field, rows, tables["from_x"], tables["to_x"], tables["to_y"], tables["from_y"],
            weights, tables["turn"], tables["to_z"], tables["from_z"], *maps,
        )
    result = pl.pallas_call(
        functools.partial(last_kernel, layer_count - 1),
        out_shape=field_shape,
        in_specs=[anywhere, vmem, anywhere] + [vmem] * 4,
        out_specs=vmem,
        scratch_shapes=[field_held, held("from_x"), lift_held, pltpu.SemaphoreType.DMA((2,))],
        compiler_params=pltpu.CompilerParams(vmem_limit_bytes=VMEM_LIMIT),
        name="last_layer",
    )(field, rows, tables["from_x"], *maps)
    result = result.reshape(blocks, planes, channels, YB, length_x)
    return result.transpose(2, 1, 0, 3, 4).reshape(noisy_field.shape)


def pick(noisy_field, spectral_weights, *rest):
    groups, quarters = lax.axis_size("gz"), lax.axis_size("gy")
    channels, planes, quarter, _ = noisy_field.shape
    fits = (
        KZ % groups == 0
        and spectral_weights.shape[2] == KZ // groups * KY * MX
        and spectral_weights.shape[2] <= 8 * 128 - 128
        and channels == 8 * quarters
        and planes == 2
        and quarter % YB == 0
    )
    body = fast_device if fits else per_device
    return body(noisy_field, spectral_weights, *rest)


def solution(mesh):
    in_specs = (P(None, "gz", "gy", None), P(None, None, "gz", None, "gy"), P(), P(), P(), P())
    out_specs = P(None, "gz", "gy", None)
    return jax.shard_map(
        pick, mesh=mesh, in_specs=in_specs, out_specs=out_specs, check_vma=False
    )
```

```python
import functools
import math

import jax
import jax.numpy as jnp
from jax import lax
from jax.experimental import pallas as pl
from jax.experimental.pallas import tpu as pltpu
from jax.sharding import PartitionSpec as P
import ml_dtypes
import numpy as np

MX = 12
KY = 24
KZ = 24
KP = KY // 2
LANES = 128
ROWS = 32
F32 = jnp.float32
BF16 = jnp.bfloat16


def angles(number, positions, length, signed):
    kept = jnp.arange(number, dtype=jnp.int32)
    if signed:
        kept = jnp.where(kept < number // 2, kept, kept - number)
    phases = jnp.mod(kept[:, None] * positions[None, :], length)
    radians = 2.0 * math.pi / length * phases.astype(jnp.float32)
    return (jnp.cos(radians), jnp.sin(radians))


def forward_table(length):
    cosine, sine = angles(MX, jnp.arange(length, dtype=jnp.int32), length, False)
    part = jnp.concatenate([cosine, -sine, -sine, -cosine], 0)
    table = jnp.concatenate([part, part], 0).T.astype(BF16)
    return jnp.pad(table, ((0, 0), (0, LANES - 8 * MX)))


def inverse_table(length):
    cosine, sine = angles(MX, jnp.arange(length, dtype=jnp.int32), length, False)
    factor = jnp.where(jnp.arange(MX) == 0, F32(1.0), F32(2.0))[:, None]
    scale = 1.0 / math.sqrt(2.0 * KZ * KY * MX)
    half = jnp.concatenate([cosine * factor, -sine * factor], 0) * scale
    table = jnp.concatenate([half] * 4, 0).astype(BF16)
    return jnp.pad(table, ((0, LANES - 8 * MX), (0, 0)))


def y_weights(positions, length):
    cosine, sine = angles(KY, positions, length, True)
    both = jnp.stack([cosine, sine], -1).transpose(1, 0, 2)
    lanes = jnp.repeat(both.reshape(positions.shape[0], KP, 4), 2 * MX, axis=2)
    return jnp.pad(lanes, ((0, 0), (0, 0), (0, LANES - 8 * MX)))


def gelu(value):
    return 0.5 * value * (1.0 + lax.erf(value * F32(math.sqrt(0.5))))


def accumulate_modes(along, weight_ref, modes_ref):
    rows, channels = along.shape[0], along.shape[1]

    @pl.when(pl.program_id(1) == 0)
    def _():
        modes_ref[...] = jnp.zeros_like(modes_ref)

    for kp in range(KP):
        total = along[0] * weight_ref[0, kp : kp + 1, :]
        for y in range(1, rows):
            total = total + along[y] * weight_ref[y, kp : kp + 1, :]
        modes_ref[0, kp] += total


def forward_kernel(field_ref, weight_ref, table_ref, modes_ref):
    rows, channels, length = field_ref.shape
    flat = field_ref[...].reshape(rows * channels, length)
    along = jnp.dot(flat, table_ref[...], preferred_element_type=F32)
    accumulate_modes(along.reshape(rows, channels, LANES), weight_ref, modes_ref)


def layer_body(
    field_ref, planes_ref, weight_ref, inverse_ref, skip_ref, lift_ref, bias_ref, down_ref, out_ref
):
    rows, channels, length = field_ref.shape
    parts = []
    for y in range(rows):
        total = planes_ref[0, 0] * weight_ref[y, 0:1, :]
        for kp in range(1, KP):
            total = total + planes_ref[0, kp] * weight_ref[y, kp : kp + 1, :]
        parts.append(total.astype(BF16))
    stacked = jnp.concatenate(parts, 0)
    spatial = jnp.dot(stacked, inverse_ref[...], preferred_element_type=F32)
    wide_spatial = jnp.concatenate(
        [spatial[y * channels : (y + 1) * channels] for y in range(rows)], 1
    )
    wide_field = jnp.concatenate([field_ref[y] for y in range(rows)], 1)
    mixed = wide_spatial + jnp.dot(skip_ref[...], wide_field, preferred_element_type=F32)
    before = jnp.dot(lift_ref[...], mixed.astype(BF16), preferred_element_type=F32)
    hidden = gelu(before + bias_ref[...]).astype(BF16)
    result = mixed + jnp.dot(down_ref[...], hidden, preferred_element_type=F32)
    result = result.astype(BF16)
    for y in range(rows):
        out_ref[y] = result[:, y * length : (y + 1) * length]


def middle_kernel(
    field_ref, planes_ref, weight_ref, inverse_ref, skip_ref, lift_ref, bias_ref, down_ref,
    table_ref, out_ref, modes_ref,
):
    layer_body(
        field_ref, planes_ref, weight_ref, inverse_ref, skip_ref, lift_ref, bias_ref, down_ref,
        out_ref,
    )
    forward_kernel(out_ref, weight_ref, table_ref, modes_ref)


def whole(shape):
    return pl.BlockSpec(shape, lambda z, y: (0,) * len(shape))


def run_forward(field, weights_y, table, planes):
    total, channels, length = field.shape
    steps = total // planes // ROWS
    return pl.pallas_call(
        forward_kernel,
        grid=(planes, steps),
        in_specs=[
            pl.BlockSpec((ROWS, channels, length), lambda z, y: (z * steps + y, 0, 0)),
            pl.BlockSpec((ROWS, KP, LANES), lambda z, y: (y, 0, 0)),
            whole(table.shape),
        ],
        out_specs=pl.BlockSpec((1, KP, channels, LANES), lambda z, y: (z, 0, 0, 0)),
        out_shape=jax.ShapeDtypeStruct((planes, KP, channels, LANES), F32),
        name="forward_modes",
    )(field, weights_y, table)


def run_layer(field, plane_modes, weights_y, inverse, skip, lift, bias, down, table):
    total, channels, length = field.shape
    planes = plane_modes.shape[0]
    steps = total // planes // ROWS
    field_spec = pl.BlockSpec((ROWS, channels, length), lambda z, y: (z * steps + y, 0, 0))
    modes_spec = pl.BlockSpec((1, KP, channels, LANES), lambda z, y: (z, 0, 0, 0))
    field_shape = jax.ShapeDtypeStruct(field.shape, BF16)
    modes_shape = jax.ShapeDtypeStruct(plane_modes.shape, F32)
    args = [field, plane_modes, weights_y, inverse, skip, lift, bias, down]
    specs = [
        field_spec,
        modes_spec,
        pl.BlockSpec((ROWS, KP, LANES), lambda z, y: (y, 0, 0)),
        whole(inverse.shape),
        whole(skip.shape),
        whole(lift.shape),
        whole(bias.shape),
        whole(down.shape),
    ]
    if table is None:
        return pl.pallas_call(
            layer_body,
            grid=(planes, steps),
            in_specs=specs,
            out_specs=field_spec,
            out_shape=field_shape,
            name="last_layer",
        )(*args)
    return pl.pallas_call(
        middle_kernel,
        grid=(planes, steps),
        in_specs=specs + [whole(table.shape)],
        out_specs=[field_spec, modes_spec],
        out_shape=[field_shape, modes_shape],
        name="middle_layer",
    )(*args, table)


def fold_modes(modes, scale):
    planes, _, channels, _ = modes.shape
    split = modes[..., : 8 * MX].reshape(planes, KP, channels, 2, 2, 2, MX)
    folded = (split[:, :, :, :, 0] + split[:, :, :, :, 1]) * scale
    ordered = folded.transpose(0, 4, 2, 1, 3, 5)
    return ordered.reshape(planes * 2, channels, KY * MX)


def unfold_modes(rows, planes):
    channels = rows.shape[1]
    real, imag = (
        rows.astype(F32).reshape(planes, 2, channels, KP, 2, MX)[:, part] for part in range(2)
    )
    lanes = jnp.stack([real, imag, -imag, real], axis=4)
    lanes = lanes.transpose(0, 2, 1, 3, 4, 5).reshape(planes, KP, channels, 8 * MX)
    return jnp.pad(lanes, ((0, 0), (0, 0), (0, 0), (0, LANES - 8 * MX)))


def greet(axes):
    barrier = pltpu.get_barrier_semaphore()
    total = 0
    for axis, count in axes:
        me = lax.axis_index(axis)
        for step in range(1, count):
            pl.semaphore_signal(
                barrier,
                inc=1,
                device_id={axis: lax.rem(me + step, count)},
                device_id_type=pl.DeviceIdType.MESH,
            )
        total += count - 1
    pl.semaphore_wait(barrier, total)


def spread(axis, count, source, held, send_sem, recv_sem):
    me = lax.axis_index(axis)
    copies = []
    for step in range(1, count):
        peer = lax.rem(me + step, count)
        copy = pltpu.make_async_remote_copy(
            src_ref=source(peer),
            dst_ref=held.at[step],
            send_sem=send_sem.at[step],
            recv_sem=recv_sem.at[step],
            device_id={axis: peer},
            device_id_type=pl.DeviceIdType.MESH,
        )
        copy.start()
        copies.append(copy)
    return copies


def collect(axis, count, own, held, copies, out_ref):
    me = lax.axis_index(axis)
    out_ref[me] = own
    for step, copy in enumerate(copies, 1):
        copy.wait_recv()
        out_ref[lax.rem(me - step + count, count)] = held[step]


def z_and_y(groups, quarters, own_ref, matrix_ref, out_ref, held_z, all_z, stage, held_y, sems):
    send_z, recv_z, send_y, recv_y = sems
    first = spread("gz", groups, lambda peer: own_ref, held_z, send_z, recv_z)
    collect("gz", groups, own_ref[...], held_z, first, all_z)
    rows = all_z[...].reshape(-1, all_z.shape[-1]).astype(F32)
    stage[...] = jnp.dot(
        matrix_ref[...], rows, precision=lax.Precision.HIGHEST, preferred_element_type=F32
    ).astype(BF16)
    second = spread("gy", quarters, lambda peer: stage, held_y, send_y, recv_y)
    collect("gy", quarters, stage[...], held_y, second, out_ref)
    return first + second


def sum_kernel(
    groups, quarters, own_ref, matrix_ref, out_ref, held_sum, summed, held_z, all_z, stage, held_y,
    send_sum, recv_sum, *sems,
):
    greet((("gz", groups), ("gy", quarters)))
    copies = spread("gy", quarters, lambda peer: own_ref.at[peer], held_sum, send_sum, recv_sum)
    total = own_ref[lax.axis_index("gy")]
    for step, copy in enumerate(copies, 1):
        copy.wait_recv()
        total = total + held_sum[step]
    summed[...] = total.astype(BF16)
    copies += z_and_y(
        groups, quarters, summed, matrix_ref, out_ref, held_z, all_z, stage, held_y, sems
    )
    for copy in copies:
        copy.wait_send()


def spread_kernel(
    groups, quarters, own_ref, matrix_ref, out_ref, held_z, all_z, stage, held_y, *sems
):
    greet((("gz", groups), ("gy", quarters)))
    copies = z_and_y(
        groups, quarters, own_ref, matrix_ref, out_ref, held_z, all_z, stage, held_y, sems
    )
    for copy in copies:
        copy.wait_send()


def communicate(value, matrix, summing, number):
    groups, quarters = lax.axis_size("gz"), lax.axis_size("gy")
    block = value.shape[-2:]
    result = (matrix.shape[0], block[1])
    vmem = pl.BlockSpec(memory_space=pltpu.VMEM)
    scratch = [
        pltpu.VMEM((groups,) + block, BF16),
        pltpu.VMEM((groups,) + block, BF16),
        pltpu.VMEM(result, BF16),
        pltpu.VMEM((quarters,) + result, BF16),
    ]
    sems = [pltpu.SemaphoreType.DMA((count,)) for count in (groups, groups, quarters, quarters)]
    if summing:
        scratch = [pltpu.VMEM((quarters,) + block, F32), pltpu.VMEM(block, BF16)] + scratch
        sems = [pltpu.SemaphoreType.DMA((quarters,))] * 2 + sems
    return pl.pallas_call(
        functools.partial(sum_kernel if summing else spread_kernel, groups, quarters),
        out_shape=jax.ShapeDtypeStruct((quarters,) + result, BF16),
        in_specs=[vmem, vmem],
        out_specs=vmem,
        scratch_shapes=scratch + sems,
        compiler_params=pltpu.CompilerParams(collective_id=number, has_side_effects=True),
        name="exchange",
    )(value, matrix)


def z_matrix(cosine, sine, inverse):
    sign = -1.0 if inverse else 1.0
    return jnp.stack(
        [jnp.stack([cosine, sign * sine]), jnp.stack([-sign * sine, cosine])]
    )


def weigh(spectrum, coefficients):
    real, imag = spectrum[0], spectrum[1]

    def product(left, right):
        return jnp.einsum("zcq,zqco->zoq", left, right, preferred_element_type=F32)

    modal_real = product(real, coefficients[0]) - product(imag, coefficients[1])
    modal_imag = product(real, coefficients[1]) + product(imag, coefficients[0])
    return jnp.stack([modal_real, modal_imag]).astype(BF16)


def exchange(partial, local_weights, planes, full_z, number):
    highest = lax.Precision.HIGHEST
    channels = partial.shape[1]
    modes = KY * MX
    here_z = lax.axis_index("gz") * planes + jnp.arange(planes, dtype=jnp.int32)
    all_z = jnp.arange(full_z, dtype=jnp.int32)
    own_modes = local_weights.shape[1]
    groups = lax.axis_size("gz")
    if own_modes % modes == 0:
        own_kz = own_modes // modes
        cosine, sine = angles(KZ, all_z, full_z, True)
        first = lax.axis_index("gz") * own_kz
        cosine = lax.dynamic_slice_in_dim(cosine, first, own_kz, 0)
        sine = lax.dynamic_slice_in_dim(sine, first, own_kz, 0)
        forward = z_matrix(cosine, sine, False).transpose(0, 2, 3, 1)
        forward = forward.reshape(2 * own_kz, 2 * full_z)
        quarters = lax.axis_size("gy")
        share = channels // quarters
        split = partial.reshape(planes * 2, quarters, share, modes).transpose(1, 0, 2, 3)
        spectrum = communicate(
            split.reshape(quarters, planes * 2 * share, modes),
            jnp.kron(forward, jnp.eye(share, dtype=F32)),
            True,
            number,
        )
        spectrum = spectrum.reshape(quarters, 2, own_kz, share, modes).transpose(1, 2, 0, 3, 4)
        spectrum = spectrum.reshape(2, own_kz, channels, modes)
        coefficients = local_weights.reshape(2, own_kz, modes, channels, -1)
        modal = weigh(spectrum, coefficients)
        outputs = modal.shape[2]
        cosine, sine = angles(KZ, here_z, full_z, True)
        inverse = z_matrix(cosine, sine, True).reshape(2, 2, groups, own_kz, planes)
        inverse = inverse.transpose(4, 0, 2, 1, 3).reshape(planes * 2, groups * 2 * own_kz)
        rows = communicate(
            modal.reshape(2 * own_kz * outputs, modes),
            jnp.kron(inverse, jnp.eye(outputs, dtype=F32)),
            False,
            number + 1,
        )
        rows = rows.reshape(quarters, planes * 2, outputs, modes).transpose(1, 0, 2, 3)
        return rows.reshape(planes * 2, channels, modes)
    cosine, sine = angles(KZ, here_z, full_z, True)
    forward = z_matrix(cosine, sine, False).transpose(0, 2, 3, 1)
    sums = jnp.einsum(
        "akr,rcq->ackq", forward.reshape(2, KZ, planes * 2), partial, precision=highest
    ).reshape(2, channels, KZ * modes)
    sums = lax.psum_scatter(sums, "gz", scatter_dimension=2, tiled=True)
    spectrum = lax.psum(sums, "gy").astype(BF16)[:, None]
    coefficients = lax.all_gather(local_weights, "gy", axis=3, tiled=True)[:, None]
    modal = weigh(spectrum, coefficients)[:, 0]
    modal = lax.all_gather(modal, "gz", axis=2, tiled=True)
    modal = modal.astype(F32).reshape(2, channels, KZ, modes)
    inverse = z_matrix(cosine, sine, True)
    rows = jnp.einsum("abkz,bckq->zacq", inverse, modal, precision=highest)
    return rows.reshape(planes * 2, channels, modes)


def per_device(noisy_field, spectral_weights, skip_weights, in_weights, in_bias, out_weights):
    channels, planes, quarter, length_x = noisy_field.shape
    layer_count = spectral_weights.shape[0]
    full_y = quarter * lax.axis_size("gy")
    full_z = planes * lax.axis_size("gz")
    y_positions = lax.axis_index("gy") * quarter + jnp.arange(quarter, dtype=jnp.int32)
    weights_y = y_weights(y_positions, full_y)
    table = forward_table(length_x)
    inverse = inverse_table(length_x)
    scale = 1.0 / math.sqrt(length_x * full_y * full_z)
    field = noisy_field.transpose(1, 2, 0, 3).reshape(planes * quarter, channels, length_x)
    modes = run_forward(field, weights_y, table, planes)
    for layer in range(layer_count):
        rows = exchange(
            fold_modes(modes, scale), spectral_weights[layer], planes, full_z, 2 * layer
        )
        last = layer == layer_count - 1
        result = run_layer(
            field,
            unfold_modes(rows, planes),
            weights_y,
            inverse,
            skip_weights[layer],
            in_weights[layer],
            in_bias[layer][:, None],
            out_weights[layer],
            None if last else table,
        )
        if last:
            field = result
        else:
            field, modes = result
    return field.reshape(planes, quarter, channels, length_x).transpose(2, 0, 1, 3)


HALF = math.sqrt(0.5)
WIDE = 384
SUB = 32
YB = 8
VMEM_LIMIT = 60 * 2**20


def np_angles(number, positions, length, signed):
    kept = np.arange(number)
    if signed:
        kept = np.where(kept < number // 2, kept, kept - number)
    phases = np.mod(kept[:, None] * np.asarray(positions)[None, :], length)
    radians = 2.0 * math.pi / length * phases
    return np.cos(radians), np.sin(radians)


def np_tables(groups, quarters, planes, quarter, length_x, channels):
    full_y, full_z = quarter * quarters, planes * groups
    share = channels // quarters
    own_kz = KZ // groups
    modes = KY * MX
    x_cos, x_sin = np_angles(MX, range(length_x), length_x, False)
    to_x = np.zeros((YB, length_x, YB, SUB))
    from_x = np.zeros((YB, SUB, YB, length_x))
    factor = np.where(np.arange(MX) == 0, 1.0, 2.0)[:, None] / math.sqrt(2.0 * KZ * KY * MX)
    for j in range(YB):
        to_x[j, :, j, :MX] = x_cos.T
        to_x[j, :, j, MX : 2 * MX] = -x_sin.T
        from_x[j, :MX, j, :] = x_cos * factor
        from_x[j, MX : 2 * MX, j, :] = -x_sin * factor
    y_cos, y_sin = np_angles(KY, range(quarter), full_y, True)
    to_y = np.zeros((quarter, SUB, 2, WIDE))
    from_y = np.zeros((2, WIDE, quarter, SUB))
    scale = 1.0 / math.sqrt(length_x * full_y * full_z)
    for ky in range(KY):
        for kx in range(MX):
            at = ky * MX + kx
            cosine, sine = y_cos[ky], y_sin[ky]
            to_y[:, kx, 0, at] = cosine * scale
            to_y[:, MX + kx, 0, at] = sine * scale
            to_y[:, kx, 1, at] = -sine * scale
            to_y[:, MX + kx, 1, at] = cosine * scale
            from_y[0, at, :, kx] = cosine
            from_y[1, at, :, kx] = -sine
            from_y[0, at, :, MX + kx] = sine
            from_y[1, at, :, MX + kx] = cosine
    turn_cos, turn_sin = np_angles(KY, np.arange(quarters) * quarter, full_y, True)
    turn = np.zeros((quarters, 2, WIDE))
    turn[:, 0, :modes] = np.repeat(turn_cos.T, MX, axis=1)
    turn[:, 1, :modes] = np.repeat(turn_sin.T, MX, axis=1)
    z_cos, z_sin = np_angles(KZ, range(full_z), full_z, True)
    z_cos = z_cos.reshape(groups, own_kz, groups, planes)
    z_sin = z_sin.reshape(groups, own_kz, groups, planes)
    forward = np.zeros((groups, 2, own_kz, groups, planes, 2))
    forward[:, 0, :, :, :, 0] = z_cos
    forward[:, 0, :, :, :, 1] = z_sin
    forward[:, 1, :, :, :, 0] = -z_sin
    forward[:, 1, :, :, :, 1] = z_cos
    forward = forward.reshape(groups, 2 * own_kz, groups * planes * 2)
    back_cos = z_cos.transpose(0, 2, 3, 1)
    back_sin = z_sin.transpose(0, 2, 3, 1)
    inverse = np.zeros((groups, groups, planes, 2, own_kz, 2))
    inverse[:, :, :, 0, :, 0] = back_cos
    inverse[:, :, :, 0, :, 1] = -back_sin
    inverse[:, :, :, 1, :, 0] = back_sin
    inverse[:, :, :, 1, :, 1] = back_cos
    inverse = inverse.reshape(groups, groups * planes * 2, own_kz * 2)
    eye = np.eye(share)[None]
    lines = 2 * YB
    to_rows = np.eye(channels * lines).reshape(channels, lines, -1).transpose(1, 0, 2)
    from_rows = np.eye(channels * YB).reshape(YB, channels, -1).transpose(1, 0, 2)

    def low(array):
        return array.astype(np.float32).astype(ml_dtypes.bfloat16)

    return dict(
        to_x=low(to_x.reshape(YB * length_x, YB * SUB)),
        from_x=low(from_x.reshape(YB * SUB, YB * length_x)),
        to_y=low(to_y.reshape(quarter * SUB, 2 * WIDE)),
        from_y=low(from_y.reshape(2 * WIDE, quarter * SUB)),
        turn=turn.astype(np.float32),
        to_rows=low(to_rows.reshape(channels * lines, channels * lines)),
        from_rows=low(from_rows.reshape(channels * YB, channels * YB)),
        to_z=low(np.kron(forward, eye)),
        from_z=low(np.kron(inverse, eye)),
    )


def send(axis, count, source, target, send_sem, recv_sem):
    me = lax.axis_index(axis)
    copies = []
    for step in range(1, count):
        peer = lax.rem(me + step, count)
        copy = pltpu.make_async_remote_copy(
            src_ref=source(peer),
            dst_ref=target(me, step),
            send_sem=send_sem.at[step],
            recv_sem=recv_sem.at[step],
            device_id={axis: peer},
            device_id_type=pl.DeviceIdType.MESH,
        )
        copy.start()
        copies.append(copy)
    return copies


def spectra(field, to_x, to_y):
    blocks, rows, _ = field.shape
    along = jnp.dot(
        field[...].reshape(blocks * rows, -1), to_x[...], preferred_element_type=F32
    ).astype(BF16)
    along = jnp.concatenate([along[b * rows : (b + 1) * rows] for b in range(blocks)], 1)
    return jnp.dot(along, to_y[...], preferred_element_type=F32)


def weigh_modes(spec, weights, modal):
    share = 8
    length = weights.shape[-1]
    for start in range(0, length, 256):
        width = min(256, length - start)
        cols = slice(start, start + width)

        def group(cg, total, cols=cols, width=width):
            real, imag = total
            lines = spec[pl.ds(pl.multiple_of(cg * 16, 16), 16), cols]
            for t in range(share // 2):
                at = pl.ds(pl.multiple_of(cg * share * share + 16 * t, 16), 16)
                w_real = weights[0, at, cols].astype(F32)
                w_imag = weights[1, at, cols].astype(F32)
                parts = []
                for part in range(2):
                    rows = [
                        jnp.broadcast_to(lines[at_row : at_row + 1], (share, width))
                        for at_row in (part * share + 2 * t, part * share + 2 * t + 1)
                    ]
                    parts.append(jnp.concatenate(rows, 0))
                real = real + parts[0] * w_real - parts[1] * w_imag
                imag = imag + parts[0] * w_imag + parts[1] * w_real
            return real, imag

        zero = jnp.zeros((16, width), F32)
        real, imag = lax.fori_loop(0, spec.shape[0] // 16, group, (zero, zero))
        modal[:share, cols] = real[:share] + real[share:]
        modal[share:, cols] = imag[:share] + imag[share:]


def exchange_modes(spectrum, tables, weights, buffers, sems, ready):
    turn_ref, to_z, from_z, from_y = tables
    part, held_sum, all_z, all_c, spec, modal, out_z, held_z, all_o = buffers
    groups, quarters = all_z.shape[0], part.shape[0]
    share = 8
    planes = all_z.shape[1] // (2 * share)
    channels = quarters * share
    own_kz = to_z.shape[1] // (2 * share)
    g, q = lax.axis_index("gz"), lax.axis_index("gy")
    turn = turn_ref[q]
    cosine, sine = turn[0:1], turn[1:2]
    real, imag = spectrum[:, :WIDE], spectrum[:, WIDE:]
    real, imag = cosine * real + sine * imag, cosine * imag - sine * real
    for quarter in range(quarters):
        rows = []
        for z in range(planes):
            at = z * channels + quarter * share
            rows += [real[at : at + share], imag[at : at + share]]
        part[quarter] = jnp.concatenate(rows, 0).astype(BF16)
    ready["greet"]()
    copies = send(
        "gy", quarters, lambda peer: part.at[peer], lambda me, step: held_sum.at[step], *sems[0]
    )
    total = part[q].astype(F32)
    for step, copy in enumerate(copies, 1):
        copy.wait_recv()
        total = total + held_sum[step].astype(F32)
    all_z[g] = total.astype(BF16)
    more = send("gz", groups, lambda peer: all_z.at[g], lambda me, step: all_z.at[me], *sems[1])
    for copy in more:
        copy.wait_recv()
    copies += more
    rows = all_z[...].reshape(-1, WIDE)
    bins = jnp.dot(to_z[g], rows, preferred_element_type=F32)
    modes = KY * MX
    length = 8 * 128
    zero = jnp.zeros((share, length - WIDE), F32)
    halves = []
    for half in range(2):
        for kz in range(own_kz):
            at = (half * own_kz + kz) * share
            wide = jnp.concatenate([bins[at : at + share], zero], 1)
            if kz == 0:
                line = wide
            else:
                line = line + pltpu.roll(wide, kz * modes, 1)
        halves.append(line)
    all_c[q] = jnp.concatenate(halves, 0)[:, : all_c.shape[-1]].astype(BF16)
    more = send("gy", quarters, lambda peer: all_c.at[q], lambda me, step: all_c.at[me], *sems[2])
    for copy in more:
        copy.wait_recv()
    copies += more
    spec[...] = all_c[...].reshape(spec.shape).astype(F32)
    modal[...] = jnp.zeros_like(modal)
    ready["weights"]()
    weigh_modes(spec, weights, modal)
    line = modal[...]
    rows = []
    for kz in range(own_kz):
        moved = line if kz == 0 else pltpu.roll(line, length - kz * modes, 1)
        rows.append(moved[:, :WIDE])
    rows = jnp.concatenate(rows, 0).astype(BF16)
    back = jnp.dot(from_z[g], rows, preferred_element_type=F32)
    out_z[...] = back.astype(BF16).reshape(out_z.shape)
    more = send(
        "gz", groups, lambda peer: out_z.at[peer], lambda me, step: held_z.at[step], *sems[3]
    )
    total = out_z[g].astype(F32)
    for step, copy in enumerate(more, 1):
        copy.wait_recv()
        total = total + held_z[step].astype(F32)
    copies += more
    all_o[q] = total.astype(BF16)
    more = send("gy", quarters, lambda peer: all_o.at[q], lambda me, step: all_o.at[me], *sems[4])
    for copy in more:
        copy.wait_recv()
    copies += more
    ready["from_y"]()
    real, imag = [], []
    pieces = [all_o[quarter].astype(F32) for quarter in range(quarters)]
    for z in range(planes):
        for piece in pieces:
            at = z * 2 * share
            real.append(piece[at : at + share])
            imag.append(piece[at + share : at + 2 * share])
    real, imag = jnp.concatenate(real, 0), jnp.concatenate(imag, 0)
    real, imag = cosine * real - sine * imag, sine * real + cosine * imag
    rows = jnp.concatenate([real, imag], 1).astype(BF16)
    result = jnp.dot(rows, from_y[...], preferred_element_type=F32).astype(BF16)
    for copy in copies:
        copy.wait_send()
    return result


def prepare_maps(skip, lift_t, bias, lift, planes):
    channels, hidden = lift_t.shape
    scaled = bias * F32(HALF)
    high = scaled.astype(BF16).astype(F32)
    middle = (scaled - high).astype(BF16).astype(F32)
    low = scaled - high - middle
    tail = jnp.zeros((128 - channels - 3, hidden), F32)
    tall = jnp.concatenate([lift_t.astype(F32), high, middle, low, tail], 0)
    lift[...] = tall.T.astype(BF16)
    blank = jnp.zeros((channels, channels), F32)
    skip = skip.astype(F32)
    block_rows = []
    for z in range(planes):
        block_rows.append(
            jnp.concatenate([skip if z == other else blank for other in range(planes)], 1)
        )
    return jnp.concatenate(block_rows, 0).astype(BF16)


def pointwise(current, rows_y, from_x, skip_all, lift, down):
    rows, length = current.shape
    channels = down.shape[0]
    planes = rows // channels
    ones = (lax.broadcasted_iota(jnp.int32, (16, planes * length), 0) < 3).astype(F32).astype(BF16)
    spatial = jnp.dot(rows_y, from_x[...], preferred_element_type=F32)
    mixed = spatial + jnp.dot(skip_all, current, preferred_element_type=F32)
    lower = (mixed * F32(HALF)).astype(BF16)
    wide = jnp.concatenate([lower[z * channels : (z + 1) * channels] for z in range(planes)], 1)
    wide = jnp.concatenate([wide, ones], 0)
    value = jnp.dot(lift[:, : channels + 16], wide, preferred_element_type=F32)
    value = (value + value * lax.erf(value)).astype(BF16)
    change = jnp.dot(down, value, preferred_element_type=F32) * F32(HALF)
    return [
        (mixed[z * channels : (z + 1) * channels] + change[:, z * length : (z + 1) * length]).astype(BF16)
        for z in range(planes)
    ]


def meet(groups, quarters):
    barrier = pltpu.get_barrier_semaphore()
    for axis, count in (("gz", groups), ("gy", quarters)):
        me = lax.axis_index(axis)
        for step in range(1, count):
            pl.semaphore_signal(
                barrier,
                inc=1,
                device_id={axis: lax.rem(me + step, count)},
                device_id_type=pl.DeviceIdType.MESH,
            )
    return lambda: pl.semaphore_wait(barrier, groups + quarters - 2)


def loads(pairs, sem):
    copies = [
        pltpu.make_async_copy(source, target, sem.at[at])
        for at, (source, target) in enumerate(pairs)
    ]
    for copy in copies:
        copy.start()
    return copies


def modes_kernel(
    sizes, raw_hbm, to_rows_hbm, to_x_hbm, to_y_hbm, weights_hbm, from_y_hbm, from_x_hbm,
    turn_hbm, to_z_hbm, from_z_hbm, skip_hbm, lift_t_hbm, bias_hbm, down_hbm,
    rows_out, field_hbm, raw, to_rows, to_x, to_y, weights, from_y, from_x, turn, to_z, from_z,
    skip, lift_t, bias, down, field, later, lift, rows_y, local_sem, out_sem, *rest,
):
    groups, quarters = sizes
    layers = weights_hbm.shape[0]
    greeting = meet(groups, quarters)
    channels, planes, quarter, length_x = raw.shape
    lines = 2 * YB
    pieces = quarter // lines
    copies = loads(
        [(to_rows_hbm, to_rows)]
        + [
            (raw_hbm.at[:, :, pl.ds(at * lines, lines)], raw.at[:, :, pl.ds(at * lines, lines)])
            for at in range(pieces)
        ]
        + [(to_x_hbm, to_x), (to_y_hbm, to_y)]
        + [(weights_hbm.at[layer], weights.at[layer]) for layer in range(layers)]
        + [(from_y_hbm, from_y), (from_x_hbm, from_x)]
        + [(turn_hbm, turn), (to_z_hbm, to_z), (from_z_hbm, from_z), (skip_hbm, skip)]
        + [(lift_t_hbm, lift_t), (bias_hbm, bias), (down_hbm, down)],
        local_sem,
    )
    small = copies[-7:]
    copies[0].wait()
    for at in range(pieces):
        copies[1 + at].wait()
        for z in range(planes):
            block = raw[:, z, at * lines : (at + 1) * lines, :].reshape(channels * lines, length_x)
            turned = jnp.dot(to_rows[...], block, preferred_element_type=F32).astype(BF16)
            for y in range(lines):
                field[
                    at * 2 + y // YB,
                    z * channels : (z + 1) * channels,
                    (y % YB) * length_x : (y % YB + 1) * length_x,
                ] = turned[y * channels : (y + 1) * channels]
    copies[1 + pieces].wait()
    copies[2 + pieces].wait()
    waits = copies[3 + pieces :]
    for copy in small:
        copy.wait()
    current = field
    for layer in range(layers):
        if layer > 0:
            skip_all = prepare_maps(
                skip[layer - 1], lift_t[layer - 1], bias[layer - 1 : layer], lift, planes
            )
            if layer == 1:
                waits[layers + 1].wait()
            source, current = current, (later if layer % 2 else field)
            for b in range(quarter // YB):
                parts = pointwise(
                    source[b], rows_y[:, b * YB * SUB : (b + 1) * YB * SUB], from_x, skip_all,
                    lift, down[layer - 1],
                )
                for z, part in enumerate(parts):
                    current[b, z * channels : (z + 1) * channels, :] = part
            if layer == layers - 1:
                leave = pltpu.make_async_copy(current, field_hbm, out_sem.at[0])
                leave.start()
        spectrum = spectra(current, to_x, to_y)
        buffers = rest[9 * layer : 9 * layer + 9]
        at = 9 * layers + 10 * layer
        sems = [(rest[at + 2 * phase], rest[at + 2 * phase + 1]) for phase in range(5)]
        nothing = lambda: None
        ready = {
            "greet": nothing if layer else greeting,
            "weights": waits[layer].wait,
            "from_y": nothing if layer else waits[layers].wait,
        }
        rows = exchange_modes(
            spectrum, (turn, to_z, from_z, from_y), weights.at[layer], buffers, sems, ready
        )
        if layer == layers - 1:
            rows_out[...] = rows
        else:
            rows_y[...] = rows
    leave.wait()


def last_kernel(
    layer, field_hbm, rows_hbm, from_x_hbm, from_rows_hbm, skip_hbm, lift_t_hbm, bias_hbm,
    down_hbm, out_hbm, rows_y, from_x, from_rows, skip, lift_t, bias, down, field, lift, result,
    in_sem, out_sem,
):
    blocks = field.shape[0]
    channels, planes, _, length_x = result.shape
    lines = 2 * YB
    steps = blocks // 2
    copies = loads(
        [
            (skip_hbm, skip), (lift_t_hbm, lift_t), (bias_hbm, bias), (down_hbm, down),
            (rows_hbm, rows_y), (from_x_hbm, from_x), (from_rows_hbm, from_rows),
        ]
        + [(field_hbm.at[pl.ds(2 * at, 2)], field.at[pl.ds(2 * at, 2)]) for at in range(steps)],
        in_sem,
    )
    for copy in copies[:7]:
        copy.wait()
    copies = copies[7:]
    skip_all = prepare_maps(skip[layer], lift_t[layer], bias[layer : layer + 1], lift, planes)
    outs = []
    for at in range(steps):
        copies[at].wait()
        turned = [[] for _ in range(planes)]
        for b in (2 * at, 2 * at + 1):
            parts = pointwise(
                field[b], rows_y[:, b * YB * SUB : (b + 1) * YB * SUB], from_x, skip_all, lift,
                down[layer],
            )
            for z, part in enumerate(parts):
                tall = jnp.concatenate(
                    [part[:, j * length_x : (j + 1) * length_x] for j in range(YB)], 0
                )
                tall = jnp.dot(from_rows[...], tall, preferred_element_type=F32)
                turned[z].append(tall.reshape(channels, YB, length_x))
        window = pl.ds(at * lines, lines)
        for z in range(planes):
            result[:, z, window, :] = jnp.concatenate(turned[z], 1).astype(BF16)
        copy = pltpu.make_async_copy(
            result.at[:, :, window], out_hbm.at[:, :, window], out_sem.at[at]
        )
        copy.start()
        outs.append(copy)
    for copy in outs:
        copy.wait()


def fast_device(noisy_field, spectral_weights, skip_weights, in_weights, in_bias, out_weights):
    channels, planes, quarter, length_x = noisy_field.shape
    layer_count = spectral_weights.shape[0]
    groups, quarters = lax.axis_size("gz"), lax.axis_size("gy")
    own_kz = KZ // groups
    own_modes = spectral_weights.shape[2]
    share = channels // quarters
    blocks = quarter // YB
    hidden = in_weights.shape[1]
    tables = np_tables(groups, quarters, planes, quarter, length_x, channels)
    tables = {name: jnp.asarray(value) for name, value in tables.items()}
    weights = spectral_weights.transpose(0, 1, 3, 4, 2)
    weights = weights.reshape(layer_count, 2, channels * share, own_modes)
    lift_t = in_weights.transpose(0, 2, 1)
    rows_shape = jax.ShapeDtypeStruct((planes * channels, quarter * SUB), BF16)
    field_shape = jax.ShapeDtypeStruct((blocks, planes * channels, YB * length_x), BF16)
    anywhere = pl.BlockSpec(memory_space=pltpu.HBM)
    vmem = pl.BlockSpec(memory_space=pltpu.VMEM)

    def held(name):
        return pltpu.VMEM(tables[name].shape, tables[name].dtype)

    full = -(-own_modes // 128) * 128
    block = (planes * 2 * share, WIDE)
    traffic = [
        pltpu.VMEM((quarters,) + block, BF16),
        pltpu.VMEM((quarters,) + block, BF16),
        pltpu.VMEM((groups,) + block, BF16),
        pltpu.VMEM((quarters, 2 * share, full), BF16),
        pltpu.VMEM((quarters * 2 * share, full), F32),
        pltpu.VMEM((2 * share, 8 * 128), F32),
        pltpu.VMEM((groups,) + block, BF16),
        pltpu.VMEM((groups,) + block, BF16),
        pltpu.VMEM((quarters,) + block, BF16),
    ]
    signals = []
    for count in (quarters, groups, quarters, groups, quarters):
        signals += [pltpu.SemaphoreType.DMA((count,))] * 2
    lift_held = pltpu.VMEM((hidden, 128), BF16)
    field_held = pltpu.VMEM(field_shape.shape, BF16)
    raw_held = pltpu.VMEM(noisy_field.shape, BF16)
    maps = (skip_weights, lift_t, in_bias, out_weights)
    maps_held = [pltpu.VMEM(value.shape, value.dtype) for value in maps]
    pieces = quarter // (2 * YB)
    rows, field = pl.pallas_call(
        functools.partial(modes_kernel, (groups, quarters)),
        out_shape=[rows_shape, field_shape],
        in_specs=[anywhere] * 14,
        out_specs=[vmem, anywhere],
        scratch_shapes=[
            raw_held, held("to_rows"), held("to_x"), held("to_y"),
            pltpu.VMEM(weights.shape, BF16), held("from_y"), held("from_x"),
            held("turn"), held("to_z"), held("from_z"), *maps_held, field_held, field_held, lift_held, pltpu.VMEM(rows_shape.shape, BF16),
            pltpu.SemaphoreType.DMA((12 + pieces + layer_count,)), pltpu.SemaphoreType.DMA((1,)),
        ] + traffic * layer_count + signals * layer_count,
        compiler_params=pltpu.CompilerParams(
            collective_id=0, has_side_effects=True, vmem_limit_bytes=VMEM_LIMIT
        ),
        name="modes",
    )(
        noisy_field, tables["to_rows"], tables["to_x"], tables["to_y"], weights, tables["from_y"],
        tables["from_x"], tables["turn"], tables["to_z"], tables["from_z"], *maps,
    )
    return pl.pallas_call(
        functools.partial(last_kernel, layer_count - 1),
        out_shape=jax.ShapeDtypeStruct(noisy_field.shape, BF16),
        in_specs=[anywhere, pl.BlockSpec(memory_space=pl.ANY)] + [anywhere] * 6,
        out_specs=anywhere,
        scratch_shapes=[
            pltpu.VMEM(rows_shape.shape, BF16), held("from_x"), held("from_rows"), *maps_held,
            field_held, lift_held, raw_held, pltpu.SemaphoreType.DMA((7 + pieces,)),
            pltpu.SemaphoreType.DMA((pieces,)),
        ],
        compiler_params=pltpu.CompilerParams(vmem_limit_bytes=VMEM_LIMIT),
        name="last_layer",
    )(field, rows, tables["from_x"], tables["from_rows"], *maps)


def pick(noisy_field, spectral_weights, *rest):
    groups, quarters = lax.axis_size("gz"), lax.axis_size("gy")
    channels, planes, quarter, _ = noisy_field.shape
    fits = (
        KZ % groups == 0
        and spectral_weights.shape[2] == KZ // groups * KY * MX
        and spectral_weights.shape[2] <= 8 * 128 - 128
        and channels == 8 * quarters
        and planes == 2
        and quarter % (2 * YB) == 0
    )
    body = fast_device if fits else per_device
    return body(noisy_field, spectral_weights, *rest)


def solution(mesh):
    in_specs = (P(None, "gz", "gy", None), P(None, None, "gz", None, "gy"), P(), P(), P(), P())
    out_specs = P(None, "gz", "gy", None)
    return jax.shard_map(
        pick, mesh=mesh, in_specs=in_specs, out_specs=out_specs, check_vma=False
    )
```

```python
import functools
import math

import jax
import jax.numpy as jnp
from jax import lax
from jax.experimental import pallas as pl
from jax.experimental.pallas import tpu as pltpu
from jax.sharding import PartitionSpec as P
import ml_dtypes
import numpy as np

MX = 12
KY = 24
KZ = 24
KP = KY // 2
LANES = 128
ROWS = 32
F32 = jnp.float32
BF16 = jnp.bfloat16


def angles(number, positions, length, signed):
    kept = jnp.arange(number, dtype=jnp.int32)
    if signed:
        kept = jnp.where(kept < number // 2, kept, kept - number)
    phases = jnp.mod(kept[:, None] * positions[None, :], length)
    radians = 2.0 * math.pi / length * phases.astype(jnp.float32)
    return (jnp.cos(radians), jnp.sin(radians))


def forward_table(length):
    cosine, sine = angles(MX, jnp.arange(length, dtype=jnp.int32), length, False)
    part = jnp.concatenate([cosine, -sine, -sine, -cosine], 0)
    table = jnp.concatenate([part, part], 0).T.astype(BF16)
    return jnp.pad(table, ((0, 0), (0, LANES - 8 * MX)))


def inverse_table(length):
    cosine, sine = angles(MX, jnp.arange(length, dtype=jnp.int32), length, False)
    factor = jnp.where(jnp.arange(MX) == 0, F32(1.0), F32(2.0))[:, None]
    scale = 1.0 / math.sqrt(2.0 * KZ * KY * MX)
    half = jnp.concatenate([cosine * factor, -sine * factor], 0) * scale
    table = jnp.concatenate([half] * 4, 0).astype(BF16)
    return jnp.pad(table, ((0, LANES - 8 * MX), (0, 0)))


def y_weights(positions, length):
    cosine, sine = angles(KY, positions, length, True)
    both = jnp.stack([cosine, sine], -1).transpose(1, 0, 2)
    lanes = jnp.repeat(both.reshape(positions.shape[0], KP, 4), 2 * MX, axis=2)
    return jnp.pad(lanes, ((0, 0), (0, 0), (0, LANES - 8 * MX)))


def gelu(value):
    return 0.5 * value * (1.0 + lax.erf(value * F32(math.sqrt(0.5))))


def accumulate_modes(along, weight_ref, modes_ref):
    rows, channels = along.shape[0], along.shape[1]

    @pl.when(pl.program_id(1) == 0)
    def _():
        modes_ref[...] = jnp.zeros_like(modes_ref)

    for kp in range(KP):
        total = along[0] * weight_ref[0, kp : kp + 1, :]
        for y in range(1, rows):
            total = total + along[y] * weight_ref[y, kp : kp + 1, :]
        modes_ref[0, kp] += total


def forward_kernel(field_ref, weight_ref, table_ref, modes_ref):
    rows, channels, length = field_ref.shape
    flat = field_ref[...].reshape(rows * channels, length)
    along = jnp.dot(flat, table_ref[...], preferred_element_type=F32)
    accumulate_modes(along.reshape(rows, channels, LANES), weight_ref, modes_ref)


def layer_body(
    field_ref, planes_ref, weight_ref, inverse_ref, skip_ref, lift_ref, bias_ref, down_ref, out_ref
):
    rows, channels, length = field_ref.shape
    parts = []
    for y in range(rows):
        total = planes_ref[0, 0] * weight_ref[y, 0:1, :]
        for kp in range(1, KP):
            total = total + planes_ref[0, kp] * weight_ref[y, kp : kp + 1, :]
        parts.append(total.astype(BF16))
    stacked = jnp.concatenate(parts, 0)
    spatial = jnp.dot(stacked, inverse_ref[...], preferred_element_type=F32)
    wide_spatial = jnp.concatenate(
        [spatial[y * channels : (y + 1) * channels] for y in range(rows)], 1
    )
    wide_field = jnp.concatenate([field_ref[y] for y in range(rows)], 1)
    mixed = wide_spatial + jnp.dot(skip_ref[...], wide_field, preferred_element_type=F32)
    before = jnp.dot(lift_ref[...], mixed.astype(BF16), preferred_element_type=F32)
    hidden = gelu(before + bias_ref[...]).astype(BF16)
    result = mixed + jnp.dot(down_ref[...], hidden, preferred_element_type=F32)
    result = result.astype(BF16)
    for y in range(rows):
        out_ref[y] = result[:, y * length : (y + 1) * length]


def middle_kernel(
    field_ref, planes_ref, weight_ref, inverse_ref, skip_ref, lift_ref, bias_ref, down_ref,
    table_ref, out_ref, modes_ref,
):
    layer_body(
        field_ref, planes_ref, weight_ref, inverse_ref, skip_ref, lift_ref, bias_ref, down_ref,
        out_ref,
    )
    forward_kernel(out_ref, weight_ref, table_ref, modes_ref)


def whole(shape):
    return pl.BlockSpec(shape, lambda z, y: (0,) * len(shape))


def run_forward(field, weights_y, table, planes):
    total, channels, length = field.shape
    steps = total // planes // ROWS
    return pl.pallas_call(
        forward_kernel,
        grid=(planes, steps),
        in_specs=[
            pl.BlockSpec((ROWS, channels, length), lambda z, y: (z * steps + y, 0, 0)),
            pl.BlockSpec((ROWS, KP, LANES), lambda z, y: (y, 0, 0)),
            whole(table.shape),
        ],
        out_specs=pl.BlockSpec((1, KP, channels, LANES), lambda z, y: (z, 0, 0, 0)),
        out_shape=jax.ShapeDtypeStruct((planes, KP, channels, LANES), F32),
        name="forward_modes",
    )(field, weights_y, table)


def run_layer(field, plane_modes, weights_y, inverse, skip, lift, bias, down, table):
    total, channels, length = field.shape
    planes = plane_modes.shape[0]
    steps = total // planes // ROWS
    field_spec = pl.BlockSpec((ROWS, channels, length), lambda z, y: (z * steps + y, 0, 0))
    modes_spec = pl.BlockSpec((1, KP, channels, LANES), lambda z, y: (z, 0, 0, 0))
    field_shape = jax.ShapeDtypeStruct(field.shape, BF16)
    modes_shape = jax.ShapeDtypeStruct(plane_modes.shape, F32)
    args = [field, plane_modes, weights_y, inverse, skip, lift, bias, down]
    specs = [
        field_spec,
        modes_spec,
        pl.BlockSpec((ROWS, KP, LANES), lambda z, y: (y, 0, 0)),
        whole(inverse.shape),
        whole(skip.shape),
        whole(lift.shape),
        whole(bias.shape),
        whole(down.shape),
    ]
    if table is None:
        return pl.pallas_call(
            layer_body,
            grid=(planes, steps),
            in_specs=specs,
            out_specs=field_spec,
            out_shape=field_shape,
            name="last_layer",
        )(*args)
    return pl.pallas_call(
        middle_kernel,
        grid=(planes, steps),
        in_specs=specs + [whole(table.shape)],
        out_specs=[field_spec, modes_spec],
        out_shape=[field_shape, modes_shape],
        name="middle_layer",
    )(*args, table)


def fold_modes(modes, scale):
    planes, _, channels, _ = modes.shape
    split = modes[..., : 8 * MX].reshape(planes, KP, channels, 2, 2, 2, MX)
    folded = (split[:, :, :, :, 0] + split[:, :, :, :, 1]) * scale
    ordered = folded.transpose(0, 4, 2, 1, 3, 5)
    return ordered.reshape(planes * 2, channels, KY * MX)


def unfold_modes(rows, planes):
    channels = rows.shape[1]
    real, imag = (
        rows.astype(F32).reshape(planes, 2, channels, KP, 2, MX)[:, part] for part in range(2)
    )
    lanes = jnp.stack([real, imag, -imag, real], axis=4)
    lanes = lanes.transpose(0, 2, 1, 3, 4, 5).reshape(planes, KP, channels, 8 * MX)
    return jnp.pad(lanes, ((0, 0), (0, 0), (0, 0), (0, LANES - 8 * MX)))


def greet(axes):
    barrier = pltpu.get_barrier_semaphore()
    total = 0
    for axis, count in axes:
        me = lax.axis_index(axis)
        for step in range(1, count):
            pl.semaphore_signal(
                barrier,
                inc=1,
                device_id={axis: lax.rem(me + step, count)},
                device_id_type=pl.DeviceIdType.MESH,
            )
        total += count - 1
    pl.semaphore_wait(barrier, total)


def spread(axis, count, source, held, send_sem, recv_sem):
    me = lax.axis_index(axis)
    copies = []
    for step in range(1, count):
        peer = lax.rem(me + step, count)
        copy = pltpu.make_async_remote_copy(
            src_ref=source(peer),
            dst_ref=held.at[step],
            send_sem=send_sem.at[step],
            recv_sem=recv_sem.at[step],
            device_id={axis: peer},
            device_id_type=pl.DeviceIdType.MESH,
        )
        copy.start()
        copies.append(copy)
    return copies


def collect(axis, count, own, held, copies, out_ref):
    me = lax.axis_index(axis)
    out_ref[me] = own
    for step, copy in enumerate(copies, 1):
        copy.wait_recv()
        out_ref[lax.rem(me - step + count, count)] = held[step]


def z_and_y(groups, quarters, own_ref, matrix_ref, out_ref, held_z, all_z, stage, held_y, sems):
    send_z, recv_z, send_y, recv_y = sems
    first = spread("gz", groups, lambda peer: own_ref, held_z, send_z, recv_z)
    collect("gz", groups, own_ref[...], held_z, first, all_z)
    rows = all_z[...].reshape(-1, all_z.shape[-1]).astype(F32)
    stage[...] = jnp.dot(
        matrix_ref[...], rows, precision=lax.Precision.HIGHEST, preferred_element_type=F32
    ).astype(BF16)
    second = spread("gy", quarters, lambda peer: stage, held_y, send_y, recv_y)
    collect("gy", quarters, stage[...], held_y, second, out_ref)
    return first + second


def sum_kernel(
    groups, quarters, own_ref, matrix_ref, out_ref, held_sum, summed, held_z, all_z, stage, held_y,
    send_sum, recv_sum, *sems,
):
    greet((("gz", groups), ("gy", quarters)))
    copies = spread("gy", quarters, lambda peer: own_ref.at[peer], held_sum, send_sum, recv_sum)
    total = own_ref[lax.axis_index("gy")]
    for step, copy in enumerate(copies, 1):
        copy.wait_recv()
        total = total + held_sum[step]
    summed[...] = total.astype(BF16)
    copies += z_and_y(
        groups, quarters, summed, matrix_ref, out_ref, held_z, all_z, stage, held_y, sems
    )
    for copy in copies:
        copy.wait_send()


def spread_kernel(
    groups, quarters, own_ref, matrix_ref, out_ref, held_z, all_z, stage, held_y, *sems
):
    greet((("gz", groups), ("gy", quarters)))
    copies = z_and_y(
        groups, quarters, own_ref, matrix_ref, out_ref, held_z, all_z, stage, held_y, sems
    )
    for copy in copies:
        copy.wait_send()


def communicate(value, matrix, summing, number):
    groups, quarters = lax.axis_size("gz"), lax.axis_size("gy")
    block = value.shape[-2:]
    result = (matrix.shape[0], block[1])
    vmem = pl.BlockSpec(memory_space=pltpu.VMEM)
    scratch = [
        pltpu.VMEM((groups,) + block, BF16),
        pltpu.VMEM((groups,) + block, BF16),
        pltpu.VMEM(result, BF16),
        pltpu.VMEM((quarters,) + result, BF16),
    ]
    sems = [pltpu.SemaphoreType.DMA((count,)) for count in (groups, groups, quarters, quarters)]
    if summing:
        scratch = [pltpu.VMEM((quarters,) + block, F32), pltpu.VMEM(block, BF16)] + scratch
        sems = [pltpu.SemaphoreType.DMA((quarters,))] * 2 + sems
    return pl.pallas_call(
        functools.partial(sum_kernel if summing else spread_kernel, groups, quarters),
        out_shape=jax.ShapeDtypeStruct((quarters,) + result, BF16),
        in_specs=[vmem, vmem],
        out_specs=vmem,
        scratch_shapes=scratch + sems,
        compiler_params=pltpu.CompilerParams(collective_id=number, has_side_effects=True),
        name="exchange",
    )(value, matrix)


def z_matrix(cosine, sine, inverse):
    sign = -1.0 if inverse else 1.0
    return jnp.stack(
        [jnp.stack([cosine, sign * sine]), jnp.stack([-sign * sine, cosine])]
    )


def weigh(spectrum, coefficients):
    real, imag = spectrum[0], spectrum[1]

    def product(left, right):
        return jnp.einsum("zcq,zqco->zoq", left, right, preferred_element_type=F32)

    modal_real = product(real, coefficients[0]) - product(imag, coefficients[1])
    modal_imag = product(real, coefficients[1]) + product(imag, coefficients[0])
    return jnp.stack([modal_real, modal_imag]).astype(BF16)


def exchange(partial, local_weights, planes, full_z, number):
    highest = lax.Precision.HIGHEST
    channels = partial.shape[1]
    modes = KY * MX
    here_z = lax.axis_index("gz") * planes + jnp.arange(planes, dtype=jnp.int32)
    all_z = jnp.arange(full_z, dtype=jnp.int32)
    own_modes = local_weights.shape[1]
    groups = lax.axis_size("gz")
    if own_modes % modes == 0:
        own_kz = own_modes // modes
        cosine, sine = angles(KZ, all_z, full_z, True)
        first = lax.axis_index("gz") * own_kz
        cosine = lax.dynamic_slice_in_dim(cosine, first, own_kz, 0)
        sine = lax.dynamic_slice_in_dim(sine, first, own_kz, 0)
        forward = z_matrix(cosine, sine, False).transpose(0, 2, 3, 1)
        forward = forward.reshape(2 * own_kz, 2 * full_z)
        quarters = lax.axis_size("gy")
        share = channels // quarters
        split = partial.reshape(planes * 2, quarters, share, modes).transpose(1, 0, 2, 3)
        spectrum = communicate(
            split.reshape(quarters, planes * 2 * share, modes),
            jnp.kron(forward, jnp.eye(share, dtype=F32)),
            True,
            number,
        )
        spectrum = spectrum.reshape(quarters, 2, own_kz, share, modes).transpose(1, 2, 0, 3, 4)
        spectrum = spectrum.reshape(2, own_kz, channels, modes)
        coefficients = local_weights.reshape(2, own_kz, modes, channels, -1)
        modal = weigh(spectrum, coefficients)
        outputs = modal.shape[2]
        cosine, sine = angles(KZ, here_z, full_z, True)
        inverse = z_matrix(cosine, sine, True).reshape(2, 2, groups, own_kz, planes)
        inverse = inverse.transpose(4, 0, 2, 1, 3).reshape(planes * 2, groups * 2 * own_kz)
        rows = communicate(
            modal.reshape(2 * own_kz * outputs, modes),
            jnp.kron(inverse, jnp.eye(outputs, dtype=F32)),
            False,
            number + 1,
        )
        rows = rows.reshape(quarters, planes * 2, outputs, modes).transpose(1, 0, 2, 3)
        return rows.reshape(planes * 2, channels, modes)
    cosine, sine = angles(KZ, here_z, full_z, True)
    forward = z_matrix(cosine, sine, False).transpose(0, 2, 3, 1)
    sums = jnp.einsum(
        "akr,rcq->ackq", forward.reshape(2, KZ, planes * 2), partial, precision=highest
    ).reshape(2, channels, KZ * modes)
    sums = lax.psum_scatter(sums, "gz", scatter_dimension=2, tiled=True)
    spectrum = lax.psum(sums, "gy").astype(BF16)[:, None]
    coefficients = lax.all_gather(local_weights, "gy", axis=3, tiled=True)[:, None]
    modal = weigh(spectrum, coefficients)[:, 0]
    modal = lax.all_gather(modal, "gz", axis=2, tiled=True)
    modal = modal.astype(F32).reshape(2, channels, KZ, modes)
    inverse = z_matrix(cosine, sine, True)
    rows = jnp.einsum("abkz,bckq->zacq", inverse, modal, precision=highest)
    return rows.reshape(planes * 2, channels, modes)


def per_device(noisy_field, spectral_weights, skip_weights, in_weights, in_bias, out_weights):
    channels, planes, quarter, length_x = noisy_field.shape
    layer_count = spectral_weights.shape[0]
    full_y = quarter * lax.axis_size("gy")
    full_z = planes * lax.axis_size("gz")
    y_positions = lax.axis_index("gy") * quarter + jnp.arange(quarter, dtype=jnp.int32)
    weights_y = y_weights(y_positions, full_y)
    table = forward_table(length_x)
    inverse = inverse_table(length_x)
    scale = 1.0 / math.sqrt(length_x * full_y * full_z)
    field = noisy_field.transpose(1, 2, 0, 3).reshape(planes * quarter, channels, length_x)
    modes = run_forward(field, weights_y, table, planes)
    for layer in range(layer_count):
        rows = exchange(
            fold_modes(modes, scale), spectral_weights[layer], planes, full_z, 2 * layer
        )
        last = layer == layer_count - 1
        result = run_layer(
            field,
            unfold_modes(rows, planes),
            weights_y,
            inverse,
            skip_weights[layer],
            in_weights[layer],
            in_bias[layer][:, None],
            out_weights[layer],
            None if last else table,
        )
        if last:
            field = result
        else:
            field, modes = result
    return field.reshape(planes, quarter, channels, length_x).transpose(2, 0, 1, 3)


HALF = math.sqrt(0.5)
WIDE = 384
SUB = 32
YB = 8
VMEM_LIMIT = 60 * 2**20


def np_angles(number, positions, length, signed):
    kept = np.arange(number)
    if signed:
        kept = np.where(kept < number // 2, kept, kept - number)
    phases = np.mod(kept[:, None] * np.asarray(positions)[None, :], length)
    radians = 2.0 * math.pi / length * phases
    return np.cos(radians), np.sin(radians)


def np_tables(groups, quarters, planes, quarter, length_x, channels):
    full_y, full_z = quarter * quarters, planes * groups
    share = channels // quarters
    own_kz = KZ // groups
    modes = KY * MX
    x_cos, x_sin = np_angles(MX, range(length_x), length_x, False)
    to_x = np.zeros((YB, length_x, YB, SUB))
    from_x = np.zeros((YB, SUB, YB, length_x))
    factor = np.where(np.arange(MX) == 0, 1.0, 2.0)[:, None] / math.sqrt(2.0 * KZ * KY * MX)
    for j in range(YB):
        to_x[j, :, j, :MX] = x_cos.T
        to_x[j, :, j, MX : 2 * MX] = -x_sin.T
        from_x[j, :MX, j, :] = x_cos * factor
        from_x[j, MX : 2 * MX, j, :] = -x_sin * factor
    y_cos, y_sin = np_angles(KY, range(quarter), full_y, True)
    to_y = np.zeros((quarter, SUB, 2, WIDE))
    from_y = np.zeros((2, WIDE, quarter, SUB))
    scale = 1.0 / math.sqrt(length_x * full_y * full_z)
    for ky in range(KY):
        for kx in range(MX):
            at = ky * MX + kx
            cosine, sine = y_cos[ky], y_sin[ky]
            to_y[:, kx, 0, at] = cosine * scale
            to_y[:, MX + kx, 0, at] = sine * scale
            to_y[:, kx, 1, at] = -sine * scale
            to_y[:, MX + kx, 1, at] = cosine * scale
            from_y[0, at, :, kx] = cosine
            from_y[1, at, :, kx] = -sine
            from_y[0, at, :, MX + kx] = sine
            from_y[1, at, :, MX + kx] = cosine
    turn_cos, turn_sin = np_angles(KY, np.arange(quarters) * quarter, full_y, True)
    turn = np.zeros((quarters, 2, WIDE))
    turn[:, 0, :modes] = np.repeat(turn_cos.T, MX, axis=1)
    turn[:, 1, :modes] = np.repeat(turn_sin.T, MX, axis=1)
    z_cos, z_sin = np_angles(KZ, range(full_z), full_z, True)
    z_cos = z_cos.reshape(groups, own_kz, groups, planes)
    z_sin = z_sin.reshape(groups, own_kz, groups, planes)
    forward = np.zeros((groups, 2, own_kz, groups, planes, 2))
    forward[:, 0, :, :, :, 0] = z_cos
    forward[:, 0, :, :, :, 1] = z_sin
    forward[:, 1, :, :, :, 0] = -z_sin
    forward[:, 1, :, :, :, 1] = z_cos
    forward = forward.reshape(groups, 2 * own_kz, groups * planes * 2)
    back_cos = z_cos.transpose(0, 2, 3, 1)
    back_sin = z_sin.transpose(0, 2, 3, 1)
    inverse = np.zeros((groups, groups, planes, 2, own_kz, 2))
    inverse[:, :, :, 0, :, 0] = back_cos
    inverse[:, :, :, 0, :, 1] = -back_sin
    inverse[:, :, :, 1, :, 0] = back_sin
    inverse[:, :, :, 1, :, 1] = back_cos
    inverse = inverse.reshape(groups, groups * planes * 2, own_kz * 2)
    eye = np.eye(share)[None]
    lines = 2 * YB
    to_rows = np.eye(channels * lines).reshape(channels, lines, -1).transpose(1, 0, 2)
    from_rows = np.eye(channels * YB).reshape(YB, channels, -1).transpose(1, 0, 2)

    def low(array):
        return array.astype(np.float32).astype(ml_dtypes.bfloat16)

    return dict(
        to_x=low(to_x.reshape(YB * length_x, YB * SUB)),
        from_x=low(from_x.reshape(YB * SUB, YB * length_x)),
        to_y=low(to_y.reshape(quarter * SUB, 2 * WIDE)),
        from_y=low(from_y.reshape(2 * WIDE, quarter * SUB)),
        turn=turn.astype(np.float32),
        to_rows=low(to_rows.reshape(channels * lines, channels * lines)),
        from_rows=low(from_rows.reshape(channels * YB, channels * YB)),
        to_z=low(np.kron(forward, eye)),
        from_z=low(np.kron(inverse, eye)),
    )


def pack(blocks):
    tail = blocks[0][:, 256:]
    for at, block in enumerate(blocks[1:], 1):
        tail = tail + pltpu.roll(block[:, 256:], at * 32, 1)
    firsts = [block[:, :128] for block in blocks]
    seconds = [block[:, 128:256] for block in blocks]
    return jnp.concatenate(firsts + seconds + [tail], 0)


def unpack(piece):
    tail = piece[64:72]
    blocks = []
    for at in range(4):
        rest = tail if at == 0 else pltpu.roll(tail, 128 - at * 32, 1)
        blocks.append(
            jnp.concatenate([piece[at * 8 : at * 8 + 8], piece[32 + at * 8 : 40 + at * 8], rest], 1)
        )
    return blocks


def send(axis, count, source, target, send_sem, recv_sem):
    me = lax.axis_index(axis)
    copies = []
    for step in range(1, count):
        peer = lax.rem(me + step, count)
        copy = pltpu.make_async_remote_copy(
            src_ref=source(peer),
            dst_ref=target(me, step),
            send_sem=send_sem.at[step],
            recv_sem=recv_sem.at[step],
            device_id={axis: peer},
            device_id_type=pl.DeviceIdType.MESH,
        )
        copy.start()
        copies.append(copy)
    return copies


def spectra(field, to_x, to_y):
    blocks, rows, _ = field.shape
    along = jnp.dot(
        field[...].reshape(blocks * rows, -1), to_x[...], preferred_element_type=F32
    ).astype(BF16)
    along = jnp.concatenate([along[b * rows : (b + 1) * rows] for b in range(blocks)], 1)
    return jnp.dot(along, to_y[...], preferred_element_type=F32)


def weigh_modes(spec, weights, modal):
    share = 8
    length = weights.shape[-1]
    for start in range(0, length, 256):
        width = min(256, length - start)
        cols = slice(start, start + width)

        def group(cg, total, cols=cols, width=width):
            real, imag = total
            lines = spec[pl.ds(pl.multiple_of(cg * 16, 16), 16), cols]
            for t in range(share // 2):
                at = pl.ds(pl.multiple_of(cg * share * share + 16 * t, 16), 16)
                w_real = weights[0, at, cols].astype(F32)
                w_imag = weights[1, at, cols].astype(F32)
                parts = []
                for part in range(2):
                    rows = [
                        jnp.broadcast_to(lines[at_row : at_row + 1], (share, width))
                        for at_row in (part * share + 2 * t, part * share + 2 * t + 1)
                    ]
                    parts.append(jnp.concatenate(rows, 0))
                real = real + parts[0] * w_real - parts[1] * w_imag
                imag = imag + parts[0] * w_imag + parts[1] * w_real
            return real, imag

        zero = jnp.zeros((16, width), F32)
        real, imag = lax.fori_loop(0, spec.shape[0] // 16, group, (zero, zero))
        modal[:share, cols] = real[:share] + real[share:]
        modal[share:, cols] = imag[:share] + imag[share:]


def exchange_modes(spectrum, tables, weights, buffers, sems, ready):
    turn_ref, to_z, from_z, from_y = tables
    part, held_sum, all_z, all_c, spec, modal, out_z, held_z, all_o = buffers
    groups, quarters = all_z.shape[0], part.shape[0]
    share = 8
    planes = to_z.shape[2] // (2 * share * groups)
    channels = quarters * share
    kept = lax.broadcasted_iota(jnp.int32, (1, WIDE), 1) < KY * MX
    own_kz = to_z.shape[1] // (2 * share)
    g, q = lax.axis_index("gz"), lax.axis_index("gy")
    turn = turn_ref[q]
    cosine, sine = turn[0:1], turn[1:2]
    real, imag = spectrum[:, :WIDE], spectrum[:, WIDE:]
    real, imag = cosine * real + sine * imag, cosine * imag - sine * real
    for quarter in range(quarters):
        rows = []
        for z in range(planes):
            at = z * channels + quarter * share
            rows += [real[at : at + share], imag[at : at + share]]
        part[quarter] = pack(rows).astype(BF16)
    ready["greet"]()
    copies = send(
        "gy", quarters, lambda peer: part.at[peer], lambda me, step: held_sum.at[step], *sems[0]
    )
    total = part[q].astype(F32)
    for step, copy in enumerate(copies, 1):
        copy.wait_recv()
        total = total + held_sum[step].astype(F32)
    all_z[g] = total.astype(BF16)
    more = send("gz", groups, lambda peer: all_z.at[g], lambda me, step: all_z.at[me], *sems[1])
    for copy in more:
        copy.wait_recv()
    copies += more
    ready["to_z"]()
    rows = []
    for group in range(groups):
        rows += unpack(all_z[group].astype(F32))
    rows = jnp.concatenate(rows, 0).astype(BF16)
    bins = jnp.where(kept, jnp.dot(to_z[g], rows, preferred_element_type=F32), 0.0)
    modes = KY * MX
    length = 8 * 128
    zero = jnp.zeros((share, length - WIDE), F32)
    halves = []
    for half in range(2):
        for kz in range(own_kz):
            at = (half * own_kz + kz) * share
            wide = jnp.concatenate([bins[at : at + share], zero], 1)
            if kz == 0:
                line = wide
            else:
                line = line + pltpu.roll(wide, kz * modes, 1)
        halves.append(line)
    all_c[q] = jnp.concatenate(halves, 0)[:, : all_c.shape[-1]].astype(BF16)
    more = send("gy", quarters, lambda peer: all_c.at[q], lambda me, step: all_c.at[me], *sems[2])
    for copy in more:
        copy.wait_recv()
    copies += more
    spec[...] = all_c[...].reshape(spec.shape).astype(F32)
    modal[...] = jnp.zeros_like(modal)
    ready["weights"]()
    weigh_modes(spec, weights, modal)
    line = modal[...]
    rows = []
    for kz in range(own_kz):
        moved = line if kz == 0 else pltpu.roll(line, length - kz * modes, 1)
        rows.append(moved[:, :WIDE])
    rows = jnp.concatenate(rows, 0).astype(BF16)
    ready["from_z"]()
    back = jnp.dot(from_z[g], rows, preferred_element_type=F32)
    back = jnp.where(kept, back, 0.0)
    for group in range(groups):
        first = group * planes * 2 * share
        blocks = [back[first + at * share : first + (at + 1) * share] for at in range(2 * planes)]
        out_z[group] = pack(blocks).astype(BF16)
    more = send(
        "gz", groups, lambda peer: out_z.at[peer], lambda me, step: held_z.at[step], *sems[3]
    )
    total = out_z[g].astype(F32)
    for step, copy in enumerate(more, 1):
        copy.wait_recv()
        total = total + held_z[step].astype(F32)
    copies += more
    all_o[q] = total.astype(BF16)
    more = send("gy", quarters, lambda peer: all_o.at[q], lambda me, step: all_o.at[me], *sems[4])
    for copy in more:
        copy.wait_recv()
    copies += more
    ready["from_y"]()
    real, imag = [], []
    pieces = [unpack(all_o[quarter].astype(F32)) for quarter in range(quarters)]
    for z in range(planes):
        for piece in pieces:
            real.append(piece[2 * z])
            imag.append(piece[2 * z + 1])
    real, imag = jnp.concatenate(real, 0), jnp.concatenate(imag, 0)
    real, imag = cosine * real - sine * imag, sine * real + cosine * imag
    rows = jnp.concatenate([real, imag], 1).astype(BF16)
    result = jnp.dot(rows, from_y[...], preferred_element_type=F32).astype(BF16)
    for copy in copies:
        copy.wait_send()
    return result


def prepare_maps(skip, lift_t, bias, lift, planes):
    channels, hidden = lift_t.shape
    scaled = bias * F32(HALF)
    high = scaled.astype(BF16).astype(F32)
    middle = (scaled - high).astype(BF16).astype(F32)
    low = scaled - high - middle
    tail = jnp.zeros((128 - channels - 3, hidden), F32)
    tall = jnp.concatenate([lift_t.astype(F32), high, middle, low, tail], 0)
    lift[...] = tall.T.astype(BF16)
    blank = jnp.zeros((channels, channels), F32)
    skip = skip.astype(F32)
    block_rows = []
    for z in range(planes):
        block_rows.append(
            jnp.concatenate([skip if z == other else blank for other in range(planes)], 1)
        )
    return jnp.concatenate(block_rows, 0).astype(BF16)


def pointwise(current, rows_y, from_x, skip_all, lift, down):
    rows, length = current.shape
    channels = down.shape[0]
    planes = rows // channels
    ones = (lax.broadcasted_iota(jnp.int32, (16, planes * length), 0) < 3).astype(F32).astype(BF16)
    mixed = jnp.dot(
        jnp.concatenate([rows_y, skip_all], 1),
        jnp.concatenate([from_x[...], current], 0),
        preferred_element_type=F32,
    )
    lower = (mixed * F32(HALF)).astype(BF16)
    wide = jnp.concatenate([lower[z * channels : (z + 1) * channels] for z in range(planes)], 1)
    wide = jnp.concatenate([wide, ones], 0)
    value = jnp.dot(lift[:, : channels + 16], wide, preferred_element_type=F32)
    value = (value + value * lax.erf(value)).astype(BF16)
    change = jnp.dot(down, value, preferred_element_type=F32) * F32(HALF)
    return [
        (mixed[z * channels : (z + 1) * channels] + change[:, z * length : (z + 1) * length]).astype(BF16)
        for z in range(planes)
    ]


def meet(groups, quarters):
    barrier = pltpu.get_barrier_semaphore()
    for axis, count in (("gz", groups), ("gy", quarters)):
        me = lax.axis_index(axis)
        for step in range(1, count):
            pl.semaphore_signal(
                barrier,
                inc=1,
                device_id={axis: lax.rem(me + step, count)},
                device_id_type=pl.DeviceIdType.MESH,
            )
    return lambda: pl.semaphore_wait(barrier, groups + quarters - 2)


def loads(pairs, sem):
    copies = [
        pltpu.make_async_copy(source, target, sem.at[at])
        for at, (source, target) in enumerate(pairs)
    ]
    for copy in copies:
        copy.start()
    return copies


def modes_kernel(
    sizes, raw_hbm, to_rows_hbm, to_x_hbm, to_y_hbm, weights_hbm, from_y_hbm, from_x_hbm,
    turn_hbm, to_z_hbm, from_z_hbm, skip_hbm, lift_t_hbm, bias_hbm, down_hbm,
    rows_out, field_hbm, raw, to_rows, to_x, to_y, weights, from_y, from_x, turn, to_z, from_z,
    skip, lift_t, bias, down, field, later, lift, rows_y, local_sem, late_sem, out_sem, *rest,
):
    groups, quarters = sizes
    layers = weights_hbm.shape[0]
    greeting = meet(groups, quarters)
    channels, planes, quarter, length_x = raw.shape
    lines = 2 * YB
    pieces = quarter // lines
    copies = loads(
        [(to_rows_hbm, to_rows)]
        + [
            (raw_hbm.at[:, :, pl.ds(at * lines, lines)], raw.at[:, :, pl.ds(at * lines, lines)])
            for at in range(pieces)
        ]
        + [(to_x_hbm, to_x), (to_y_hbm, to_y), (turn_hbm, turn)],
        local_sem,
    )
    copies[0].wait()
    for at in range(pieces):
        copies[1 + at].wait()
        for z in range(planes):
            block = raw[:, z, at * lines : (at + 1) * lines, :].reshape(channels * lines, length_x)
            turned = jnp.dot(to_rows[...], block, preferred_element_type=F32).astype(BF16)
            for y in range(lines):
                field[
                    at * 2 + y // YB,
                    z * channels : (z + 1) * channels,
                    (y % YB) * length_x : (y % YB + 1) * length_x,
                ] = turned[y * channels : (y + 1) * channels]
    for copy in copies[1 + pieces :]:
        copy.wait()
    waits = loads(
        [(to_z_hbm, to_z)]
        + [(weights_hbm.at[layer], weights.at[layer]) for layer in range(layers)]
        + [(from_z_hbm, from_z), (from_y_hbm, from_y), (from_x_hbm, from_x)]
        + [(skip_hbm, skip), (lift_t_hbm, lift_t), (bias_hbm, bias), (down_hbm, down)],
        late_sem,
    )
    current = field
    for layer in range(layers):
        if layer > 0:
            if layer == 1:
                for copy in waits[layers + 3 :]:
                    copy.wait()
            skip_all = prepare_maps(
                skip[layer - 1], lift_t[layer - 1], bias[layer - 1 : layer], lift, planes
            )
            source, current = current, (later if layer % 2 else field)
            for b in range(quarter // YB):
                parts = pointwise(
                    source[b], rows_y[:, b * YB * SUB : (b + 1) * YB * SUB], from_x, skip_all,
                    lift, down[layer - 1],
                )
                for z, part in enumerate(parts):
                    current[b, z * channels : (z + 1) * channels, :] = part
            if layer == layers - 1:
                leave = pltpu.make_async_copy(current, field_hbm, out_sem.at[0])
                leave.start()
        spectrum = spectra(current, to_x, to_y)
        buffers = rest[9 * layer : 9 * layer + 9]
        at = 9 * layers + 10 * layer
        sems = [(rest[at + 2 * phase], rest[at + 2 * phase + 1]) for phase in range(5)]
        nothing = lambda: None
        ready = {
            "greet": nothing if layer else greeting,
            "to_z": nothing if layer else waits[0].wait,
            "weights": waits[1 + layer].wait,
            "from_z": nothing if layer else waits[layers + 1].wait,
            "from_y": nothing if layer else waits[layers + 2].wait,
        }
        rows = exchange_modes(
            spectrum, (turn, to_z, from_z, from_y), weights.at[layer], buffers, sems, ready
        )
        if layer == layers - 1:
            rows_out[...] = rows
        else:
            rows_y[...] = rows
    leave.wait()


def last_kernel(
    layer, field_hbm, rows_hbm, from_x_hbm, from_rows_hbm, skip_hbm, lift_t_hbm, bias_hbm,
    down_hbm, out_hbm, rows_y, from_x, from_rows, skip, lift_t, bias, down, field, lift, result,
    in_sem, out_sem,
):
    blocks = field.shape[0]
    channels, planes, _, length_x = result.shape
    lines = 2 * YB
    steps = blocks // 2
    copies = loads(
        [
            (skip_hbm, skip), (lift_t_hbm, lift_t), (bias_hbm, bias), (down_hbm, down),
            (rows_hbm, rows_y), (from_x_hbm, from_x), (from_rows_hbm, from_rows),
        ]
        + [(field_hbm.at[pl.ds(2 * at, 2)], field.at[pl.ds(2 * at, 2)]) for at in range(steps)],
        in_sem,
    )
    for copy in copies[:7]:
        copy.wait()
    copies = copies[7:]
    skip_all = prepare_maps(skip[layer], lift_t[layer], bias[layer : layer + 1], lift, planes)
    outs = []
    for at in range(steps):
        copies[at].wait()
        turned = [[] for _ in range(planes)]
        for b in (2 * at, 2 * at + 1):
            parts = pointwise(
                field[b], rows_y[:, b * YB * SUB : (b + 1) * YB * SUB], from_x, skip_all, lift,
                down[layer],
            )
            for z, part in enumerate(parts):
                tall = jnp.concatenate(
                    [part[:, j * length_x : (j + 1) * length_x] for j in range(YB)], 0
                )
                tall = jnp.dot(from_rows[...], tall, preferred_element_type=F32)
                turned[z].append(tall.reshape(channels, YB, length_x))
        window = pl.ds(at * lines, lines)
        for z in range(planes):
            result[:, z, window, :] = jnp.concatenate(turned[z], 1).astype(BF16)
        copy = pltpu.make_async_copy(
            result.at[:, :, window], out_hbm.at[:, :, window], out_sem.at[at]
        )
        copy.start()
        outs.append(copy)
    for copy in outs:
        copy.wait()


def fast_device(noisy_field, spectral_weights, skip_weights, in_weights, in_bias, out_weights):
    channels, planes, quarter, length_x = noisy_field.shape
    layer_count = spectral_weights.shape[0]
    groups, quarters = lax.axis_size("gz"), lax.axis_size("gy")
    own_kz = KZ // groups
    own_modes = spectral_weights.shape[2]
    share = channels // quarters
    blocks = quarter // YB
    hidden = in_weights.shape[1]
    tables = np_tables(groups, quarters, planes, quarter, length_x, channels)
    tables = {name: jnp.asarray(value) for name, value in tables.items()}
    weights = spectral_weights.transpose(0, 1, 3, 4, 2)
    weights = weights.reshape(layer_count, 2, channels * share, own_modes)
    lift_t = in_weights.transpose(0, 2, 1)
    rows_shape = jax.ShapeDtypeStruct((planes * channels, quarter * SUB), BF16)
    field_shape = jax.ShapeDtypeStruct((blocks, planes * channels, YB * length_x), BF16)
    anywhere = pl.BlockSpec(memory_space=pltpu.HBM)
    vmem = pl.BlockSpec(memory_space=pltpu.VMEM)

    def held(name):
        return pltpu.VMEM(tables[name].shape, tables[name].dtype)

    full = -(-own_modes // 128) * 128
    block = (planes * 2 * share * 2 + share, 128)
    traffic = [
        pltpu.VMEM((quarters,) + block, BF16),
        pltpu.VMEM((quarters,) + block, BF16),
        pltpu.VMEM((groups,) + block, BF16),
        pltpu.VMEM((quarters, 2 * share, full), BF16),
        pltpu.VMEM((quarters * 2 * share, full), F32),
        pltpu.VMEM((2 * share, 8 * 128), F32),
        pltpu.VMEM((groups,) + block, BF16),
        pltpu.VMEM((groups,) + block, BF16),
        pltpu.VMEM((quarters,) + block, BF16),
    ]
    signals = []
    for count in (quarters, groups, quarters, groups, quarters):
        signals += [pltpu.SemaphoreType.DMA((count,))] * 2
    lift_held = pltpu.VMEM((hidden, 128), BF16)
    field_held = pltpu.VMEM(field_shape.shape, BF16)
    raw_held = pltpu.VMEM(noisy_field.shape, BF16)
    maps = (skip_weights, lift_t, in_bias, out_weights)
    maps_held = [pltpu.VMEM(value.shape, value.dtype) for value in maps]
    pieces = quarter // (2 * YB)
    rows, field = pl.pallas_call(
        functools.partial(modes_kernel, (groups, quarters)),
        out_shape=[rows_shape, field_shape],
        in_specs=[anywhere] * 14,
        out_specs=[vmem, anywhere],
        scratch_shapes=[
            raw_held, held("to_rows"), held("to_x"), held("to_y"),
            pltpu.VMEM(weights.shape, BF16), held("from_y"), held("from_x"),
            held("turn"), held("to_z"), held("from_z"), *maps_held, field_held, field_held, lift_held, pltpu.VMEM(rows_shape.shape, BF16),
            pltpu.SemaphoreType.DMA((4 + pieces,)), pltpu.SemaphoreType.DMA((8 + layer_count,)),
            pltpu.SemaphoreType.DMA((1,)),
        ] + traffic * layer_count + signals * layer_count,
        compiler_params=pltpu.CompilerParams(
            collective_id=0, has_side_effects=True, vmem_limit_bytes=VMEM_LIMIT
        ),
        name="modes",
    )(
        noisy_field, tables["to_rows"], tables["to_x"], tables["to_y"], weights, tables["from_y"],
        tables["from_x"], tables["turn"], tables["to_z"], tables["from_z"], *maps,
    )
    return pl.pallas_call(
        functools.partial(last_kernel, layer_count - 1),
        out_shape=jax.ShapeDtypeStruct(noisy_field.shape, BF16),
        in_specs=[anywhere, pl.BlockSpec(memory_space=pl.ANY)] + [anywhere] * 6,
        out_specs=anywhere,
        scratch_shapes=[
            pltpu.VMEM(rows_shape.shape, BF16), held("from_x"), held("from_rows"), *maps_held,
            field_held, lift_held, raw_held, pltpu.SemaphoreType.DMA((7 + pieces,)),
            pltpu.SemaphoreType.DMA((pieces,)),
        ],
        compiler_params=pltpu.CompilerParams(vmem_limit_bytes=VMEM_LIMIT),
        name="last_layer",
    )(field, rows, tables["from_x"], tables["from_rows"], *maps)


def pick(noisy_field, spectral_weights, *rest):
    groups, quarters = lax.axis_size("gz"), lax.axis_size("gy")
    channels, planes, quarter, _ = noisy_field.shape
    fits = (
        KZ % groups == 0
        and spectral_weights.shape[2] == KZ // groups * KY * MX
        and spectral_weights.shape[2] <= 8 * 128 - 128
        and channels == 8 * quarters
        and planes == 2
        and quarter % (2 * YB) == 0
    )
    body = fast_device if fits else per_device
    return body(noisy_field, spectral_weights, *rest)


def solution(mesh):
    in_specs = (P(None, "gz", "gy", None), P(None, None, "gz", None, "gy"), P(), P(), P(), P())
    out_specs = P(None, "gz", "gy", None)
    return jax.shard_map(
        pick, mesh=mesh, in_specs=in_specs, out_specs=out_specs, check_vma=False
    )
```

```python
import functools
import math

import jax
import jax.numpy as jnp
from jax import lax
from jax.experimental import pallas as pl
from jax.experimental.pallas import tpu as pltpu
from jax.sharding import PartitionSpec as P
import ml_dtypes
import numpy as np

MX = 12
KY = 24
KZ = 24
KP = KY // 2
LANES = 128
ROWS = 32
F32 = jnp.float32
BF16 = jnp.bfloat16


def angles(number, positions, length, signed):
    kept = jnp.arange(number, dtype=jnp.int32)
    if signed:
        kept = jnp.where(kept < number // 2, kept, kept - number)
    phases = jnp.mod(kept[:, None] * positions[None, :], length)
    radians = 2.0 * math.pi / length * phases.astype(jnp.float32)
    return (jnp.cos(radians), jnp.sin(radians))


def forward_table(length):
    cosine, sine = angles(MX, jnp.arange(length, dtype=jnp.int32), length, False)
    part = jnp.concatenate([cosine, -sine, -sine, -cosine], 0)
    table = jnp.concatenate([part, part], 0).T.astype(BF16)
    return jnp.pad(table, ((0, 0), (0, LANES - 8 * MX)))


def inverse_table(length):
    cosine, sine = angles(MX, jnp.arange(length, dtype=jnp.int32), length, False)
    factor = jnp.where(jnp.arange(MX) == 0, F32(1.0), F32(2.0))[:, None]
    scale = 1.0 / math.sqrt(2.0 * KZ * KY * MX)
    half = jnp.concatenate([cosine * factor, -sine * factor], 0) * scale
    table = jnp.concatenate([half] * 4, 0).astype(BF16)
    return jnp.pad(table, ((0, LANES - 8 * MX), (0, 0)))


def y_weights(positions, length):
    cosine, sine = angles(KY, positions, length, True)
    both = jnp.stack([cosine, sine], -1).transpose(1, 0, 2)
    lanes = jnp.repeat(both.reshape(positions.shape[0], KP, 4), 2 * MX, axis=2)
    return jnp.pad(lanes, ((0, 0), (0, 0), (0, LANES - 8 * MX)))


def gelu(value):
    return 0.5 * value * (1.0 + lax.erf(value * F32(math.sqrt(0.5))))


def accumulate_modes(along, weight_ref, modes_ref):
    rows, channels = along.shape[0], along.shape[1]

    @pl.when(pl.program_id(1) == 0)
    def _():
        modes_ref[...] = jnp.zeros_like(modes_ref)

    for kp in range(KP):
        total = along[0] * weight_ref[0, kp : kp + 1, :]
        for y in range(1, rows):
            total = total + along[y] * weight_ref[y, kp : kp + 1, :]
        modes_ref[0, kp] += total


def forward_kernel(field_ref, weight_ref, table_ref, modes_ref):
    rows, channels, length = field_ref.shape
    flat = field_ref[...].reshape(rows * channels, length)
    along = jnp.dot(flat, table_ref[...], preferred_element_type=F32)
    accumulate_modes(along.reshape(rows, channels, LANES), weight_ref, modes_ref)


def layer_body(
    field_ref, planes_ref, weight_ref, inverse_ref, skip_ref, lift_ref, bias_ref, down_ref, out_ref
):
    rows, channels, length = field_ref.shape
    parts = []
    for y in range(rows):
        total = planes_ref[0, 0] * weight_ref[y, 0:1, :]
        for kp in range(1, KP):
            total = total + planes_ref[0, kp] * weight_ref[y, kp : kp + 1, :]
        parts.append(total.astype(BF16))
    stacked = jnp.concatenate(parts, 0)
    spatial = jnp.dot(stacked, inverse_ref[...], preferred_element_type=F32)
    wide_spatial = jnp.concatenate(
        [spatial[y * channels : (y + 1) * channels] for y in range(rows)], 1
    )
    wide_field = jnp.concatenate([field_ref[y] for y in range(rows)], 1)
    mixed = wide_spatial + jnp.dot(skip_ref[...], wide_field, preferred_element_type=F32)
    before = jnp.dot(lift_ref[...], mixed.astype(BF16), preferred_element_type=F32)
    hidden = gelu(before + bias_ref[...]).astype(BF16)
    result = mixed + jnp.dot(down_ref[...], hidden, preferred_element_type=F32)
    result = result.astype(BF16)
    for y in range(rows):
        out_ref[y] = result[:, y * length : (y + 1) * length]


def middle_kernel(
    field_ref, planes_ref, weight_ref, inverse_ref, skip_ref, lift_ref, bias_ref, down_ref,
    table_ref, out_ref, modes_ref,
):
    layer_body(
        field_ref, planes_ref, weight_ref, inverse_ref, skip_ref, lift_ref, bias_ref, down_ref,
        out_ref,
    )
    forward_kernel(out_ref, weight_ref, table_ref, modes_ref)


def whole(shape):
    return pl.BlockSpec(shape, lambda z, y: (0,) * len(shape))


def run_forward(field, weights_y, table, planes):
    total, channels, length = field.shape
    steps = total // planes // ROWS
    return pl.pallas_call(
        forward_kernel,
        grid=(planes, steps),
        in_specs=[
            pl.BlockSpec((ROWS, channels, length), lambda z, y: (z * steps + y, 0, 0)),
            pl.BlockSpec((ROWS, KP, LANES), lambda z, y: (y, 0, 0)),
            whole(table.shape),
        ],
        out_specs=pl.BlockSpec((1, KP, channels, LANES), lambda z, y: (z, 0, 0, 0)),
        out_shape=jax.ShapeDtypeStruct((planes, KP, channels, LANES), F32),
        name="forward_modes",
    )(field, weights_y, table)


def run_layer(field, plane_modes, weights_y, inverse, skip, lift, bias, down, table):
    total, channels, length = field.shape
    planes = plane_modes.shape[0]
    steps = total // planes // ROWS
    field_spec = pl.BlockSpec((ROWS, channels, length), lambda z, y: (z * steps + y, 0, 0))
    modes_spec = pl.BlockSpec((1, KP, channels, LANES), lambda z, y: (z, 0, 0, 0))
    field_shape = jax.ShapeDtypeStruct(field.shape, BF16)
    modes_shape = jax.ShapeDtypeStruct(plane_modes.shape, F32)
    args = [field, plane_modes, weights_y, inverse, skip, lift, bias, down]
    specs = [
        field_spec,
        modes_spec,
        pl.BlockSpec((ROWS, KP, LANES), lambda z, y: (y, 0, 0)),
        whole(inverse.shape),
        whole(skip.shape),
        whole(lift.shape),
        whole(bias.shape),
        whole(down.shape),
    ]
    if table is None:
        return pl.pallas_call(
            layer_body,
            grid=(planes, steps),
            in_specs=specs,
            out_specs=field_spec,
            out_shape=field_shape,
            name="last_layer",
        )(*args)
    return pl.pallas_call(
        middle_kernel,
        grid=(planes, steps),
        in_specs=specs + [whole(table.shape)],
        out_specs=[field_spec, modes_spec],
        out_shape=[field_shape, modes_shape],
        name="middle_layer",
    )(*args, table)


def fold_modes(modes, scale):
    planes, _, channels, _ = modes.shape
    split = modes[..., : 8 * MX].reshape(planes, KP, channels, 2, 2, 2, MX)
    folded = (split[:, :, :, :, 0] + split[:, :, :, :, 1]) * scale
    ordered = folded.transpose(0, 4, 2, 1, 3, 5)
    return ordered.reshape(planes * 2, channels, KY * MX)


def unfold_modes(rows, planes):
    channels = rows.shape[1]
    real, imag = (
        rows.astype(F32).reshape(planes, 2, channels, KP, 2, MX)[:, part] for part in range(2)
    )
    lanes = jnp.stack([real, imag, -imag, real], axis=4)
    lanes = lanes.transpose(0, 2, 1, 3, 4, 5).reshape(planes, KP, channels, 8 * MX)
    return jnp.pad(lanes, ((0, 0), (0, 0), (0, 0), (0, LANES - 8 * MX)))


def greet(axes):
    barrier = pltpu.get_barrier_semaphore()
    total = 0
    for axis, count in axes:
        me = lax.axis_index(axis)
        for step in range(1, count):
            pl.semaphore_signal(
                barrier,
                inc=1,
                device_id={axis: lax.rem(me + step, count)},
                device_id_type=pl.DeviceIdType.MESH,
            )
        total += count - 1
    pl.semaphore_wait(barrier, total)


def spread(axis, count, source, held, send_sem, recv_sem):
    me = lax.axis_index(axis)
    copies = []
    for step in range(1, count):
        peer = lax.rem(me + step, count)
        copy = pltpu.make_async_remote_copy(
            src_ref=source(peer),
            dst_ref=held.at[step],
            send_sem=send_sem.at[step],
            recv_sem=recv_sem.at[step],
            device_id={axis: peer},
            device_id_type=pl.DeviceIdType.MESH,
        )
        copy.start()
        copies.append(copy)
    return copies


def collect(axis, count, own, held, copies, out_ref):
    me = lax.axis_index(axis)
    out_ref[me] = own
    for step, copy in enumerate(copies, 1):
        copy.wait_recv()
        out_ref[lax.rem(me - step + count, count)] = held[step]


def z_and_y(groups, quarters, own_ref, matrix_ref, out_ref, held_z, all_z, stage, held_y, sems):
    send_z, recv_z, send_y, recv_y = sems
    first = spread("gz", groups, lambda peer: own_ref, held_z, send_z, recv_z)
    collect("gz", groups, own_ref[...], held_z, first, all_z)
    rows = all_z[...].reshape(-1, all_z.shape[-1]).astype(F32)
    stage[...] = jnp.dot(
        matrix_ref[...], rows, precision=lax.Precision.HIGHEST, preferred_element_type=F32
    ).astype(BF16)
    second = spread("gy", quarters, lambda peer: stage, held_y, send_y, recv_y)
    collect("gy", quarters, stage[...], held_y, second, out_ref)
    return first + second


def sum_kernel(
    groups, quarters, own_ref, matrix_ref, out_ref, held_sum, summed, held_z, all_z, stage, held_y,
    send_sum, recv_sum, *sems,
):
    greet((("gz", groups), ("gy", quarters)))
    copies = spread("gy", quarters, lambda peer: own_ref.at[peer], held_sum, send_sum, recv_sum)
    total = own_ref[lax.axis_index("gy")]
    for step, copy in enumerate(copies, 1):
        copy.wait_recv()
        total = total + held_sum[step]
    summed[...] = total.astype(BF16)
    copies += z_and_y(
        groups, quarters, summed, matrix_ref, out_ref, held_z, all_z, stage, held_y, sems
    )
    for copy in copies:
        copy.wait_send()


def spread_kernel(
    groups, quarters, own_ref, matrix_ref, out_ref, held_z, all_z, stage, held_y, *sems
):
    greet((("gz", groups), ("gy", quarters)))
    copies = z_and_y(
        groups, quarters, own_ref, matrix_ref, out_ref, held_z, all_z, stage, held_y, sems
    )
    for copy in copies:
        copy.wait_send()


def communicate(value, matrix, summing, number):
    groups, quarters = lax.axis_size("gz"), lax.axis_size("gy")
    block = value.shape[-2:]
    result = (matrix.shape[0], block[1])
    vmem = pl.BlockSpec(memory_space=pltpu.VMEM)
    scratch = [
        pltpu.VMEM((groups,) + block, BF16),
        pltpu.VMEM((groups,) + block, BF16),
        pltpu.VMEM(result, BF16),
        pltpu.VMEM((quarters,) + result, BF16),
    ]
    sems = [pltpu.SemaphoreType.DMA((count,)) for count in (groups, groups, quarters, quarters)]
    if summing:
        scratch = [pltpu.VMEM((quarters,) + block, F32), pltpu.VMEM(block, BF16)] + scratch
        sems = [pltpu.SemaphoreType.DMA((quarters,))] * 2 + sems
    return pl.pallas_call(
        functools.partial(sum_kernel if summing else spread_kernel, groups, quarters),
        out_shape=jax.ShapeDtypeStruct((quarters,) + result, BF16),
        in_specs=[vmem, vmem],
        out_specs=vmem,
        scratch_shapes=scratch + sems,
        compiler_params=pltpu.CompilerParams(collective_id=number, has_side_effects=True),
        name="exchange",
    )(value, matrix)


def z_matrix(cosine, sine, inverse):
    sign = -1.0 if inverse else 1.0
    return jnp.stack(
        [jnp.stack([cosine, sign * sine]), jnp.stack([-sign * sine, cosine])]
    )


def weigh(spectrum, coefficients):
    real, imag = spectrum[0], spectrum[1]

    def product(left, right):
        return jnp.einsum("zcq,zqco->zoq", left, right, preferred_element_type=F32)

    modal_real = product(real, coefficients[0]) - product(imag, coefficients[1])
    modal_imag = product(real, coefficients[1]) + product(imag, coefficients[0])
    return jnp.stack([modal_real, modal_imag]).astype(BF16)


def exchange(partial, local_weights, planes, full_z, number):
    highest = lax.Precision.HIGHEST
    channels = partial.shape[1]
    modes = KY * MX
    here_z = lax.axis_index("gz") * planes + jnp.arange(planes, dtype=jnp.int32)
    all_z = jnp.arange(full_z, dtype=jnp.int32)
    own_modes = local_weights.shape[1]
    groups = lax.axis_size("gz")
    if own_modes % modes == 0:
        own_kz = own_modes // modes
        cosine, sine = angles(KZ, all_z, full_z, True)
        first = lax.axis_index("gz") * own_kz
        cosine = lax.dynamic_slice_in_dim(cosine, first, own_kz, 0)
        sine = lax.dynamic_slice_in_dim(sine, first, own_kz, 0)
        forward = z_matrix(cosine, sine, False).transpose(0, 2, 3, 1)
        forward = forward.reshape(2 * own_kz, 2 * full_z)
        quarters = lax.axis_size("gy")
        share = channels // quarters
        split = partial.reshape(planes * 2, quarters, share, modes).transpose(1, 0, 2, 3)
        spectrum = communicate(
            split.reshape(quarters, planes * 2 * share, modes),
            jnp.kron(forward, jnp.eye(share, dtype=F32)),
            True,
            number,
        )
        spectrum = spectrum.reshape(quarters, 2, own_kz, share, modes).transpose(1, 2, 0, 3, 4)
        spectrum = spectrum.reshape(2, own_kz, channels, modes)
        coefficients = local_weights.reshape(2, own_kz, modes, channels, -1)
        modal = weigh(spectrum, coefficients)
        outputs = modal.shape[2]
        cosine, sine = angles(KZ, here_z, full_z, True)
        inverse = z_matrix(cosine, sine, True).reshape(2, 2, groups, own_kz, planes)
        inverse = inverse.transpose(4, 0, 2, 1, 3).reshape(planes * 2, groups * 2 * own_kz)
        rows = communicate(
            modal.reshape(2 * own_kz * outputs, modes),
            jnp.kron(inverse, jnp.eye(outputs, dtype=F32)),
            False,
            number + 1,
        )
        rows = rows.reshape(quarters, planes * 2, outputs, modes).transpose(1, 0, 2, 3)
        return rows.reshape(planes * 2, channels, modes)
    cosine, sine = angles(KZ, here_z, full_z, True)
    forward = z_matrix(cosine, sine, False).transpose(0, 2, 3, 1)
    sums = jnp.einsum(
        "akr,rcq->ackq", forward.reshape(2, KZ, planes * 2), partial, precision=highest
    ).reshape(2, channels, KZ * modes)
    sums = lax.psum_scatter(sums, "gz", scatter_dimension=2, tiled=True)
    spectrum = lax.psum(sums, "gy").astype(BF16)[:, None]
    coefficients = lax.all_gather(local_weights, "gy", axis=3, tiled=True)[:, None]
    modal = weigh(spectrum, coefficients)[:, 0]
    modal = lax.all_gather(modal, "gz", axis=2, tiled=True)
    modal = modal.astype(F32).reshape(2, channels, KZ, modes)
    inverse = z_matrix(cosine, sine, True)
    rows = jnp.einsum("abkz,bckq->zacq", inverse, modal, precision=highest)
    return rows.reshape(planes * 2, channels, modes)


def per_device(noisy_field, spectral_weights, skip_weights, in_weights, in_bias, out_weights):
    channels, planes, quarter, length_x = noisy_field.shape
    layer_count = spectral_weights.shape[0]
    full_y = quarter * lax.axis_size("gy")
    full_z = planes * lax.axis_size("gz")
    y_positions = lax.axis_index("gy") * quarter + jnp.arange(quarter, dtype=jnp.int32)
    weights_y = y_weights(y_positions, full_y)
    table = forward_table(length_x)
    inverse = inverse_table(length_x)
    scale = 1.0 / math.sqrt(length_x * full_y * full_z)
    field = noisy_field.transpose(1, 2, 0, 3).reshape(planes * quarter, channels, length_x)
    modes = run_forward(field, weights_y, table, planes)
    for layer in range(layer_count):
        rows = exchange(
            fold_modes(modes, scale), spectral_weights[layer], planes, full_z, 2 * layer
        )
        last = layer == layer_count - 1
        result = run_layer(
            field,
            unfold_modes(rows, planes),
            weights_y,
            inverse,
            skip_weights[layer],
            in_weights[layer],
            in_bias[layer][:, None],
            out_weights[layer],
            None if last else table,
        )
        if last:
            field = result
        else:
            field, modes = result
    return field.reshape(planes, quarter, channels, length_x).transpose(2, 0, 1, 3)


HALF = math.sqrt(0.5)
WIDE = 384
SUB = 32
YB = 8
HJ = 4
VMEM_LIMIT = 60 * 2**20


def np_angles(number, positions, length, signed):
    kept = np.arange(number)
    if signed:
        kept = np.where(kept < number // 2, kept, kept - number)
    phases = np.mod(kept[:, None] * np.asarray(positions)[None, :], length)
    radians = 2.0 * math.pi / length * phases
    return np.cos(radians), np.sin(radians)


def np_tables(groups, quarters, planes, quarter, length_x, channels):
    full_y, full_z = quarter * quarters, planes * groups
    share = channels // quarters
    own_kz = KZ // groups
    modes = KY * MX
    x_cos, x_sin = np_angles(MX, range(length_x), length_x, False)
    to_x = np.zeros((HJ, length_x, HJ, SUB))
    from_x = np.zeros((HJ, SUB, HJ, length_x))
    factor = np.where(np.arange(MX) == 0, 1.0, 2.0)[:, None] / math.sqrt(2.0 * KZ * KY * MX)
    for j in range(HJ):
        to_x[j, :, j, :MX] = x_cos.T
        to_x[j, :, j, MX : 2 * MX] = -x_sin.T
        from_x[j, :MX, j, :] = x_cos * factor
        from_x[j, MX : 2 * MX, j, :] = -x_sin * factor
    y_cos, y_sin = np_angles(KY, range(quarter), full_y, True)
    to_y = np.zeros((quarter, SUB, 2, WIDE))
    from_y = np.zeros((2, WIDE, quarter, SUB))
    scale = 1.0 / math.sqrt(length_x * full_y * full_z)
    for ky in range(KY):
        for kx in range(MX):
            at = ky * MX + kx
            cosine, sine = y_cos[ky], y_sin[ky]
            to_y[:, kx, 0, at] = cosine * scale
            to_y[:, MX + kx, 0, at] = sine * scale
            to_y[:, kx, 1, at] = -sine * scale
            to_y[:, MX + kx, 1, at] = cosine * scale
            from_y[0, at, :, kx] = cosine
            from_y[1, at, :, kx] = -sine
            from_y[0, at, :, MX + kx] = sine
            from_y[1, at, :, MX + kx] = cosine
    turn_cos, turn_sin = np_angles(KY, np.arange(quarters) * quarter, full_y, True)
    turn = np.zeros((quarters, 2, WIDE))
    turn[:, 0, :modes] = np.repeat(turn_cos.T, MX, axis=1)
    turn[:, 1, :modes] = np.repeat(turn_sin.T, MX, axis=1)
    z_cos, z_sin = np_angles(KZ, range(full_z), full_z, True)
    z_cos = z_cos.reshape(groups, own_kz, groups, planes)
    z_sin = z_sin.reshape(groups, own_kz, groups, planes)
    forward = np.zeros((groups, 2, own_kz, groups, planes, 2))
    forward[:, 0, :, :, :, 0] = z_cos
    forward[:, 0, :, :, :, 1] = z_sin
    forward[:, 1, :, :, :, 0] = -z_sin
    forward[:, 1, :, :, :, 1] = z_cos
    forward = forward.reshape(groups, 2 * own_kz, groups * planes * 2)
    back_cos = z_cos.transpose(0, 2, 3, 1)
    back_sin = z_sin.transpose(0, 2, 3, 1)
    inverse = np.zeros((groups, groups, planes, 2, own_kz, 2))
    inverse[:, :, :, 0, :, 0] = back_cos
    inverse[:, :, :, 0, :, 1] = -back_sin
    inverse[:, :, :, 1, :, 0] = back_sin
    inverse[:, :, :, 1, :, 1] = back_cos
    inverse = inverse.reshape(groups, groups * planes * 2, own_kz * 2)
    eye = np.eye(share)[None]
    to_rows = np.eye(channels * YB).reshape(channels, YB, -1).transpose(1, 0, 2)
    from_rows = np.eye(channels * YB).reshape(YB, channels, -1).transpose(1, 0, 2)

    def low(array):
        return array.astype(np.float32).astype(ml_dtypes.bfloat16)

    return dict(
        to_x=low(to_x.reshape(HJ * length_x, HJ * SUB)),
        from_x=low(from_x.reshape(HJ * SUB, HJ * length_x)),
        to_y=low(to_y.reshape(quarter * SUB, 2 * WIDE)),
        from_y=low(from_y.reshape(2 * WIDE, quarter * SUB)),
        turn=turn.astype(np.float32),
        to_rows=low(to_rows.reshape(channels * YB, channels * YB)),
        from_rows=low(from_rows.reshape(channels * YB, channels * YB)),
        to_z=low(np.kron(forward, eye)),
        from_z=low(np.kron(inverse, eye)),
    )


def pack(blocks):
    tail = blocks[0][:, 256:]
    for at, block in enumerate(blocks[1:], 1):
        tail = tail + pltpu.roll(block[:, 256:], at * 32, 1)
    firsts = [block[:, :128] for block in blocks]
    seconds = [block[:, 128:256] for block in blocks]
    return jnp.concatenate(firsts + seconds + [tail], 0)


def unpack(piece):
    tail = piece[64:72]
    blocks = []
    for at in range(4):
        rest = tail if at == 0 else pltpu.roll(tail, 128 - at * 32, 1)
        blocks.append(
            jnp.concatenate([piece[at * 8 : at * 8 + 8], piece[32 + at * 8 : 40 + at * 8], rest], 1)
        )
    return blocks


def send(axis, count, source, target, send_sem, recv_sem):
    me = lax.axis_index(axis)
    copies = []
    for step in range(1, count):
        peer = lax.rem(me + step, count)
        copy = pltpu.make_async_remote_copy(
            src_ref=source(peer),
            dst_ref=target(me, step),
            send_sem=send_sem.at[step],
            recv_sem=recv_sem.at[step],
            device_id={axis: peer},
            device_id_type=pl.DeviceIdType.MESH,
        )
        copy.start()
        copies.append(copy)
    return copies


def along_x(field, first, count, to_x):
    rows = field.shape[1]
    depth, width = to_x.shape
    parts = []
    for b in range(first, first + count):
        for half in range(YB // HJ):
            parts.append(field[b, :, half * depth : (half + 1) * depth])
    along = jnp.dot(jnp.concatenate(parts, 0), to_x[...], preferred_element_type=F32).astype(BF16)
    return [along[at * rows : (at + 1) * rows] for at in range(len(parts))]


def weigh_modes(spec, weights, modal):
    share = 8
    length = weights.shape[-1]
    for start in range(0, length, 256):
        width = min(256, length - start)
        cols = slice(start, start + width)

        def group(cg, total, cols=cols, width=width):
            real, imag = total
            lines = spec[pl.ds(pl.multiple_of(cg * 16, 16), 16), cols]
            for t in range(share // 2):
                at = pl.ds(pl.multiple_of(cg * share * share + 16 * t, 16), 16)
                w_real = weights[0, at, cols].astype(F32)
                w_imag = weights[1, at, cols].astype(F32)
                parts = []
                for part in range(2):
                    rows = [
                        jnp.broadcast_to(lines[at_row : at_row + 1], (share, width))
                        for at_row in (part * share + 2 * t, part * share + 2 * t + 1)
                    ]
                    parts.append(jnp.concatenate(rows, 0))
                real = real + parts[0] * w_real - parts[1] * w_imag
                imag = imag + parts[0] * w_imag + parts[1] * w_real
            return real, imag

        zero = jnp.zeros((16, width), F32)
        real, imag = lax.fori_loop(0, spec.shape[0] // 16, group, (zero, zero))
        modal[:share, cols] = real[:share] + real[share:]
        modal[share:, cols] = imag[:share] + imag[share:]


def exchange_modes(spectrum, tables, weights, buffers, sems, ready):
    turn_ref, to_z, from_z, from_y = tables
    part, held_sum, all_z, all_c, spec, modal, out_z, held_z, all_o = buffers
    groups, quarters = all_z.shape[0], part.shape[0]
    share = 8
    planes = to_z.shape[2] // (2 * share * groups)
    channels = quarters * share
    kept = lax.broadcasted_iota(jnp.int32, (1, WIDE), 1) < KY * MX
    own_kz = to_z.shape[1] // (2 * share)
    g, q = lax.axis_index("gz"), lax.axis_index("gy")
    turn = turn_ref[q]
    cosine, sine = turn[0:1], turn[1:2]
    real, imag = spectrum[:, :WIDE], spectrum[:, WIDE:]
    real, imag = cosine * real + sine * imag, cosine * imag - sine * real
    for quarter in range(quarters):
        rows = []
        for z in range(planes):
            at = z * channels + quarter * share
            rows += [real[at : at + share], imag[at : at + share]]
        part[quarter] = pack(rows).astype(BF16)
    ready["greet"]()
    copies = send(
        "gy", quarters, lambda peer: part.at[peer], lambda me, step: held_sum.at[step], *sems[0]
    )
    total = part[q].astype(F32)
    for step, copy in enumerate(copies, 1):
        copy.wait_recv()
        total = total + held_sum[step].astype(F32)
    all_z[g] = total.astype(BF16)
    more = send("gz", groups, lambda peer: all_z.at[g], lambda me, step: all_z.at[me], *sems[1])
    for copy in more:
        copy.wait_recv()
    copies += more
    ready["to_z"]()
    rows = []
    for group in range(groups):
        rows += unpack(all_z[group].astype(F32))
    rows = jnp.concatenate(rows, 0).astype(BF16)
    bins = jnp.where(kept, jnp.dot(to_z[g], rows, preferred_element_type=F32), 0.0)
    modes = KY * MX
    length = 8 * 128
    zero = jnp.zeros((share, length - WIDE), F32)
    halves = []
    for half in range(2):
        for kz in range(own_kz):
            at = (half * own_kz + kz) * share
            wide = jnp.concatenate([bins[at : at + share], zero], 1)
            if kz == 0:
                line = wide
            else:
                line = line + pltpu.roll(wide, kz * modes, 1)
        halves.append(line)
    all_c[q] = jnp.concatenate(halves, 0)[:, : all_c.shape[-1]].astype(BF16)
    more = send("gy", quarters, lambda peer: all_c.at[q], lambda me, step: all_c.at[me], *sems[2])
    for copy in more:
        copy.wait_recv()
    copies += more
    spec[...] = all_c[...].reshape(spec.shape).astype(F32)
    modal[...] = jnp.zeros_like(modal)
    ready["weights"]()
    weigh_modes(spec, weights, modal)
    line = modal[...]
    rows = []
    for kz in range(own_kz):
        moved = line if kz == 0 else pltpu.roll(line, length - kz * modes, 1)
        rows.append(moved[:, :WIDE])
    rows = jnp.concatenate(rows, 0).astype(BF16)
    ready["from_z"]()
    back = jnp.dot(from_z[g], rows, preferred_element_type=F32)
    back = jnp.where(kept, back, 0.0)
    for group in range(groups):
        first = group * planes * 2 * share
        blocks = [back[first + at * share : first + (at + 1) * share] for at in range(2 * planes)]
        out_z[group] = pack(blocks).astype(BF16)
    more = send(
        "gz", groups, lambda peer: out_z.at[peer], lambda me, step: held_z.at[step], *sems[3]
    )
    total = out_z[g].astype(F32)
    for step, copy in enumerate(more, 1):
        copy.wait_recv()
        total = total + held_z[step].astype(F32)
    copies += more
    all_o[q] = total.astype(BF16)
    more = send("gy", quarters, lambda peer: all_o.at[q], lambda me, step: all_o.at[me], *sems[4])
    for copy in more:
        copy.wait_recv()
    copies += more
    ready["from_y"]()
    real, imag = [], []
    pieces = [unpack(all_o[quarter].astype(F32)) for quarter in range(quarters)]
    for z in range(planes):
        for piece in pieces:
            real.append(piece[2 * z])
            imag.append(piece[2 * z + 1])
    real, imag = jnp.concatenate(real, 0), jnp.concatenate(imag, 0)
    real, imag = cosine * real - sine * imag, sine * real + cosine * imag
    rows = jnp.concatenate([real, imag], 1).astype(BF16)
    result = jnp.dot(rows, from_y[...], preferred_element_type=F32).astype(BF16)
    for copy in copies:
        copy.wait_send()
    return result


def prepare_maps(skip, lift_t, bias, lift, planes):
    channels, hidden = lift_t.shape
    scaled = bias * F32(HALF)
    high = scaled.astype(BF16).astype(F32)
    middle = (scaled - high).astype(BF16).astype(F32)
    low = scaled - high - middle
    tail = jnp.zeros((128 - channels - 3, hidden), F32)
    tall = jnp.concatenate([lift_t.astype(F32), high, middle, low, tail], 0)
    lift[...] = tall.T.astype(BF16)
    blank = jnp.zeros((channels, channels), F32)
    skip = skip.astype(F32)
    block_rows = []
    for z in range(planes):
        block_rows.append(
            jnp.concatenate([skip if z == other else blank for other in range(planes)], 1)
        )
    return jnp.concatenate(block_rows, 0).astype(BF16)


def pointwise(current, rows_y, from_x, skip_all, lift, down):
    rows, length = current.shape
    channels = down.shape[0]
    planes = rows // channels
    ones = (lax.broadcasted_iota(jnp.int32, (16, planes * length), 0) < 3).astype(F32).astype(BF16)
    depth, width = from_x.shape
    halves = []
    for half in range(YB // HJ):
        left = jnp.concatenate([rows_y[:, half * depth : (half + 1) * depth], skip_all], 1)
        right = jnp.concatenate([from_x[...], current[:, half * width : (half + 1) * width]], 0)
        halves.append(jnp.dot(left, right, preferred_element_type=F32))
    mixed = jnp.concatenate(halves, 1)
    lower = (mixed * F32(HALF)).astype(BF16)
    wide = jnp.concatenate([lower[z * channels : (z + 1) * channels] for z in range(planes)], 1)
    wide = jnp.concatenate([wide, ones], 0)
    value = jnp.dot(lift[:, : channels + 16], wide, preferred_element_type=F32)
    value = (value + value * lax.erf(value)).astype(BF16)
    change = jnp.dot(down, value, preferred_element_type=F32) * F32(HALF)
    return [
        (mixed[z * channels : (z + 1) * channels] + change[:, z * length : (z + 1) * length]).astype(BF16)
        for z in range(planes)
    ]


def meet(groups, quarters):
    barrier = pltpu.get_barrier_semaphore()
    for axis, count in (("gz", groups), ("gy", quarters)):
        me = lax.axis_index(axis)
        for step in range(1, count):
            pl.semaphore_signal(
                barrier,
                inc=1,
                device_id={axis: lax.rem(me + step, count)},
                device_id_type=pl.DeviceIdType.MESH,
            )
    return lambda: pl.semaphore_wait(barrier, groups + quarters - 2)


def loads(pairs, sem):
    copies = [
        pltpu.make_async_copy(source, target, sem.at[at])
        for at, (source, target) in enumerate(pairs)
    ]
    for copy in copies:
        copy.start()
    return copies


def modes_kernel(
    sizes, raw_hbm, to_rows_hbm, to_x_hbm, to_y_hbm, weights_hbm, from_y_hbm, from_x_hbm,
    turn_hbm, to_z_hbm, from_z_hbm, skip_hbm, lift_t_hbm, bias_hbm, down_hbm,
    rows_out, field_hbm, raw, to_rows, to_x, to_y, weights, from_y, from_x, turn, to_z, from_z,
    skip, lift_t, bias, down, field, later, lift, rows_y, local_sem, late_sem, out_sem, *rest,
):
    groups, quarters = sizes
    layers = weights_hbm.shape[0]
    greeting = meet(groups, quarters)
    channels, planes, quarter, length_x = raw.shape
    lines = 2 * YB
    pieces = quarter // lines
    copies = loads(
        [(to_rows_hbm, to_rows)]
        + [
            (raw_hbm.at[:, :, pl.ds(at * lines, lines)], raw.at[:, :, pl.ds(at * lines, lines)])
            for at in range(pieces)
        ]
        + [(to_x_hbm, to_x), (to_y_hbm, to_y), (turn_hbm, turn)],
        local_sem,
    )
    copies[0].wait()
    along = []
    for at in range(pieces):
        copies[1 + at].wait()
        if at == 1:
            copies[1 + pieces].wait()
        for z in range(planes):
            block = raw[:, z, at * lines : (at + 1) * lines, :].astype(F32)
            for half in range(2):
                eight = block[:, half * YB : (half + 1) * YB].reshape(channels * YB, length_x)
                turned = jnp.dot(
                    to_rows[...], eight.astype(BF16), preferred_element_type=F32
                ).astype(BF16)
                for j in range(YB):
                    field[
                        at * 2 + half,
                        z * channels : (z + 1) * channels,
                        j * length_x : (j + 1) * length_x,
                    ] = turned[j * channels : (j + 1) * channels]
        if at > 0:
            along += along_x(field, 2 * at - 2, 2, to_x)
    along += along_x(field, 2 * pieces - 2, 2, to_x)
    for copy in copies[2 + pieces :]:
        copy.wait()
    waits = loads(
        [(to_z_hbm, to_z)]
        + [(weights_hbm.at[layer], weights.at[layer]) for layer in range(layers)]
        + [(from_z_hbm, from_z), (from_y_hbm, from_y), (from_x_hbm, from_x)]
        + [(skip_hbm, skip), (lift_t_hbm, lift_t), (bias_hbm, bias), (down_hbm, down)],
        late_sem,
    )
    current = field
    for layer in range(layers):
        if layer > 0:
            if layer == 1:
                for copy in waits[layers + 3 :]:
                    copy.wait()
            skip_all = prepare_maps(
                skip[layer - 1], lift_t[layer - 1], bias[layer - 1 : layer], lift, planes
            )
            source, current = current, (later if layer % 2 else field)
            for b in range(quarter // YB):
                parts = pointwise(
                    source[b], rows_y[:, b * YB * SUB : (b + 1) * YB * SUB], from_x, skip_all,
                    lift, down[layer - 1],
                )
                for z, part in enumerate(parts):
                    current[b, z * channels : (z + 1) * channels, :] = part
            if layer == layers - 1:
                leave = pltpu.make_async_copy(current, field_hbm, out_sem.at[0])
                leave.start()
        if layer > 0:
            along = along_x(current, 0, quarter // YB, to_x)
        spectrum = jnp.dot(jnp.concatenate(along, 1), to_y[...], preferred_element_type=F32)
        buffers = rest[9 * layer : 9 * layer + 9]
        at = 9 * layers + 10 * layer
        sems = [(rest[at + 2 * phase], rest[at + 2 * phase + 1]) for phase in range(5)]
        nothing = lambda: None
        ready = {
            "greet": nothing if layer else greeting,
            "to_z": nothing if layer else waits[0].wait,
            "weights": waits[1 + layer].wait,
            "from_z": nothing if layer else waits[layers + 1].wait,
            "from_y": nothing if layer else waits[layers + 2].wait,
        }
        rows = exchange_modes(
            spectrum, (turn, to_z, from_z, from_y), weights.at[layer], buffers, sems, ready
        )
        if layer == layers - 1:
            rows_out[...] = rows
        else:
            rows_y[...] = rows
    leave.wait()


def last_kernel(
    layer, field_hbm, rows_hbm, from_x_hbm, from_rows_hbm, skip_hbm, lift_t_hbm, bias_hbm,
    down_hbm, out_hbm, rows_y, from_x, from_rows, skip, lift_t, bias, down, field, lift, result,
    in_sem, out_sem,
):
    blocks = field.shape[0]
    channels, planes, _, length_x = result.shape
    lines = 2 * YB
    steps = blocks // 2
    copies = loads(
        [
            (skip_hbm, skip), (lift_t_hbm, lift_t), (bias_hbm, bias), (down_hbm, down),
            (rows_hbm, rows_y), (from_x_hbm, from_x), (from_rows_hbm, from_rows),
        ]
        + [(field_hbm.at[pl.ds(2 * at, 2)], field.at[pl.ds(2 * at, 2)]) for at in range(steps)],
        in_sem,
    )
    for copy in copies[:7]:
        copy.wait()
    copies = copies[7:]
    skip_all = prepare_maps(skip[layer], lift_t[layer], bias[layer : layer + 1], lift, planes)
    outs = []
    for at in range(steps):
        copies[at].wait()
        turned = [[] for _ in range(planes)]
        for b in (2 * at, 2 * at + 1):
            parts = pointwise(
                field[b], rows_y[:, b * YB * SUB : (b + 1) * YB * SUB], from_x, skip_all, lift,
                down[layer],
            )
            for z, part in enumerate(parts):
                tall = jnp.concatenate(
                    [part[:, j * length_x : (j + 1) * length_x] for j in range(YB)], 0
                )
                tall = jnp.dot(from_rows[...], tall, preferred_element_type=F32)
                turned[z].append(tall.reshape(channels, YB, length_x))
        window = pl.ds(at * lines, lines)
        for z in range(planes):
            result[:, z, window, :] = jnp.concatenate(turned[z], 1).astype(BF16)
        copy = pltpu.make_async_copy(
            result.at[:, :, window], out_hbm.at[:, :, window], out_sem.at[at]
        )
        copy.start()
        outs.append(copy)
    for copy in outs:
        copy.wait()


def fast_device(noisy_field, spectral_weights, skip_weights, in_weights, in_bias, out_weights):
    channels, planes, quarter, length_x = noisy_field.shape
    layer_count = spectral_weights.shape[0]
    groups, quarters = lax.axis_size("gz"), lax.axis_size("gy")
    own_kz = KZ // groups
    own_modes = spectral_weights.shape[2]
    share = channels // quarters
    blocks = quarter // YB
    hidden = in_weights.shape[1]
    tables = np_tables(groups, quarters, planes, quarter, length_x, channels)
    tables = {name: jnp.asarray(value) for name, value in tables.items()}
    weights = spectral_weights.transpose(0, 1, 3, 4, 2)
    weights = weights.reshape(layer_count, 2, channels * share, own_modes)
    lift_t = in_weights.transpose(0, 2, 1)
    rows_shape = jax.ShapeDtypeStruct((planes * channels, quarter * SUB), BF16)
    field_shape = jax.ShapeDtypeStruct((blocks, planes * channels, YB * length_x), BF16)
    anywhere = pl.BlockSpec(memory_space=pltpu.HBM)
    vmem = pl.BlockSpec(memory_space=pltpu.VMEM)

    def held(name):
        return pltpu.VMEM(tables[name].shape, tables[name].dtype)

    full = -(-own_modes // 128) * 128
    block = (planes * 2 * share * 2 + share, 128)
    traffic = [
        pltpu.VMEM((quarters,) + block, BF16),
        pltpu.VMEM((quarters,) + block, BF16),
        pltpu.VMEM((groups,) + block, BF16),
        pltpu.VMEM((quarters, 2 * share, full), BF16),
        pltpu.VMEM((quarters * 2 * share, full), F32),
        pltpu.VMEM((2 * share, 8 * 128), F32),
        pltpu.VMEM((groups,) + block, BF16),
        pltpu.VMEM((groups,) + block, BF16),
        pltpu.VMEM((quarters,) + block, BF16),
    ]
    signals = []
    for count in (quarters, groups, quarters, groups, quarters):
        signals += [pltpu.SemaphoreType.DMA((count,))] * 2
    lift_held = pltpu.VMEM((hidden, 128), BF16)
    field_held = pltpu.VMEM(field_shape.shape, BF16)
    raw_held = pltpu.VMEM(noisy_field.shape, BF16)
    maps = (skip_weights, lift_t, in_bias, out_weights)
    maps_held = [pltpu.VMEM(value.shape, value.dtype) for value in maps]
    pieces = quarter // (2 * YB)
    rows, field = pl.pallas_call(
        functools.partial(modes_kernel, (groups, quarters)),
        out_shape=[rows_shape, field_shape],
        in_specs=[anywhere] * 14,
        out_specs=[vmem, anywhere],
        scratch_shapes=[
            raw_held, held("to_rows"), held("to_x"), held("to_y"),
            pltpu.VMEM(weights.shape, BF16), held("from_y"), held("from_x"),
            held("turn"), held("to_z"), held("from_z"), *maps_held, field_held, field_held, lift_held, pltpu.VMEM(rows_shape.shape, BF16),
            pltpu.SemaphoreType.DMA((4 + pieces,)), pltpu.SemaphoreType.DMA((8 + layer_count,)),
            pltpu.SemaphoreType.DMA((1,)),
        ] + traffic * layer_count + signals * layer_count,
        compiler_params=pltpu.CompilerParams(
            collective_id=0, has_side_effects=True, vmem_limit_bytes=VMEM_LIMIT
        ),
        name="modes",
    )(
        noisy_field, tables["to_rows"], tables["to_x"], tables["to_y"], weights, tables["from_y"],
        tables["from_x"], tables["turn"], tables["to_z"], tables["from_z"], *maps,
    )
    return pl.pallas_call(
        functools.partial(last_kernel, layer_count - 1),
        out_shape=jax.ShapeDtypeStruct(noisy_field.shape, BF16),
        in_specs=[anywhere, pl.BlockSpec(memory_space=pl.ANY)] + [anywhere] * 6,
        out_specs=anywhere,
        scratch_shapes=[
            pltpu.VMEM(rows_shape.shape, BF16), held("from_x"), held("from_rows"), *maps_held,
            field_held, lift_held, raw_held, pltpu.SemaphoreType.DMA((7 + pieces,)),
            pltpu.SemaphoreType.DMA((pieces,)),
        ],
        compiler_params=pltpu.CompilerParams(vmem_limit_bytes=VMEM_LIMIT),
        name="last_layer",
    )(field, rows, tables["from_x"], tables["from_rows"], *maps)


def pick(noisy_field, spectral_weights, *rest):
    groups, quarters = lax.axis_size("gz"), lax.axis_size("gy")
    channels, planes, quarter, _ = noisy_field.shape
    fits = (
        KZ % groups == 0
        and spectral_weights.shape[2] == KZ // groups * KY * MX
        and spectral_weights.shape[2] <= 8 * 128 - 128
        and channels == 8 * quarters
        and planes == 2
        and quarter % (2 * YB) == 0
    )
    body = fast_device if fits else per_device
    return body(noisy_field, spectral_weights, *rest)


def solution(mesh):
    in_specs = (P(None, "gz", "gy", None), P(None, None, "gz", None, "gy"), P(), P(), P(), P())
    out_specs = P(None, "gz", "gy", None)
    return jax.shard_map(
        pick, mesh=mesh, in_specs=in_specs, out_specs=out_specs, check_vma=False
    )
```

```python
import functools
import math

import jax
import jax.numpy as jnp
from jax import lax
from jax.experimental import pallas as pl
from jax.experimental.pallas import tpu as pltpu
from jax.sharding import PartitionSpec as P
import ml_dtypes
import numpy as np

MX = 12
KY = 24
KZ = 24
KP = KY // 2
LANES = 128
ROWS = 32
F32 = jnp.float32
BF16 = jnp.bfloat16


def angles(number, positions, length, signed):
    kept = jnp.arange(number, dtype=jnp.int32)
    if signed:
        kept = jnp.where(kept < number // 2, kept, kept - number)
    phases = jnp.mod(kept[:, None] * positions[None, :], length)
    radians = 2.0 * math.pi / length * phases.astype(jnp.float32)
    return (jnp.cos(radians), jnp.sin(radians))


def forward_table(length):
    cosine, sine = angles(MX, jnp.arange(length, dtype=jnp.int32), length, False)
    part = jnp.concatenate([cosine, -sine, -sine, -cosine], 0)
    table = jnp.concatenate([part, part], 0).T.astype(BF16)
    return jnp.pad(table, ((0, 0), (0, LANES - 8 * MX)))


def inverse_table(length):
    cosine, sine = angles(MX, jnp.arange(length, dtype=jnp.int32), length, False)
    factor = jnp.where(jnp.arange(MX) == 0, F32(1.0), F32(2.0))[:, None]
    scale = 1.0 / math.sqrt(2.0 * KZ * KY * MX)
    half = jnp.concatenate([cosine * factor, -sine * factor], 0) * scale
    table = jnp.concatenate([half] * 4, 0).astype(BF16)
    return jnp.pad(table, ((0, LANES - 8 * MX), (0, 0)))


def y_weights(positions, length):
    cosine, sine = angles(KY, positions, length, True)
    both = jnp.stack([cosine, sine], -1).transpose(1, 0, 2)
    lanes = jnp.repeat(both.reshape(positions.shape[0], KP, 4), 2 * MX, axis=2)
    return jnp.pad(lanes, ((0, 0), (0, 0), (0, LANES - 8 * MX)))


def gelu(value):
    return 0.5 * value * (1.0 + lax.erf(value * F32(math.sqrt(0.5))))


def accumulate_modes(along, weight_ref, modes_ref):
    rows, channels = along.shape[0], along.shape[1]

    @pl.when(pl.program_id(1) == 0)
    def _():
        modes_ref[...] = jnp.zeros_like(modes_ref)

    for kp in range(KP):
        total = along[0] * weight_ref[0, kp : kp + 1, :]
        for y in range(1, rows):
            total = total + along[y] * weight_ref[y, kp : kp + 1, :]
        modes_ref[0, kp] += total


def forward_kernel(field_ref, weight_ref, table_ref, modes_ref):
    rows, channels, length = field_ref.shape
    flat = field_ref[...].reshape(rows * channels, length)
    along = jnp.dot(flat, table_ref[...], preferred_element_type=F32)
    accumulate_modes(along.reshape(rows, channels, LANES), weight_ref, modes_ref)


def layer_body(
    field_ref, planes_ref, weight_ref, inverse_ref, skip_ref, lift_ref, bias_ref, down_ref, out_ref
):
    rows, channels, length = field_ref.shape
    parts = []
    for y in range(rows):
        total = planes_ref[0, 0] * weight_ref[y, 0:1, :]
        for kp in range(1, KP):
            total = total + planes_ref[0, kp] * weight_ref[y, kp : kp + 1, :]
        parts.append(total.astype(BF16))
    stacked = jnp.concatenate(parts, 0)
    spatial = jnp.dot(stacked, inverse_ref[...], preferred_element_type=F32)
    wide_spatial = jnp.concatenate(
        [spatial[y * channels : (y + 1) * channels] for y in range(rows)], 1
    )
    wide_field = jnp.concatenate([field_ref[y] for y in range(rows)], 1)
    mixed = wide_spatial + jnp.dot(skip_ref[...], wide_field, preferred_element_type=F32)
    before = jnp.dot(lift_ref[...], mixed.astype(BF16), preferred_element_type=F32)
    hidden = gelu(before + bias_ref[...]).astype(BF16)
    result = mixed + jnp.dot(down_ref[...], hidden, preferred_element_type=F32)
    result = result.astype(BF16)
    for y in range(rows):
        out_ref[y] = result[:, y * length : (y + 1) * length]


def middle_kernel(
    field_ref, planes_ref, weight_ref, inverse_ref, skip_ref, lift_ref, bias_ref, down_ref,
    table_ref, out_ref, modes_ref,
):
    layer_body(
        field_ref, planes_ref, weight_ref, inverse_ref, skip_ref, lift_ref, bias_ref, down_ref,
        out_ref,
    )
    forward_kernel(out_ref, weight_ref, table_ref, modes_ref)


def whole(shape):
    return pl.BlockSpec(shape, lambda z, y: (0,) * len(shape))


def run_forward(field, weights_y, table, planes):
    total, channels, length = field.shape
    steps = total // planes // ROWS
    return pl.pallas_call(
        forward_kernel,
        grid=(planes, steps),
        in_specs=[
            pl.BlockSpec((ROWS, channels, length), lambda z, y: (z * steps + y, 0, 0)),
            pl.BlockSpec((ROWS, KP, LANES), lambda z, y: (y, 0, 0)),
            whole(table.shape),
        ],
        out_specs=pl.BlockSpec((1, KP, channels, LANES), lambda z, y: (z, 0, 0, 0)),
        out_shape=jax.ShapeDtypeStruct((planes, KP, channels, LANES), F32),
        name="forward_modes",
    )(field, weights_y, table)


def run_layer(field, plane_modes, weights_y, inverse, skip, lift, bias, down, table):
    total, channels, length = field.shape
    planes = plane_modes.shape[0]
    steps = total // planes // ROWS
    field_spec = pl.BlockSpec((ROWS, channels, length), lambda z, y: (z * steps + y, 0, 0))
    modes_spec = pl.BlockSpec((1, KP, channels, LANES), lambda z, y: (z, 0, 0, 0))
    field_shape = jax.ShapeDtypeStruct(field.shape, BF16)
    modes_shape = jax.ShapeDtypeStruct(plane_modes.shape, F32)
    args = [field, plane_modes, weights_y, inverse, skip, lift, bias, down]
    specs = [
        field_spec,
        modes_spec,
        pl.BlockSpec((ROWS, KP, LANES), lambda z, y: (y, 0, 0)),
        whole(inverse.shape),
        whole(skip.shape),
        whole(lift.shape),
        whole(bias.shape),
        whole(down.shape),
    ]
    if table is None:
        return pl.pallas_call(
            layer_body,
            grid=(planes, steps),
            in_specs=specs,
            out_specs=field_spec,
            out_shape=field_shape,
            name="last_layer",
        )(*args)
    return pl.pallas_call(
        middle_kernel,
        grid=(planes, steps),
        in_specs=specs + [whole(table.shape)],
        out_specs=[field_spec, modes_spec],
        out_shape=[field_shape, modes_shape],
        name="middle_layer",
    )(*args, table)


def fold_modes(modes, scale):
    planes, _, channels, _ = modes.shape
    split = modes[..., : 8 * MX].reshape(planes, KP, channels, 2, 2, 2, MX)
    folded = (split[:, :, :, :, 0] + split[:, :, :, :, 1]) * scale
    ordered = folded.transpose(0, 4, 2, 1, 3, 5)
    return ordered.reshape(planes * 2, channels, KY * MX)


def unfold_modes(rows, planes):
    channels = rows.shape[1]
    real, imag = (
        rows.astype(F32).reshape(planes, 2, channels, KP, 2, MX)[:, part] for part in range(2)
    )
    lanes = jnp.stack([real, imag, -imag, real], axis=4)
    lanes = lanes.transpose(0, 2, 1, 3, 4, 5).reshape(planes, KP, channels, 8 * MX)
    return jnp.pad(lanes, ((0, 0), (0, 0), (0, 0), (0, LANES - 8 * MX)))


def greet(axes):
    barrier = pltpu.get_barrier_semaphore()
    total = 0
    for axis, count in axes:
        me = lax.axis_index(axis)
        for step in range(1, count):
            pl.semaphore_signal(
                barrier,
                inc=1,
                device_id={axis: lax.rem(me + step, count)},
                device_id_type=pl.DeviceIdType.MESH,
            )
        total += count - 1
    pl.semaphore_wait(barrier, total)


def spread(axis, count, source, held, send_sem, recv_sem):
    me = lax.axis_index(axis)
    copies = []
    for step in range(1, count):
        peer = lax.rem(me + step, count)
        copy = pltpu.make_async_remote_copy(
            src_ref=source(peer),
            dst_ref=held.at[step],
            send_sem=send_sem.at[step],
            recv_sem=recv_sem.at[step],
            device_id={axis: peer},
            device_id_type=pl.DeviceIdType.MESH,
        )
        copy.start()
        copies.append(copy)
    return copies


def collect(axis, count, own, held, copies, out_ref):
    me = lax.axis_index(axis)
    out_ref[me] = own
    for step, copy in enumerate(copies, 1):
        copy.wait_recv()
        out_ref[lax.rem(me - step + count, count)] = held[step]


def z_and_y(groups, quarters, own_ref, matrix_ref, out_ref, held_z, all_z, stage, held_y, sems):
    send_z, recv_z, send_y, recv_y = sems
    first = spread("gz", groups, lambda peer: own_ref, held_z, send_z, recv_z)
    collect("gz", groups, own_ref[...], held_z, first, all_z)
    rows = all_z[...].reshape(-1, all_z.shape[-1]).astype(F32)
    stage[...] = jnp.dot(
        matrix_ref[...], rows, precision=lax.Precision.HIGHEST, preferred_element_type=F32
    ).astype(BF16)
    second = spread("gy", quarters, lambda peer: stage, held_y, send_y, recv_y)
    collect("gy", quarters, stage[...], held_y, second, out_ref)
    return first + second


def sum_kernel(
    groups, quarters, own_ref, matrix_ref, out_ref, held_sum, summed, held_z, all_z, stage, held_y,
    send_sum, recv_sum, *sems,
):
    greet((("gz", groups), ("gy", quarters)))
    copies = spread("gy", quarters, lambda peer: own_ref.at[peer], held_sum, send_sum, recv_sum)
    total = own_ref[lax.axis_index("gy")]
    for step, copy in enumerate(copies, 1):
        copy.wait_recv()
        total = total + held_sum[step]
    summed[...] = total.astype(BF16)
    copies += z_and_y(
        groups, quarters, summed, matrix_ref, out_ref, held_z, all_z, stage, held_y, sems
    )
    for copy in copies:
        copy.wait_send()


def spread_kernel(
    groups, quarters, own_ref, matrix_ref, out_ref, held_z, all_z, stage, held_y, *sems
):
    greet((("gz", groups), ("gy", quarters)))
    copies = z_and_y(
        groups, quarters, own_ref, matrix_ref, out_ref, held_z, all_z, stage, held_y, sems
    )
    for copy in copies:
        copy.wait_send()


def communicate(value, matrix, summing, number):
    groups, quarters = lax.axis_size("gz"), lax.axis_size("gy")
    block = value.shape[-2:]
    result = (matrix.shape[0], block[1])
    vmem = pl.BlockSpec(memory_space=pltpu.VMEM)
    scratch = [
        pltpu.VMEM((groups,) + block, BF16),
        pltpu.VMEM((groups,) + block, BF16),
        pltpu.VMEM(result, BF16),
        pltpu.VMEM((quarters,) + result, BF16),
    ]
    sems = [pltpu.SemaphoreType.DMA((count,)) for count in (groups, groups, quarters, quarters)]
    if summing:
        scratch = [pltpu.VMEM((quarters,) + block, F32), pltpu.VMEM(block, BF16)] + scratch
        sems = [pltpu.SemaphoreType.DMA((quarters,))] * 2 + sems
    return pl.pallas_call(
        functools.partial(sum_kernel if summing else spread_kernel, groups, quarters),
        out_shape=jax.ShapeDtypeStruct((quarters,) + result, BF16),
        in_specs=[vmem, vmem],
        out_specs=vmem,
        scratch_shapes=scratch + sems,
        compiler_params=pltpu.CompilerParams(collective_id=number, has_side_effects=True),
        name="exchange",
    )(value, matrix)


def z_matrix(cosine, sine, inverse):
    sign = -1.0 if inverse else 1.0
    return jnp.stack(
        [jnp.stack([cosine, sign * sine]), jnp.stack([-sign * sine, cosine])]
    )


def weigh(spectrum, coefficients):
    real, imag = spectrum[0], spectrum[1]

    def product(left, right):
        return jnp.einsum("zcq,zqco->zoq", left, right, preferred_element_type=F32)

    modal_real = product(real, coefficients[0]) - product(imag, coefficients[1])
    modal_imag = product(real, coefficients[1]) + product(imag, coefficients[0])
    return jnp.stack([modal_real, modal_imag]).astype(BF16)


def exchange(partial, local_weights, planes, full_z, number):
    highest = lax.Precision.HIGHEST
    channels = partial.shape[1]
    modes = KY * MX
    here_z = lax.axis_index("gz") * planes + jnp.arange(planes, dtype=jnp.int32)
    all_z = jnp.arange(full_z, dtype=jnp.int32)
    own_modes = local_weights.shape[1]
    groups = lax.axis_size("gz")
    if own_modes % modes == 0:
        own_kz = own_modes // modes
        cosine, sine = angles(KZ, all_z, full_z, True)
        first = lax.axis_index("gz") * own_kz
        cosine = lax.dynamic_slice_in_dim(cosine, first, own_kz, 0)
        sine = lax.dynamic_slice_in_dim(sine, first, own_kz, 0)
        forward = z_matrix(cosine, sine, False).transpose(0, 2, 3, 1)
        forward = forward.reshape(2 * own_kz, 2 * full_z)
        quarters = lax.axis_size("gy")
        share = channels // quarters
        split = partial.reshape(planes * 2, quarters, share, modes).transpose(1, 0, 2, 3)
        spectrum = communicate(
            split.reshape(quarters, planes * 2 * share, modes),
            jnp.kron(forward, jnp.eye(share, dtype=F32)),
            True,
            number,
        )
        spectrum = spectrum.reshape(quarters, 2, own_kz, share, modes).transpose(1, 2, 0, 3, 4)
        spectrum = spectrum.reshape(2, own_kz, channels, modes)
        coefficients = local_weights.reshape(2, own_kz, modes, channels, -1)
        modal = weigh(spectrum, coefficients)
        outputs = modal.shape[2]
        cosine, sine = angles(KZ, here_z, full_z, True)
        inverse = z_matrix(cosine, sine, True).reshape(2, 2, groups, own_kz, planes)
        inverse = inverse.transpose(4, 0, 2, 1, 3).reshape(planes * 2, groups * 2 * own_kz)
        rows = communicate(
            modal.reshape(2 * own_kz * outputs, modes),
            jnp.kron(inverse, jnp.eye(outputs, dtype=F32)),
            False,
            number + 1,
        )
        rows = rows.reshape(quarters, planes * 2, outputs, modes).transpose(1, 0, 2, 3)
        return rows.reshape(planes * 2, channels, modes)
    cosine, sine = angles(KZ, here_z, full_z, True)
    forward = z_matrix(cosine, sine, False).transpose(0, 2, 3, 1)
    sums = jnp.einsum(
        "akr,rcq->ackq", forward.reshape(2, KZ, planes * 2), partial, precision=highest
    ).reshape(2, channels, KZ * modes)
    sums = lax.psum_scatter(sums, "gz", scatter_dimension=2, tiled=True)
    spectrum = lax.psum(sums, "gy").astype(BF16)[:, None]
    coefficients = lax.all_gather(local_weights, "gy", axis=3, tiled=True)[:, None]
    modal = weigh(spectrum, coefficients)[:, 0]
    modal = lax.all_gather(modal, "gz", axis=2, tiled=True)
    modal = modal.astype(F32).reshape(2, channels, KZ, modes)
    inverse = z_matrix(cosine, sine, True)
    rows = jnp.einsum("abkz,bckq->zacq", inverse, modal, precision=highest)
    return rows.reshape(planes * 2, channels, modes)


def per_device(noisy_field, spectral_weights, skip_weights, in_weights, in_bias, out_weights):
    channels, planes, quarter, length_x = noisy_field.shape
    layer_count = spectral_weights.shape[0]
    full_y = quarter * lax.axis_size("gy")
    full_z = planes * lax.axis_size("gz")
    y_positions = lax.axis_index("gy") * quarter + jnp.arange(quarter, dtype=jnp.int32)
    weights_y = y_weights(y_positions, full_y)
    table = forward_table(length_x)
    inverse = inverse_table(length_x)
    scale = 1.0 / math.sqrt(length_x * full_y * full_z)
    field = noisy_field.transpose(1, 2, 0, 3).reshape(planes * quarter, channels, length_x)
    modes = run_forward(field, weights_y, table, planes)
    for layer in range(layer_count):
        rows = exchange(
            fold_modes(modes, scale), spectral_weights[layer], planes, full_z, 2 * layer
        )
        last = layer == layer_count - 1
        result = run_layer(
            field,
            unfold_modes(rows, planes),
            weights_y,
            inverse,
            skip_weights[layer],
            in_weights[layer],
            in_bias[layer][:, None],
            out_weights[layer],
            None if last else table,
        )
        if last:
            field = result
        else:
            field, modes = result
    return field.reshape(planes, quarter, channels, length_x).transpose(2, 0, 1, 3)


HALF = math.sqrt(0.5)
WIDE = 384
SUB = 32
YB = 8
HJ = 4
VMEM_LIMIT = 60 * 2**20


def np_angles(number, positions, length, signed):
    kept = np.arange(number)
    if signed:
        kept = np.where(kept < number // 2, kept, kept - number)
    phases = np.mod(kept[:, None] * np.asarray(positions)[None, :], length)
    radians = 2.0 * math.pi / length * phases
    return np.cos(radians), np.sin(radians)


def np_tables(groups, quarters, planes, quarter, length_x, channels):
    full_y, full_z = quarter * quarters, planes * groups
    share = channels // quarters
    own_kz = KZ // groups
    modes = KY * MX
    x_cos, x_sin = np_angles(MX, range(length_x), length_x, False)
    to_x = np.zeros((HJ, length_x, HJ, SUB))
    from_x = np.zeros((HJ, SUB, HJ, length_x))
    factor = np.where(np.arange(MX) == 0, 1.0, 2.0)[:, None] / math.sqrt(2.0 * KZ * KY * MX)
    for j in range(HJ):
        to_x[j, :, j, :MX] = x_cos.T
        to_x[j, :, j, MX : 2 * MX] = -x_sin.T
        from_x[j, :MX, j, :] = x_cos * factor
        from_x[j, MX : 2 * MX, j, :] = -x_sin * factor
    y_cos, y_sin = np_angles(KY, range(quarter), full_y, True)
    to_y = np.zeros((quarter, SUB, 2, WIDE))
    from_y = np.zeros((2, WIDE, quarter, SUB))
    scale = 1.0 / math.sqrt(length_x * full_y * full_z)
    for ky in range(KY):
        for kx in range(MX):
            at = ky * MX + kx
            cosine, sine = y_cos[ky], y_sin[ky]
            to_y[:, kx, 0, at] = cosine * scale
            to_y[:, MX + kx, 0, at] = sine * scale
            to_y[:, kx, 1, at] = -sine * scale
            to_y[:, MX + kx, 1, at] = cosine * scale
            from_y[0, at, :, kx] = cosine
            from_y[1, at, :, kx] = -sine
            from_y[0, at, :, MX + kx] = sine
            from_y[1, at, :, MX + kx] = cosine
    turn_cos, turn_sin = np_angles(KY, np.arange(quarters) * quarter, full_y, True)
    turn = np.zeros((quarters, 2, WIDE))
    turn[:, 0, :modes] = np.repeat(turn_cos.T, MX, axis=1)
    turn[:, 1, :modes] = np.repeat(turn_sin.T, MX, axis=1)
    z_cos, z_sin = np_angles(KZ, range(full_z), full_z, True)
    z_cos = z_cos.reshape(groups, own_kz, groups, planes)
    z_sin = z_sin.reshape(groups, own_kz, groups, planes)
    forward = np.zeros((groups, 2, own_kz, groups, planes, 2))
    forward[:, 0, :, :, :, 0] = z_cos
    forward[:, 0, :, :, :, 1] = z_sin
    forward[:, 1, :, :, :, 0] = -z_sin
    forward[:, 1, :, :, :, 1] = z_cos
    forward = forward.reshape(groups, 2 * own_kz, groups * planes * 2)
    back_cos = z_cos.transpose(0, 2, 3, 1)
    back_sin = z_sin.transpose(0, 2, 3, 1)
    inverse = np.zeros((groups, groups, planes, 2, own_kz, 2))
    inverse[:, :, :, 0, :, 0] = back_cos
    inverse[:, :, :, 0, :, 1] = -back_sin
    inverse[:, :, :, 1, :, 0] = back_sin
    inverse[:, :, :, 1, :, 1] = back_cos
    inverse = inverse.reshape(groups, groups * planes * 2, own_kz * 2)
    eye = np.eye(share)[None]
    to_rows = np.eye(channels * YB).reshape(channels, YB, -1).transpose(1, 0, 2)
    from_rows = np.eye(channels * YB).reshape(YB, channels, -1).transpose(1, 0, 2)

    def low(array):
        return array.astype(np.float32).astype(ml_dtypes.bfloat16)

    return dict(
        to_x=low(to_x.reshape(HJ * length_x, HJ * SUB)),
        from_x=low(from_x.reshape(HJ * SUB, HJ * length_x)),
        to_y=low(to_y.reshape(quarter * SUB, 2 * WIDE)),
        from_y=low(from_y.reshape(2 * WIDE, quarter * SUB)),
        turn=turn.astype(np.float32),
        to_rows=low(to_rows.reshape(channels * YB, channels * YB)),
        from_rows=low(from_rows.reshape(channels * YB, channels * YB)),
        to_z=low(np.kron(forward, eye)),
        from_z=low(np.kron(inverse, eye)),
    )


def pack(blocks):
    tail = blocks[0][:, 256:]
    for at, block in enumerate(blocks[1:], 1):
        tail = tail + pltpu.roll(block[:, 256:], at * 32, 1)
    firsts = [block[:, :128] for block in blocks]
    seconds = [block[:, 128:256] for block in blocks]
    return jnp.concatenate(firsts + seconds + [tail], 0)


def unpack(piece):
    tail = piece[64:72]
    blocks = []
    for at in range(4):
        rest = tail if at == 0 else pltpu.roll(tail, 128 - at * 32, 1)
        blocks.append(
            jnp.concatenate([piece[at * 8 : at * 8 + 8], piece[32 + at * 8 : 40 + at * 8], rest], 1)
        )
    return blocks


def send(axis, count, source, target, send_sem, recv_sem):
    me = lax.axis_index(axis)
    copies = []
    for step in range(1, count):
        peer = lax.rem(me + step, count)
        copy = pltpu.make_async_remote_copy(
            src_ref=source(peer),
            dst_ref=target(me, step),
            send_sem=send_sem.at[step],
            recv_sem=recv_sem.at[step],
            device_id={axis: peer},
            device_id_type=pl.DeviceIdType.MESH,
        )
        copy.start()
        copies.append(copy)
    return copies


def settle(copies, more):
    for copy in copies:
        copy.wait_send()
    return more


def along_x(field, first, count, to_x):
    rows = field.shape[1]
    depth, width = to_x.shape
    parts = []
    for b in range(first, first + count):
        for half in range(YB // HJ):
            parts.append(field[b, :, half * depth : (half + 1) * depth])
    along = jnp.dot(jnp.concatenate(parts, 0), to_x[...], preferred_element_type=F32).astype(BF16)
    return [along[at * rows : (at + 1) * rows] for at in range(len(parts))]


def weigh_modes(spec, weights, modal):
    share = 8
    length = weights.shape[-1]
    for start in range(0, length, 256):
        width = min(256, length - start)
        cols = slice(start, start + width)

        def group(cg, total, cols=cols, width=width):
            real, imag = total
            lines = spec[pl.ds(pl.multiple_of(cg * 16, 16), 16), cols]
            for t in range(share // 2):
                at = pl.ds(pl.multiple_of(cg * share * share + 16 * t, 16), 16)
                w_real = weights[0, at, cols].astype(F32)
                w_imag = weights[1, at, cols].astype(F32)
                parts = []
                for part in range(2):
                    rows = [
                        jnp.broadcast_to(lines[at_row : at_row + 1], (share, width))
                        for at_row in (part * share + 2 * t, part * share + 2 * t + 1)
                    ]
                    parts.append(jnp.concatenate(rows, 0))
                real = real + parts[0] * w_real - parts[1] * w_imag
                imag = imag + parts[0] * w_imag + parts[1] * w_real
            return real, imag

        zero = jnp.zeros((16, width), F32)
        real, imag = lax.fori_loop(0, spec.shape[0] // 16, group, (zero, zero))
        modal[:share, cols] = real[:share] + real[share:]
        modal[share:, cols] = imag[:share] + imag[share:]


def exchange_modes(spectrum, tables, weights, buffers, sems, ready):
    turn_ref, to_z, from_z, from_y = tables
    part, held_sum, all_z, all_c, spec, modal, out_z, held_z, all_o = buffers
    groups, quarters = all_z.shape[0], part.shape[0]
    share = 8
    planes = to_z.shape[2] // (2 * share * groups)
    channels = quarters * share
    kept = lax.broadcasted_iota(jnp.int32, (1, WIDE), 1) < KY * MX
    own_kz = to_z.shape[1] // (2 * share)
    g, q = lax.axis_index("gz"), lax.axis_index("gy")
    turn = turn_ref[q]
    cosine, sine = turn[0:1], turn[1:2]
    real, imag = spectrum[:, :WIDE], spectrum[:, WIDE:]
    real, imag = cosine * real + sine * imag, cosine * imag - sine * real
    for quarter in range(quarters):
        rows = []
        for z in range(planes):
            at = z * channels + quarter * share
            rows += [real[at : at + share], imag[at : at + share]]
        part[quarter] = pack(rows).astype(BF16)
    ready["greet"]()
    copies = send(
        "gy", quarters, lambda peer: part.at[peer], lambda me, step: held_sum.at[step], *sems[0]
    )
    ready["idle"]()
    total = part[q].astype(F32)
    for step, copy in enumerate(copies, 1):
        copy.wait_recv()
        total = total + held_sum[step].astype(F32)
    all_z[g] = total.astype(BF16)
    more = send("gz", groups, lambda peer: all_z.at[g], lambda me, step: all_z.at[me], *sems[1])
    copies = settle(copies, more)
    ready["to_z"]()
    for copy in more:
        copy.wait_recv()
    rows = []
    for group in range(groups):
        rows += unpack(all_z[group].astype(F32))
    rows = jnp.concatenate(rows, 0).astype(BF16)
    bins = jnp.where(kept, jnp.dot(to_z[g], rows, preferred_element_type=F32), 0.0)
    modes = KY * MX
    length = 8 * 128
    zero = jnp.zeros((share, length - WIDE), F32)
    halves = []
    for half in range(2):
        for kz in range(own_kz):
            at = (half * own_kz + kz) * share
            wide = jnp.concatenate([bins[at : at + share], zero], 1)
            if kz == 0:
                line = wide
            else:
                line = line + pltpu.roll(wide, kz * modes, 1)
        halves.append(line)
    all_c[q] = jnp.concatenate(halves, 0)[:, : all_c.shape[-1]].astype(BF16)
    more = send("gy", quarters, lambda peer: all_c.at[q], lambda me, step: all_c.at[me], *sems[2])
    copies = settle(copies, more)
    modal[...] = jnp.zeros_like(modal)
    ready["weights"]()
    for copy in more:
        copy.wait_recv()
    spec[...] = all_c[...].reshape(spec.shape).astype(F32)
    weigh_modes(spec, weights, modal)
    line = modal[...]
    rows = []
    for kz in range(own_kz):
        moved = line if kz == 0 else pltpu.roll(line, length - kz * modes, 1)
        rows.append(moved[:, :WIDE])
    rows = jnp.concatenate(rows, 0).astype(BF16)
    ready["from_z"]()
    back = jnp.dot(from_z[g], rows, preferred_element_type=F32)
    back = jnp.where(kept, back, 0.0)
    for group in range(groups):
        first = group * planes * 2 * share
        blocks = [back[first + at * share : first + (at + 1) * share] for at in range(2 * planes)]
        out_z[group] = pack(blocks).astype(BF16)
    more = send(
        "gz", groups, lambda peer: out_z.at[peer], lambda me, step: held_z.at[step], *sems[3]
    )
    copies = settle(copies, more)
    ready["from_y"]()
    total = out_z[g].astype(F32)
    for step, copy in enumerate(more, 1):
        copy.wait_recv()
        total = total + held_z[step].astype(F32)
    all_o[q] = total.astype(BF16)
    more = send("gy", quarters, lambda peer: all_o.at[q], lambda me, step: all_o.at[me], *sems[4])
    copies = settle(copies, more)
    for copy in more:
        copy.wait_recv()
    real, imag = [], []
    pieces = [unpack(all_o[quarter].astype(F32)) for quarter in range(quarters)]
    for z in range(planes):
        for piece in pieces:
            real.append(piece[2 * z])
            imag.append(piece[2 * z + 1])
    real, imag = jnp.concatenate(real, 0), jnp.concatenate(imag, 0)
    real, imag = cosine * real - sine * imag, sine * real + cosine * imag
    rows = jnp.concatenate([real, imag], 1).astype(BF16)
    result = jnp.dot(rows, from_y[...], preferred_element_type=F32).astype(BF16)
    return result, copies


def prepare_maps(skip, lift_t, bias, lift, planes):
    channels, hidden = lift_t.shape
    scaled = bias * F32(HALF)
    high = scaled.astype(BF16).astype(F32)
    middle = (scaled - high).astype(BF16).astype(F32)
    low = scaled - high - middle
    tail = jnp.zeros((128 - channels - 3, hidden), F32)
    tall = jnp.concatenate([lift_t.astype(F32), high, middle, low, tail], 0)
    lift[...] = tall.T.astype(BF16)
    blank = jnp.zeros((channels, channels), F32)
    skip = skip.astype(F32)
    block_rows = []
    for z in range(planes):
        block_rows.append(
            jnp.concatenate([skip if z == other else blank for other in range(planes)], 1)
        )
    return jnp.concatenate(block_rows, 0).astype(BF16)


def pointwise(current, rows_y, from_x, skip_all, lift, down):
    rows, length = current.shape
    channels = down.shape[0]
    planes = rows // channels
    ones = (lax.broadcasted_iota(jnp.int32, (16, planes * length), 0) < 3).astype(F32).astype(BF16)
    depth, width = from_x.shape
    halves = []
    for half in range(YB // HJ):
        left = jnp.concatenate([rows_y[:, half * depth : (half + 1) * depth], skip_all], 1)
        right = jnp.concatenate([from_x[...], current[:, half * width : (half + 1) * width]], 0)
        halves.append(jnp.dot(left, right, preferred_element_type=F32))
    mixed = jnp.concatenate(halves, 1)
    lower = (mixed * F32(HALF)).astype(BF16)
    wide = jnp.concatenate([lower[z * channels : (z + 1) * channels] for z in range(planes)], 1)
    wide = jnp.concatenate([wide, ones], 0)
    value = jnp.dot(lift[:, : channels + 16], wide, preferred_element_type=F32)
    value = (value + value * lax.erf(value)).astype(BF16)
    change = jnp.dot(down, value, preferred_element_type=F32) * F32(HALF)
    return [
        (mixed[z * channels : (z + 1) * channels] + change[:, z * length : (z + 1) * length]).astype(BF16)
        for z in range(planes)
    ]


def meet(groups, quarters):
    barrier = pltpu.get_barrier_semaphore()
    for axis, count in (("gz", groups), ("gy", quarters)):
        me = lax.axis_index(axis)
        for step in range(1, count):
            pl.semaphore_signal(
                barrier,
                inc=1,
                device_id={axis: lax.rem(me + step, count)},
                device_id_type=pl.DeviceIdType.MESH,
            )
    return lambda: pl.semaphore_wait(barrier, groups + quarters - 2)


def loads(pairs, sem):
    copies = [
        pltpu.make_async_copy(source, target, sem.at[at])
        for at, (source, target) in enumerate(pairs)
    ]
    for copy in copies:
        copy.start()
    return copies


def modes_kernel(
    sizes, raw_hbm, to_rows_hbm, to_x_hbm, to_y_hbm, weights_hbm, from_y_hbm, from_x_hbm,
    turn_hbm, to_z_hbm, from_z_hbm, skip_hbm, lift_t_hbm, bias_hbm, down_hbm,
    rows_out, field_hbm, raw, to_rows, to_x, to_y, weights, from_y, from_x, turn, to_z, from_z,
    skip, lift_t, bias, down, field, later, lift, skip_all, rows_y, local_sem, late_sem, out_sem, *rest,
):
    groups, quarters = sizes
    layers = weights_hbm.shape[0]
    greeting = meet(groups, quarters)
    channels, planes, quarter, length_x = raw.shape
    lines = 2 * YB
    pieces = quarter // lines
    copies = loads(
        [(to_rows_hbm, to_rows)]
        + [
            (raw_hbm.at[:, :, pl.ds(at * lines, lines)], raw.at[:, :, pl.ds(at * lines, lines)])
            for at in range(pieces)
        ]
        + [(to_x_hbm, to_x), (to_y_hbm, to_y), (turn_hbm, turn)],
        local_sem,
    )
    copies[0].wait()
    along = []
    for at in range(pieces):
        copies[1 + at].wait()
        if at == 1:
            copies[1 + pieces].wait()
        for z in range(planes):
            block = raw[:, z, at * lines : (at + 1) * lines, :].astype(F32)
            for half in range(2):
                eight = block[:, half * YB : (half + 1) * YB].reshape(channels * YB, length_x)
                turned = jnp.dot(
                    to_rows[...], eight.astype(BF16), preferred_element_type=F32
                ).astype(BF16)
                for j in range(YB):
                    field[
                        at * 2 + half,
                        z * channels : (z + 1) * channels,
                        j * length_x : (j + 1) * length_x,
                    ] = turned[j * channels : (j + 1) * channels]
        if at > 0:
            along += along_x(field, 2 * at - 2, 2, to_x)
    along += along_x(field, 2 * pieces - 2, 2, to_x)
    for copy in copies[2 + pieces :]:
        copy.wait()
    waits = loads(
        [(to_z_hbm, to_z)]
        + [(weights_hbm.at[layer], weights.at[layer]) for layer in range(layers)]
        + [(from_z_hbm, from_z), (from_y_hbm, from_y), (from_x_hbm, from_x)]
        + [(skip_hbm, skip), (lift_t_hbm, lift_t), (bias_hbm, bias), (down_hbm, down)],
        late_sem,
    )
    current, sent = field, []
    for layer in range(layers):
        if layer > 0:
            along = []
            source, current = current, (later if layer % 2 else field)
            for b in range(quarter // YB):
                parts = pointwise(
                    source[b], rows_y[:, b * YB * SUB : (b + 1) * YB * SUB], from_x, skip_all[...],
                    lift, down[layer - 1],
                )
                for z, part in enumerate(parts):
                    current[b, z * channels : (z + 1) * channels, :] = part
                along += along_x(current, b, 1, to_x)
            if layer == layers - 1:
                leave = pltpu.make_async_copy(current, field_hbm, out_sem.at[0])
                leave.start()
        spectrum = jnp.dot(jnp.concatenate(along, 1), to_y[...], preferred_element_type=F32)
        buffers = rest[9 * layer : 9 * layer + 9]
        at = 9 * layers + 10 * layer
        sems = [(rest[at + 2 * phase], rest[at + 2 * phase + 1]) for phase in range(5)]
        nothing = lambda: None

        def idle(layer=layer, before=sent):
            for copy in before:
                copy.wait_send()
            if layer == 0:
                for copy in waits[layers + 3 :]:
                    copy.wait()
            if layer < layers - 1:
                skip_all[...] = prepare_maps(
                    skip[layer], lift_t[layer], bias[layer : layer + 1], lift, planes
                )

        ready = {
            "greet": nothing if layer else greeting,
            "idle": idle,
            "to_z": nothing if layer else waits[0].wait,
            "weights": waits[1 + layer].wait,
            "from_z": nothing if layer else waits[layers + 1].wait,
            "from_y": nothing if layer else waits[layers + 2].wait,
        }
        rows, sent = exchange_modes(
            spectrum, (turn, to_z, from_z, from_y), weights.at[layer], buffers, sems, ready
        )
        if layer == layers - 1:
            rows_out[...] = rows
        else:
            rows_y[...] = rows
    for copy in sent:
        copy.wait_send()
    leave.wait()


def last_kernel(
    layer, field_hbm, rows_hbm, from_x_hbm, from_rows_hbm, skip_hbm, lift_t_hbm, bias_hbm,
    down_hbm, out_hbm, rows_y, from_x, from_rows, skip, lift_t, bias, down, field, lift, result,
    in_sem, out_sem,
):
    blocks = field.shape[0]
    channels, planes, _, length_x = result.shape
    lines = 2 * YB
    steps = blocks // 2
    copies = loads(
        [
            (skip_hbm, skip), (lift_t_hbm, lift_t), (bias_hbm, bias), (down_hbm, down),
            (rows_hbm, rows_y), (from_x_hbm, from_x), (from_rows_hbm, from_rows),
        ]
        + [(field_hbm.at[pl.ds(2 * at, 2)], field.at[pl.ds(2 * at, 2)]) for at in range(steps)],
        in_sem,
    )
    for copy in copies[:7]:
        copy.wait()
    copies = copies[7:]
    skip_all = prepare_maps(skip[layer], lift_t[layer], bias[layer : layer + 1], lift, planes)
    outs = []
    for at in range(steps):
        copies[at].wait()
        turned = [[] for _ in range(planes)]
        for b in (2 * at, 2 * at + 1):
            parts = pointwise(
                field[b], rows_y[:, b * YB * SUB : (b + 1) * YB * SUB], from_x, skip_all, lift,
                down[layer],
            )
            for z, part in enumerate(parts):
                tall = jnp.concatenate(
                    [part[:, j * length_x : (j + 1) * length_x] for j in range(YB)], 0
                )
                tall = jnp.dot(from_rows[...], tall, preferred_element_type=F32)
                turned[z].append(tall.reshape(channels, YB, length_x))
        window = pl.ds(at * lines, lines)
        for z in range(planes):
            result[:, z, window, :] = jnp.concatenate(turned[z], 1).astype(BF16)
        copy = pltpu.make_async_copy(
            result.at[:, :, window], out_hbm.at[:, :, window], out_sem.at[at]
        )
        copy.start()
        outs.append(copy)
    for copy in outs:
        copy.wait()


def fast_device(noisy_field, spectral_weights, skip_weights, in_weights, in_bias, out_weights):
    channels, planes, quarter, length_x = noisy_field.shape
    layer_count = spectral_weights.shape[0]
    groups, quarters = lax.axis_size("gz"), lax.axis_size("gy")
    own_kz = KZ // groups
    own_modes = spectral_weights.shape[2]
    share = channels // quarters
    blocks = quarter // YB
    hidden = in_weights.shape[1]
    tables = np_tables(groups, quarters, planes, quarter, length_x, channels)
    tables = {name: jnp.asarray(value) for name, value in tables.items()}
    weights = spectral_weights.transpose(0, 1, 3, 4, 2)
    weights = weights.reshape(layer_count, 2, channels * share, own_modes)
    lift_t = in_weights.transpose(0, 2, 1)
    rows_shape = jax.ShapeDtypeStruct((planes * channels, quarter * SUB), BF16)
    field_shape = jax.ShapeDtypeStruct((blocks, planes * channels, YB * length_x), BF16)
    anywhere = pl.BlockSpec(memory_space=pltpu.HBM)
    vmem = pl.BlockSpec(memory_space=pltpu.VMEM)

    def held(name):
        return pltpu.VMEM(tables[name].shape, tables[name].dtype)

    full = -(-own_modes // 128) * 128
    block = (planes * 2 * share * 2 + share, 128)
    traffic = [
        pltpu.VMEM((quarters,) + block, BF16),
        pltpu.VMEM((quarters,) + block, BF16),
        pltpu.VMEM((groups,) + block, BF16),
        pltpu.VMEM((quarters, 2 * share, full), BF16),
        pltpu.VMEM((quarters * 2 * share, full), F32),
        pltpu.VMEM((2 * share, 8 * 128), F32),
        pltpu.VMEM((groups,) + block, BF16),
        pltpu.VMEM((groups,) + block, BF16),
        pltpu.VMEM((quarters,) + block, BF16),
    ]
    signals = []
    for count in (quarters, groups, quarters, groups, quarters):
        signals += [pltpu.SemaphoreType.DMA((count,))] * 2
    lift_held = pltpu.VMEM((hidden, 128), BF16)
    field_held = pltpu.VMEM(field_shape.shape, BF16)
    raw_held = pltpu.VMEM(noisy_field.shape, BF16)
    maps = (skip_weights, lift_t, in_bias, out_weights)
    maps_held = [pltpu.VMEM(value.shape, value.dtype) for value in maps]
    pieces = quarter // (2 * YB)
    rows, field = pl.pallas_call(
        functools.partial(modes_kernel, (groups, quarters)),
        out_shape=[rows_shape, field_shape],
        in_specs=[anywhere] * 14,
        out_specs=[vmem, anywhere],
        scratch_shapes=[
            raw_held, held("to_rows"), held("to_x"), held("to_y"),
            pltpu.VMEM(weights.shape, BF16), held("from_y"), held("from_x"),
            held("turn"), held("to_z"), held("from_z"), *maps_held, field_held, field_held, lift_held,
            pltpu.VMEM((planes * channels, planes * channels), BF16), pltpu.VMEM(rows_shape.shape, BF16),
            pltpu.SemaphoreType.DMA((4 + pieces,)), pltpu.SemaphoreType.DMA((8 + layer_count,)),
            pltpu.SemaphoreType.DMA((1,)),
        ] + traffic * layer_count + signals * layer_count,
        compiler_params=pltpu.CompilerParams(
            collective_id=0, has_side_effects=True, vmem_limit_bytes=VMEM_LIMIT
        ),
        name="modes",
    )(
        noisy_field, tables["to_rows"], tables["to_x"], tables["to_y"], weights, tables["from_y"],
        tables["from_x"], tables["turn"], tables["to_z"], tables["from_z"], *maps,
    )
    return pl.pallas_call(
        functools.partial(last_kernel, layer_count - 1),
        out_shape=jax.ShapeDtypeStruct(noisy_field.shape, BF16),
        in_specs=[anywhere, pl.BlockSpec(memory_space=pl.ANY)] + [anywhere] * 6,
        out_specs=anywhere,
        scratch_shapes=[
            pltpu.VMEM(rows_shape.shape, BF16), held("from_x"), held("from_rows"), *maps_held,
            field_held, lift_held, raw_held, pltpu.SemaphoreType.DMA((7 + pieces,)),
            pltpu.SemaphoreType.DMA((pieces,)),
        ],
        compiler_params=pltpu.CompilerParams(vmem_limit_bytes=VMEM_LIMIT),
        name="last_layer",
    )(field, rows, tables["from_x"], tables["from_rows"], *maps)


def pick(noisy_field, spectral_weights, *rest):
    groups, quarters = lax.axis_size("gz"), lax.axis_size("gy")
    channels, planes, quarter, _ = noisy_field.shape
    fits = (
        KZ % groups == 0
        and spectral_weights.shape[2] == KZ // groups * KY * MX
        and spectral_weights.shape[2] <= 8 * 128 - 128
        and channels == 8 * quarters
        and planes == 2
        and quarter % (2 * YB) == 0
    )
    body = fast_device if fits else per_device
    return body(noisy_field, spectral_weights, *rest)


def solution(mesh):
    in_specs = (P(None, "gz", "gy", None), P(None, None, "gz", None, "gy"), P(), P(), P(), P())
    out_specs = P(None, "gz", "gy", None)
    return jax.shard_map(
        pick, mesh=mesh, in_specs=in_specs, out_specs=out_specs, check_vma=False
    )
```

```python
import functools
import math

import jax
import jax.numpy as jnp
from jax import lax
from jax.experimental import pallas as pl
from jax.experimental.pallas import tpu as pltpu
from jax.sharding import PartitionSpec as P
import ml_dtypes
import numpy as np

MX = 12
KY = 24
KZ = 24
KP = KY // 2
LANES = 128
ROWS = 32
F32 = jnp.float32
BF16 = jnp.bfloat16


def angles(number, positions, length, signed):
    kept = jnp.arange(number, dtype=jnp.int32)
    if signed:
        kept = jnp.where(kept < number // 2, kept, kept - number)
    phases = jnp.mod(kept[:, None] * positions[None, :], length)
    radians = 2.0 * math.pi / length * phases.astype(jnp.float32)
    return (jnp.cos(radians), jnp.sin(radians))


def forward_table(length):
    cosine, sine = angles(MX, jnp.arange(length, dtype=jnp.int32), length, False)
    part = jnp.concatenate([cosine, -sine, -sine, -cosine], 0)
    table = jnp.concatenate([part, part], 0).T.astype(BF16)
    return jnp.pad(table, ((0, 0), (0, LANES - 8 * MX)))


def inverse_table(length):
    cosine, sine = angles(MX, jnp.arange(length, dtype=jnp.int32), length, False)
    factor = jnp.where(jnp.arange(MX) == 0, F32(1.0), F32(2.0))[:, None]
    scale = 1.0 / math.sqrt(2.0 * KZ * KY * MX)
    half = jnp.concatenate([cosine * factor, -sine * factor], 0) * scale
    table = jnp.concatenate([half] * 4, 0).astype(BF16)
    return jnp.pad(table, ((0, LANES - 8 * MX), (0, 0)))


def y_weights(positions, length):
    cosine, sine = angles(KY, positions, length, True)
    both = jnp.stack([cosine, sine], -1).transpose(1, 0, 2)
    lanes = jnp.repeat(both.reshape(positions.shape[0], KP, 4), 2 * MX, axis=2)
    return jnp.pad(lanes, ((0, 0), (0, 0), (0, LANES - 8 * MX)))


def gelu(value):
    return 0.5 * value * (1.0 + lax.erf(value * F32(math.sqrt(0.5))))


def accumulate_modes(along, weight_ref, modes_ref):
    rows, channels = along.shape[0], along.shape[1]

    @pl.when(pl.program_id(1) == 0)
    def _():
        modes_ref[...] = jnp.zeros_like(modes_ref)

    for kp in range(KP):
        total = along[0] * weight_ref[0, kp : kp + 1, :]
        for y in range(1, rows):
            total = total + along[y] * weight_ref[y, kp : kp + 1, :]
        modes_ref[0, kp] += total


def forward_kernel(field_ref, weight_ref, table_ref, modes_ref):
    rows, channels, length = field_ref.shape
    flat = field_ref[...].reshape(rows * channels, length)
    along = jnp.dot(flat, table_ref[...], preferred_element_type=F32)
    accumulate_modes(along.reshape(rows, channels, LANES), weight_ref, modes_ref)


def layer_body(
    field_ref, planes_ref, weight_ref, inverse_ref, skip_ref, lift_ref, bias_ref, down_ref, out_ref
):
    rows, channels, length = field_ref.shape
    parts = []
    for y in range(rows):
        total = planes_ref[0, 0] * weight_ref[y, 0:1, :]
        for kp in range(1, KP):
            total = total + planes_ref[0, kp] * weight_ref[y, kp : kp + 1, :]
        parts.append(total.astype(BF16))
    stacked = jnp.concatenate(parts, 0)
    spatial = jnp.dot(stacked, inverse_ref[...], preferred_element_type=F32)
    wide_spatial = jnp.concatenate(
        [spatial[y * channels : (y + 1) * channels] for y in range(rows)], 1
    )
    wide_field = jnp.concatenate([field_ref[y] for y in range(rows)], 1)
    mixed = wide_spatial + jnp.dot(skip_ref[...], wide_field, preferred_element_type=F32)
    before = jnp.dot(lift_ref[...], mixed.astype(BF16), preferred_element_type=F32)
    hidden = gelu(before + bias_ref[...]).astype(BF16)
    result = mixed + jnp.dot(down_ref[...], hidden, preferred_element_type=F32)
    result = result.astype(BF16)
    for y in range(rows):
        out_ref[y] = result[:, y * length : (y + 1) * length]


def middle_kernel(
    field_ref, planes_ref, weight_ref, inverse_ref, skip_ref, lift_ref, bias_ref, down_ref,
    table_ref, out_ref, modes_ref,
):
    layer_body(
        field_ref, planes_ref, weight_ref, inverse_ref, skip_ref, lift_ref, bias_ref, down_ref,
        out_ref,
    )
    forward_kernel(out_ref, weight_ref, table_ref, modes_ref)


def whole(shape):
    return pl.BlockSpec(shape, lambda z, y: (0,) * len(shape))


def run_forward(field, weights_y, table, planes):
    total, channels, length = field.shape
    steps = total // planes // ROWS
    return pl.pallas_call(
        forward_kernel,
        grid=(planes, steps),
        in_specs=[
            pl.BlockSpec((ROWS, channels, length), lambda z, y: (z * steps + y, 0, 0)),
            pl.BlockSpec((ROWS, KP, LANES), lambda z, y: (y, 0, 0)),
            whole(table.shape),
        ],
        out_specs=pl.BlockSpec((1, KP, channels, LANES), lambda z, y: (z, 0, 0, 0)),
        out_shape=jax.ShapeDtypeStruct((planes, KP, channels, LANES), F32),
        name="forward_modes",
    )(field, weights_y, table)


def run_layer(field, plane_modes, weights_y, inverse, skip, lift, bias, down, table):
    total, channels, length = field.shape
    planes = plane_modes.shape[0]
    steps = total // planes // ROWS
    field_spec = pl.BlockSpec((ROWS, channels, length), lambda z, y: (z * steps + y, 0, 0))
    modes_spec = pl.BlockSpec((1, KP, channels, LANES), lambda z, y: (z, 0, 0, 0))
    field_shape = jax.ShapeDtypeStruct(field.shape, BF16)
    modes_shape = jax.ShapeDtypeStruct(plane_modes.shape, F32)
    args = [field, plane_modes, weights_y, inverse, skip, lift, bias, down]
    specs = [
        field_spec,
        modes_spec,
        pl.BlockSpec((ROWS, KP, LANES), lambda z, y: (y, 0, 0)),
        whole(inverse.shape),
        whole(skip.shape),
        whole(lift.shape),
        whole(bias.shape),
        whole(down.shape),
    ]
    if table is None:
        return pl.pallas_call(
            layer_body,
            grid=(planes, steps),
            in_specs=specs,
            out_specs=field_spec,
            out_shape=field_shape,
            name="last_layer",
        )(*args)
    return pl.pallas_call(
        middle_kernel,
        grid=(planes, steps),
        in_specs=specs + [whole(table.shape)],
        out_specs=[field_spec, modes_spec],
        out_shape=[field_shape, modes_shape],
        name="middle_layer",
    )(*args, table)


def fold_modes(modes, scale):
    planes, _, channels, _ = modes.shape
    split = modes[..., : 8 * MX].reshape(planes, KP, channels, 2, 2, 2, MX)
    folded = (split[:, :, :, :, 0] + split[:, :, :, :, 1]) * scale
    ordered = folded.transpose(0, 4, 2, 1, 3, 5)
    return ordered.reshape(planes * 2, channels, KY * MX)


def unfold_modes(rows, planes):
    channels = rows.shape[1]
    real, imag = (
        rows.astype(F32).reshape(planes, 2, channels, KP, 2, MX)[:, part] for part in range(2)
    )
    lanes = jnp.stack([real, imag, -imag, real], axis=4)
    lanes = lanes.transpose(0, 2, 1, 3, 4, 5).reshape(planes, KP, channels, 8 * MX)
    return jnp.pad(lanes, ((0, 0), (0, 0), (0, 0), (0, LANES - 8 * MX)))


def greet(axes):
    barrier = pltpu.get_barrier_semaphore()
    total = 0
    for axis, count in axes:
        me = lax.axis_index(axis)
        for step in range(1, count):
            pl.semaphore_signal(
                barrier,
                inc=1,
                device_id={axis: lax.rem(me + step, count)},
                device_id_type=pl.DeviceIdType.MESH,
            )
        total += count - 1
    pl.semaphore_wait(barrier, total)


def spread(axis, count, source, held, send_sem, recv_sem):
    me = lax.axis_index(axis)
    copies = []
    for step in range(1, count):
        peer = lax.rem(me + step, count)
        copy = pltpu.make_async_remote_copy(
            src_ref=source(peer),
            dst_ref=held.at[step],
            send_sem=send_sem.at[step],
            recv_sem=recv_sem.at[step],
            device_id={axis: peer},
            device_id_type=pl.DeviceIdType.MESH,
        )
        copy.start()
        copies.append(copy)
    return copies


def collect(axis, count, own, held, copies, out_ref):
    me = lax.axis_index(axis)
    out_ref[me] = own
    for step, copy in enumerate(copies, 1):
        copy.wait_recv()
        out_ref[lax.rem(me - step + count, count)] = held[step]


def z_and_y(groups, quarters, own_ref, matrix_ref, out_ref, held_z, all_z, stage, held_y, sems):
    send_z, recv_z, send_y, recv_y = sems
    first = spread("gz", groups, lambda peer: own_ref, held_z, send_z, recv_z)
    collect("gz", groups, own_ref[...], held_z, first, all_z)
    rows = all_z[...].reshape(-1, all_z.shape[-1]).astype(F32)
    stage[...] = jnp.dot(
        matrix_ref[...], rows, precision=lax.Precision.HIGHEST, preferred_element_type=F32
    ).astype(BF16)
    second = spread("gy", quarters, lambda peer: stage, held_y, send_y, recv_y)
    collect("gy", quarters, stage[...], held_y, second, out_ref)
    return first + second


def sum_kernel(
    groups, quarters, own_ref, matrix_ref, out_ref, held_sum, summed, held_z, all_z, stage, held_y,
    send_sum, recv_sum, *sems,
):
    greet((("gz", groups), ("gy", quarters)))
    copies = spread("gy", quarters, lambda peer: own_ref.at[peer], held_sum, send_sum, recv_sum)
    total = own_ref[lax.axis_index("gy")]
    for step, copy in enumerate(copies, 1):
        copy.wait_recv()
        total = total + held_sum[step]
    summed[...] = total.astype(BF16)
    copies += z_and_y(
        groups, quarters, summed, matrix_ref, out_ref, held_z, all_z, stage, held_y, sems
    )
    for copy in copies:
        copy.wait_send()


def spread_kernel(
    groups, quarters, own_ref, matrix_ref, out_ref, held_z, all_z, stage, held_y, *sems
):
    greet((("gz", groups), ("gy", quarters)))
    copies = z_and_y(
        groups, quarters, own_ref, matrix_ref, out_ref, held_z, all_z, stage, held_y, sems
    )
    for copy in copies:
        copy.wait_send()


def communicate(value, matrix, summing, number):
    groups, quarters = lax.axis_size("gz"), lax.axis_size("gy")
    block = value.shape[-2:]
    result = (matrix.shape[0], block[1])
    vmem = pl.BlockSpec(memory_space=pltpu.VMEM)
    scratch = [
        pltpu.VMEM((groups,) + block, BF16),
        pltpu.VMEM((groups,) + block, BF16),
        pltpu.VMEM(result, BF16),
        pltpu.VMEM((quarters,) + result, BF16),
    ]
    sems = [pltpu.SemaphoreType.DMA((count,)) for count in (groups, groups, quarters, quarters)]
    if summing:
        scratch = [pltpu.VMEM((quarters,) + block, F32), pltpu.VMEM(block, BF16)] + scratch
        sems = [pltpu.SemaphoreType.DMA((quarters,))] * 2 + sems
    return pl.pallas_call(
        functools.partial(sum_kernel if summing else spread_kernel, groups, quarters),
        out_shape=jax.ShapeDtypeStruct((quarters,) + result, BF16),
        in_specs=[vmem, vmem],
        out_specs=vmem,
        scratch_shapes=scratch + sems,
        compiler_params=pltpu.CompilerParams(collective_id=number, has_side_effects=True),
        name="exchange",
    )(value, matrix)


def z_matrix(cosine, sine, inverse):
    sign = -1.0 if inverse else 1.0
    return jnp.stack(
        [jnp.stack([cosine, sign * sine]), jnp.stack([-sign * sine, cosine])]
    )


def weigh(spectrum, coefficients):
    real, imag = spectrum[0], spectrum[1]

    def product(left, right):
        return jnp.einsum("zcq,zqco->zoq", left, right, preferred_element_type=F32)

    modal_real = product(real, coefficients[0]) - product(imag, coefficients[1])
    modal_imag = product(real, coefficients[1]) + product(imag, coefficients[0])
    return jnp.stack([modal_real, modal_imag]).astype(BF16)


def exchange(partial, local_weights, planes, full_z, number):
    highest = lax.Precision.HIGHEST
    channels = partial.shape[1]
    modes = KY * MX
    here_z = lax.axis_index("gz") * planes + jnp.arange(planes, dtype=jnp.int32)
    all_z = jnp.arange(full_z, dtype=jnp.int32)
    own_modes = local_weights.shape[1]
    groups = lax.axis_size("gz")
    if own_modes % modes == 0:
        own_kz = own_modes // modes
        cosine, sine = angles(KZ, all_z, full_z, True)
        first = lax.axis_index("gz") * own_kz
        cosine = lax.dynamic_slice_in_dim(cosine, first, own_kz, 0)
        sine = lax.dynamic_slice_in_dim(sine, first, own_kz, 0)
        forward = z_matrix(cosine, sine, False).transpose(0, 2, 3, 1)
        forward = forward.reshape(2 * own_kz, 2 * full_z)
        quarters = lax.axis_size("gy")
        share = channels // quarters
        split = partial.reshape(planes * 2, quarters, share, modes).transpose(1, 0, 2, 3)
        spectrum = communicate(
            split.reshape(quarters, planes * 2 * share, modes),
            jnp.kron(forward, jnp.eye(share, dtype=F32)),
            True,
            number,
        )
        spectrum = spectrum.reshape(quarters, 2, own_kz, share, modes).transpose(1, 2, 0, 3, 4)
        spectrum = spectrum.reshape(2, own_kz, channels, modes)
        coefficients = local_weights.reshape(2, own_kz, modes, channels, -1)
        modal = weigh(spectrum, coefficients)
        outputs = modal.shape[2]
        cosine, sine = angles(KZ, here_z, full_z, True)
        inverse = z_matrix(cosine, sine, True).reshape(2, 2, groups, own_kz, planes)
        inverse = inverse.transpose(4, 0, 2, 1, 3).reshape(planes * 2, groups * 2 * own_kz)
        rows = communicate(
            modal.reshape(2 * own_kz * outputs, modes),
            jnp.kron(inverse, jnp.eye(outputs, dtype=F32)),
            False,
            number + 1,
        )
        rows = rows.reshape(quarters, planes * 2, outputs, modes).transpose(1, 0, 2, 3)
        return rows.reshape(planes * 2, channels, modes)
    cosine, sine = angles(KZ, here_z, full_z, True)
    forward = z_matrix(cosine, sine, False).transpose(0, 2, 3, 1)
    sums = jnp.einsum(
        "akr,rcq->ackq", forward.reshape(2, KZ, planes * 2), partial, precision=highest
    ).reshape(2, channels, KZ * modes)
    sums = lax.psum_scatter(sums, "gz", scatter_dimension=2, tiled=True)
    spectrum = lax.psum(sums, "gy").astype(BF16)[:, None]
    coefficients = lax.all_gather(local_weights, "gy", axis=3, tiled=True)[:, None]
    modal = weigh(spectrum, coefficients)[:, 0]
    modal = lax.all_gather(modal, "gz", axis=2, tiled=True)
    modal = modal.astype(F32).reshape(2, channels, KZ, modes)
    inverse = z_matrix(cosine, sine, True)
    rows = jnp.einsum("abkz,bckq->zacq", inverse, modal, precision=highest)
    return rows.reshape(planes * 2, channels, modes)


def per_device(noisy_field, spectral_weights, skip_weights, in_weights, in_bias, out_weights):
    channels, planes, quarter, length_x = noisy_field.shape
    layer_count = spectral_weights.shape[0]
    full_y = quarter * lax.axis_size("gy")
    full_z = planes * lax.axis_size("gz")
    y_positions = lax.axis_index("gy") * quarter + jnp.arange(quarter, dtype=jnp.int32)
    weights_y = y_weights(y_positions, full_y)
    table = forward_table(length_x)
    inverse = inverse_table(length_x)
    scale = 1.0 / math.sqrt(length_x * full_y * full_z)
    field = noisy_field.transpose(1, 2, 0, 3).reshape(planes * quarter, channels, length_x)
    modes = run_forward(field, weights_y, table, planes)
    for layer in range(layer_count):
        rows = exchange(
            fold_modes(modes, scale), spectral_weights[layer], planes, full_z, 2 * layer
        )
        last = layer == layer_count - 1
        result = run_layer(
            field,
            unfold_modes(rows, planes),
            weights_y,
            inverse,
            skip_weights[layer],
            in_weights[layer],
            in_bias[layer][:, None],
            out_weights[layer],
            None if last else table,
        )
        if last:
            field = result
        else:
            field, modes = result
    return field.reshape(planes, quarter, channels, length_x).transpose(2, 0, 1, 3)


HALF = math.sqrt(0.5)
WIDE = 384
SUB = 32
YB = 8
HJ = 4
VMEM_LIMIT = 60 * 2**20


def np_angles(number, positions, length, signed):
    kept = np.arange(number)
    if signed:
        kept = np.where(kept < number // 2, kept, kept - number)
    phases = np.mod(kept[:, None] * np.asarray(positions)[None, :], length)
    radians = 2.0 * math.pi / length * phases
    return np.cos(radians), np.sin(radians)


def np_tables(groups, quarters, planes, quarter, length_x, channels):
    full_y, full_z = quarter * quarters, planes * groups
    share = channels // quarters
    own_kz = KZ // groups
    modes = KY * MX
    x_cos, x_sin = np_angles(MX, range(length_x), length_x, False)
    to_x = np.zeros((HJ, length_x, HJ, SUB))
    from_x = np.zeros((HJ, SUB, HJ, length_x))
    factor = np.where(np.arange(MX) == 0, 1.0, 2.0)[:, None] / math.sqrt(2.0 * KZ * KY * MX)
    for j in range(HJ):
        to_x[j, :, j, :MX] = x_cos.T
        to_x[j, :, j, MX : 2 * MX] = -x_sin.T
        from_x[j, :MX, j, :] = x_cos * factor
        from_x[j, MX : 2 * MX, j, :] = -x_sin * factor
    y_cos, y_sin = np_angles(KY, range(quarter), full_y, True)
    to_y = np.zeros((quarter, SUB, 2, WIDE))
    from_y = np.zeros((2, WIDE, quarter, SUB))
    scale = 1.0 / math.sqrt(length_x * full_y * full_z)
    for ky in range(KY):
        for kx in range(MX):
            at = ky * MX + kx
            cosine, sine = y_cos[ky], y_sin[ky]
            to_y[:, kx, 0, at] = cosine * scale
            to_y[:, MX + kx, 0, at] = sine * scale
            to_y[:, kx, 1, at] = -sine * scale
            to_y[:, MX + kx, 1, at] = cosine * scale
            from_y[0, at, :, kx] = cosine
            from_y[1, at, :, kx] = -sine
            from_y[0, at, :, MX + kx] = sine
            from_y[1, at, :, MX + kx] = cosine
    turn_cos, turn_sin = np_angles(KY, np.arange(quarters) * quarter, full_y, True)
    turn = np.zeros((quarters, 2, WIDE))
    turn[:, 0, :modes] = np.repeat(turn_cos.T, MX, axis=1)
    turn[:, 1, :modes] = np.repeat(turn_sin.T, MX, axis=1)
    z_cos, z_sin = np_angles(KZ, range(full_z), full_z, True)
    z_cos = z_cos.reshape(groups, own_kz, groups, planes)
    z_sin = z_sin.reshape(groups, own_kz, groups, planes)
    forward = np.zeros((groups, 2, own_kz, groups, planes, 2))
    forward[:, 0, :, :, :, 0] = z_cos
    forward[:, 0, :, :, :, 1] = z_sin
    forward[:, 1, :, :, :, 0] = -z_sin
    forward[:, 1, :, :, :, 1] = z_cos
    forward = forward.reshape(groups, 2 * own_kz, groups * planes * 2)
    back_cos = z_cos.transpose(0, 2, 3, 1)
    back_sin = z_sin.transpose(0, 2, 3, 1)
    inverse = np.zeros((groups, groups, planes, 2, own_kz, 2))
    inverse[:, :, :, 0, :, 0] = back_cos
    inverse[:, :, :, 0, :, 1] = -back_sin
    inverse[:, :, :, 1, :, 0] = back_sin
    inverse[:, :, :, 1, :, 1] = back_cos
    inverse = inverse.reshape(groups, groups * planes * 2, own_kz * 2)
    eye = np.eye(share)[None]
    to_rows = np.eye(channels * YB).reshape(channels, YB, -1).transpose(1, 0, 2)
    from_rows = np.eye(channels * YB).reshape(YB, channels, -1).transpose(1, 0, 2)

    def low(array):
        return array.astype(np.float32).astype(ml_dtypes.bfloat16)

    return dict(
        to_x=low(to_x.reshape(HJ * length_x, HJ * SUB)),
        from_x=low(from_x.reshape(HJ * SUB, HJ * length_x)),
        to_y=low(to_y.reshape(quarter * SUB, 2 * WIDE)),
        from_y=low(from_y.reshape(2 * WIDE, quarter * SUB)),
        turn=turn.astype(np.float32),
        to_rows=low(to_rows.reshape(channels * YB, channels * YB)),
        from_rows=low(from_rows.reshape(channels * YB, channels * YB)),
        to_z=low(np.kron(forward, eye)),
        from_z=low(np.kron(inverse, eye)),
    )


def pack(blocks):
    tail = blocks[0][:, 256:]
    for at, block in enumerate(blocks[1:], 1):
        tail = tail + pltpu.roll(block[:, 256:], at * 32, 1)
    firsts = [block[:, :128] for block in blocks]
    seconds = [block[:, 128:256] for block in blocks]
    return jnp.concatenate(firsts + seconds + [tail], 0)


def unpack(piece):
    tail = piece[64:72]
    blocks = []
    for at in range(4):
        rest = tail if at == 0 else pltpu.roll(tail, 128 - at * 32, 1)
        blocks.append(
            jnp.concatenate([piece[at * 8 : at * 8 + 8], piece[32 + at * 8 : 40 + at * 8], rest], 1)
        )
    return blocks


def send(axis, count, source, target, send_sem, recv_sem):
    me = lax.axis_index(axis)
    copies = []
    for step in range(1, count):
        peer = lax.rem(me + step, count)
        copy = pltpu.make_async_remote_copy(
            src_ref=source(peer),
            dst_ref=target(me, step),
            send_sem=send_sem.at[step],
            recv_sem=recv_sem.at[step],
            device_id={axis: peer},
            device_id_type=pl.DeviceIdType.MESH,
        )
        copy.start()
        copies.append(copy)
    return copies


def settle(copies, more):
    for copy in copies:
        copy.wait_send()
    return more


def along_x(field, first, count, to_x):
    rows = field.shape[1]
    depth, width = to_x.shape
    parts = []
    for b in range(first, first + count):
        for half in range(YB // HJ):
            parts.append(field[b, :, half * depth : (half + 1) * depth])
    along = jnp.dot(jnp.concatenate(parts, 0), to_x[...], preferred_element_type=F32).astype(BF16)
    return [along[at * rows : (at + 1) * rows] for at in range(len(parts))]


def weigh_modes(spec, weights, modal):
    share = 8
    length = weights.shape[-1]
    for start in range(0, length, 256):
        width = min(256, length - start)
        cols = slice(start, start + width)

        def group(cg, total, cols=cols, width=width):
            real, imag = total
            lines = spec[pl.ds(pl.multiple_of(cg * 16, 16), 16), cols]
            for t in range(share // 2):
                at = pl.ds(pl.multiple_of(cg * share * share + 16 * t, 16), 16)
                w_real = weights[0, at, cols].astype(F32)
                w_imag = weights[1, at, cols].astype(F32)
                parts = []
                for part in range(2):
                    rows = [
                        jnp.broadcast_to(lines[at_row : at_row + 1], (share, width))
                        for at_row in (part * share + 2 * t, part * share + 2 * t + 1)
                    ]
                    parts.append(jnp.concatenate(rows, 0))
                real = real + parts[0] * w_real - parts[1] * w_imag
                imag = imag + parts[0] * w_imag + parts[1] * w_real
            return real, imag

        zero = jnp.zeros((16, width), F32)
        real, imag = lax.fori_loop(0, spec.shape[0] // 16, group, (zero, zero))
        modal[:share, cols] = real[:share] + real[share:]
        modal[share:, cols] = imag[:share] + imag[share:]


def exchange_modes(spectrum, tables, weights, buffers, sems, ready):
    turn_ref, to_z, from_z, from_y = tables
    part, held_sum, all_z, all_c, spec, modal, out_z, held_z, all_o = buffers
    groups, quarters = all_z.shape[0], part.shape[0]
    share = 8
    planes = to_z.shape[2] // (2 * share * groups)
    channels = quarters * share
    kept = lax.broadcasted_iota(jnp.int32, (1, WIDE), 1) < KY * MX
    own_kz = to_z.shape[1] // (2 * share)
    g, q = lax.axis_index("gz"), lax.axis_index("gy")
    turn = turn_ref[q]
    cosine, sine = turn[0:1], turn[1:2]
    real, imag = spectrum[:, :WIDE], spectrum[:, WIDE:]
    real, imag = cosine * real + sine * imag, cosine * imag - sine * real
    for quarter in range(quarters):
        rows = []
        for z in range(planes):
            at = z * channels + quarter * share
            rows += [real[at : at + share], imag[at : at + share]]
        part[quarter] = pack(rows).astype(BF16)
    ready["greet"]()
    copies = send(
        "gy", quarters, lambda peer: part.at[peer], lambda me, step: held_sum.at[step], *sems[0]
    )
    ready["idle"]()
    total = part[q].astype(F32)
    for step, copy in enumerate(copies, 1):
        copy.wait_recv()
        total = total + held_sum[step].astype(F32)
    all_z[g] = total.astype(BF16)
    more = send("gz", groups, lambda peer: all_z.at[g], lambda me, step: all_z.at[me], *sems[1])
    copies = settle(copies, more)
    ready["to_z"]()
    for copy in more:
        copy.wait_recv()
    rows = []
    for group in range(groups):
        rows += unpack(all_z[group].astype(F32))
    rows = jnp.concatenate(rows, 0).astype(BF16)
    bins = jnp.where(kept, jnp.dot(to_z[g], rows, preferred_element_type=F32), 0.0)
    modes = KY * MX
    length = 8 * 128
    zero = jnp.zeros((share, length - WIDE), F32)
    halves = []
    for half in range(2):
        for kz in range(own_kz):
            at = (half * own_kz + kz) * share
            wide = jnp.concatenate([bins[at : at + share], zero], 1)
            if kz == 0:
                line = wide
            else:
                line = line + pltpu.roll(wide, kz * modes, 1)
        halves.append(line)
    all_c[q] = jnp.concatenate(halves, 0)[:, : all_c.shape[-1]].astype(BF16)
    more = send("gy", quarters, lambda peer: all_c.at[q], lambda me, step: all_c.at[me], *sems[2])
    copies = settle(copies, more)
    modal[...] = jnp.zeros_like(modal)
    ready["weights"]()
    for copy in more:
        copy.wait_recv()
    spec[...] = all_c[...].reshape(spec.shape).astype(F32)
    weigh_modes(spec, weights, modal)
    line = modal[...]
    rows = []
    for kz in range(own_kz):
        moved = line if kz == 0 else pltpu.roll(line, length - kz * modes, 1)
        rows.append(moved[:, :WIDE])
    rows = jnp.concatenate(rows, 0).astype(BF16)
    ready["from_z"]()
    back = jnp.dot(from_z[g], rows, preferred_element_type=F32)
    back = jnp.where(kept, back, 0.0)
    for group in range(groups):
        first = group * planes * 2 * share
        blocks = [back[first + at * share : first + (at + 1) * share] for at in range(2 * planes)]
        out_z[group] = pack(blocks).astype(BF16)
    more = send(
        "gz", groups, lambda peer: out_z.at[peer], lambda me, step: held_z.at[step], *sems[3]
    )
    copies = settle(copies, more)
    ready["from_y"]()
    total = out_z[g].astype(F32)
    for step, copy in enumerate(more, 1):
        copy.wait_recv()
        total = total + held_z[step].astype(F32)
    all_o[q] = total.astype(BF16)
    more = send("gy", quarters, lambda peer: all_o.at[q], lambda me, step: all_o.at[me], *sems[4])
    copies = settle(copies, more)
    for copy in more:
        copy.wait_recv()
    real, imag = [], []
    pieces = [unpack(all_o[quarter].astype(F32)) for quarter in range(quarters)]
    for z in range(planes):
        for piece in pieces:
            real.append(piece[2 * z])
            imag.append(piece[2 * z + 1])
    real, imag = jnp.concatenate(real, 0), jnp.concatenate(imag, 0)
    real, imag = cosine * real - sine * imag, sine * real + cosine * imag
    rows = jnp.concatenate([real, imag], 1).astype(BF16)
    result = jnp.dot(rows, from_y[...], preferred_element_type=F32).astype(BF16)
    return result, copies


def prepare_maps(skip, lift_t, bias, lift, planes):
    channels, hidden = lift_t.shape
    scaled = bias * F32(HALF)
    high = scaled.astype(BF16).astype(F32)
    middle = (scaled - high).astype(BF16).astype(F32)
    low = scaled - high - middle
    tail = jnp.zeros((128 - channels - 3, hidden), F32)
    tall = jnp.concatenate([lift_t.astype(F32), high, middle, low, tail], 0)
    lift[...] = tall.T.astype(BF16)
    blank = jnp.zeros((channels, channels), F32)
    skip = skip.astype(F32)
    block_rows = []
    for z in range(planes):
        block_rows.append(
            jnp.concatenate([skip if z == other else blank for other in range(planes)], 1)
        )
    return jnp.concatenate(block_rows, 0).astype(BF16)


def pointwise(current, rows_y, from_x, skip_all, lift, down):
    rows, length = current.shape
    channels = down.shape[0]
    planes = rows // channels
    ones = (lax.broadcasted_iota(jnp.int32, (16, planes * length), 0) < 3).astype(F32).astype(BF16)
    depth, width = from_x.shape
    halves = []
    for half in range(length // width):
        left = jnp.concatenate([rows_y[:, half * depth : (half + 1) * depth], skip_all], 1)
        right = jnp.concatenate([from_x[...], current[:, half * width : (half + 1) * width]], 0)
        halves.append(jnp.dot(left, right, preferred_element_type=F32))
    mixed = jnp.concatenate(halves, 1)
    lower = (mixed * F32(HALF)).astype(BF16)
    wide = jnp.concatenate([lower[z * channels : (z + 1) * channels] for z in range(planes)], 1)
    wide = jnp.concatenate([wide, ones], 0)
    value = jnp.dot(lift[:, : channels + 16], wide, preferred_element_type=F32)
    value = (value + value * lax.erf(value)).astype(BF16)
    change = jnp.dot(down, value, preferred_element_type=F32) * F32(HALF)
    return [
        (mixed[z * channels : (z + 1) * channels] + change[:, z * length : (z + 1) * length]).astype(BF16)
        for z in range(planes)
    ]


def meet(groups, quarters):
    barrier = pltpu.get_barrier_semaphore()
    for axis, count in (("gz", groups), ("gy", quarters)):
        me = lax.axis_index(axis)
        for step in range(1, count):
            pl.semaphore_signal(
                barrier,
                inc=1,
                device_id={axis: lax.rem(me + step, count)},
                device_id_type=pl.DeviceIdType.MESH,
            )
    return lambda: pl.semaphore_wait(barrier, groups + quarters - 2)


def loads(pairs, sem):
    copies = [
        pltpu.make_async_copy(source, target, sem.at[at])
        for at, (source, target) in enumerate(pairs)
    ]
    for copy in copies:
        copy.start()
    return copies


def modes_kernel(
    sizes, raw_hbm, to_rows_hbm, to_x_hbm, to_y_hbm, weights_hbm, from_y_hbm, from_x_hbm,
    turn_hbm, to_z_hbm, from_z_hbm, skip_hbm, lift_t_hbm, bias_hbm, down_hbm,
    rows_out, field_hbm, raw, to_rows, to_x, to_y, weights, from_y, from_x, turn, to_z, from_z,
    skip, lift_t, bias, down, field, later, lift, skip_all, rows_y, local_sem, late_sem, out_sem, *rest,
):
    groups, quarters = sizes
    layers = weights_hbm.shape[0]
    greeting = meet(groups, quarters)
    channels, planes, quarter, length_x = raw.shape
    lines = 2 * YB
    pieces = quarter // lines
    copies = loads(
        [(to_rows_hbm, to_rows)]
        + [
            (raw_hbm.at[:, :, pl.ds(at * lines, lines)], raw.at[:, :, pl.ds(at * lines, lines)])
            for at in range(pieces)
        ]
        + [(to_x_hbm, to_x), (to_y_hbm, to_y), (turn_hbm, turn)],
        local_sem,
    )
    copies[0].wait()
    along = []
    for at in range(pieces):
        copies[1 + at].wait()
        if at == 1:
            copies[1 + pieces].wait()
        for z in range(planes):
            block = raw[:, z, at * lines : (at + 1) * lines, :].astype(F32)
            for half in range(2):
                eight = block[:, half * YB : (half + 1) * YB].reshape(channels * YB, length_x)
                turned = jnp.dot(
                    to_rows[...], eight.astype(BF16), preferred_element_type=F32
                ).astype(BF16)
                for j in range(YB):
                    field[
                        at * 2 + half,
                        z * channels : (z + 1) * channels,
                        j * length_x : (j + 1) * length_x,
                    ] = turned[j * channels : (j + 1) * channels]
        if at > 0:
            along += along_x(field, 2 * at - 2, 2, to_x)
    along += along_x(field, 2 * pieces - 2, 2, to_x)
    for copy in copies[2 + pieces :]:
        copy.wait()
    waits = loads(
        [(to_z_hbm, to_z)]
        + [(weights_hbm.at[layer], weights.at[layer]) for layer in range(layers)]
        + [(from_z_hbm, from_z), (from_y_hbm, from_y), (from_x_hbm, from_x)]
        + [(skip_hbm, skip), (lift_t_hbm, lift_t), (bias_hbm, bias), (down_hbm, down)],
        late_sem,
    )
    current, sent = field, []
    for layer in range(layers):
        if layer > 0:
            along = []
            source, current = current, (later if layer % 2 else field)
            for first in range(0, quarter // YB, 2):
                parts = pointwise(
                    jnp.concatenate([source[b] for b in range(first, first + 2)], 1),
                    rows_y[:, first * YB * SUB : (first + 2) * YB * SUB], from_x, skip_all[...],
                    lift, down[layer - 1],
                )
                for z, part in enumerate(parts):
                    for b in range(2):
                        current[first + b, z * channels : (z + 1) * channels, :] = part[
                            :, b * YB * length_x : (b + 1) * YB * length_x
                        ]
                along += along_x(current, first, 2, to_x)
            if layer == layers - 1:
                leave = pltpu.make_async_copy(current, field_hbm, out_sem.at[0])
                leave.start()
        spectrum = jnp.dot(jnp.concatenate(along, 1), to_y[...], preferred_element_type=F32)
        buffers = rest[9 * layer : 9 * layer + 9]
        at = 9 * layers + 10 * layer
        sems = [(rest[at + 2 * phase], rest[at + 2 * phase + 1]) for phase in range(5)]
        nothing = lambda: None

        def idle(layer=layer, before=sent):
            for copy in before:
                copy.wait_send()
            if layer == 0:
                for copy in waits[layers + 3 :]:
                    copy.wait()
            if layer < layers - 1:
                skip_all[...] = prepare_maps(
                    skip[layer], lift_t[layer], bias[layer : layer + 1], lift, planes
                )

        ready = {
            "greet": nothing if layer else greeting,
            "idle": idle,
            "to_z": nothing if layer else waits[0].wait,
            "weights": waits[1 + layer].wait,
            "from_z": nothing if layer else waits[layers + 1].wait,
            "from_y": nothing if layer else waits[layers + 2].wait,
        }
        rows, sent = exchange_modes(
            spectrum, (turn, to_z, from_z, from_y), weights.at[layer], buffers, sems, ready
        )
        if layer == layers - 1:
            rows_out[...] = rows
        else:
            rows_y[...] = rows
    for copy in sent:
        copy.wait_send()
    leave.wait()


def last_kernel(
    layer, field_hbm, rows_hbm, from_x_hbm, from_rows_hbm, skip_hbm, lift_t_hbm, bias_hbm,
    down_hbm, out_hbm, rows_y, from_x, from_rows, skip, lift_t, bias, down, field, lift, result,
    in_sem, out_sem,
):
    blocks = field.shape[0]
    channels, planes, _, length_x = result.shape
    lines = 2 * YB
    steps = blocks // 2
    copies = loads(
        [
            (skip_hbm, skip), (lift_t_hbm, lift_t), (bias_hbm, bias), (down_hbm, down),
            (rows_hbm, rows_y), (from_x_hbm, from_x), (from_rows_hbm, from_rows),
        ]
        + [(field_hbm.at[pl.ds(2 * at, 2)], field.at[pl.ds(2 * at, 2)]) for at in range(steps)],
        in_sem,
    )
    for copy in copies[:7]:
        copy.wait()
    copies = copies[7:]
    skip_all = prepare_maps(skip[layer], lift_t[layer], bias[layer : layer + 1], lift, planes)
    outs = []
    for first in range(0, blocks, 4):
        for at in range(first // 2, (first + 4) // 2):
            copies[at].wait()
        group = range(first, first + 4)
        both = pointwise(
            jnp.concatenate([field[b] for b in group], 1),
            rows_y[:, first * YB * SUB : (first + 4) * YB * SUB], from_x, skip_all, lift,
            down[layer],
        )
        for at in range(first // 2, (first + 4) // 2):
            window = pl.ds(at * lines, lines)
            for z, part in enumerate(both):
                turned = []
                for b in (2 * at, 2 * at + 1):
                    rows = [
                        part[:, j * length_x : (j + 1) * length_x]
                        for j in range((b - first) * YB, (b - first + 1) * YB)
                    ]
                    tall = jnp.concatenate(rows, 0)
                    tall = jnp.dot(from_rows[...], tall, preferred_element_type=F32)
                    turned.append(tall.reshape(channels, YB, length_x))
                result[:, z, window, :] = jnp.concatenate(turned, 1).astype(BF16)
            copy = pltpu.make_async_copy(
                result.at[:, :, window], out_hbm.at[:, :, window], out_sem.at[at]
            )
            copy.start()
            outs.append(copy)
    for copy in outs:
        copy.wait()


def fast_device(noisy_field, spectral_weights, skip_weights, in_weights, in_bias, out_weights):
    channels, planes, quarter, length_x = noisy_field.shape
    layer_count = spectral_weights.shape[0]
    groups, quarters = lax.axis_size("gz"), lax.axis_size("gy")
    own_kz = KZ // groups
    own_modes = spectral_weights.shape[2]
    share = channels // quarters
    blocks = quarter // YB
    hidden = in_weights.shape[1]
    tables = np_tables(groups, quarters, planes, quarter, length_x, channels)
    tables = {name: jnp.asarray(value) for name, value in tables.items()}
    weights = spectral_weights.transpose(0, 1, 3, 4, 2)
    weights = weights.reshape(layer_count, 2, channels * share, own_modes)
    lift_t = in_weights.transpose(0, 2, 1)
    rows_shape = jax.ShapeDtypeStruct((planes * channels, quarter * SUB), BF16)
    field_shape = jax.ShapeDtypeStruct((blocks, planes * channels, YB * length_x), BF16)
    anywhere = pl.BlockSpec(memory_space=pltpu.HBM)
    vmem = pl.BlockSpec(memory_space=pltpu.VMEM)

    def held(name):
        return pltpu.VMEM(tables[name].shape, tables[name].dtype)

    full = -(-own_modes // 128) * 128
    block = (planes * 2 * share * 2 + share, 128)
    traffic = [
        pltpu.VMEM((quarters,) + block, BF16),
        pltpu.VMEM((quarters,) + block, BF16),
        pltpu.VMEM((groups,) + block, BF16),
        pltpu.VMEM((quarters, 2 * share, full), BF16),
        pltpu.VMEM((quarters * 2 * share, full), F32),
        pltpu.VMEM((2 * share, 8 * 128), F32),
        pltpu.VMEM((groups,) + block, BF16),
        pltpu.VMEM((groups,) + block, BF16),
        pltpu.VMEM((quarters,) + block, BF16),
    ]
    signals = []
    for count in (quarters, groups, quarters, groups, quarters):
        signals += [pltpu.SemaphoreType.DMA((count,))] * 2
    lift_held = pltpu.VMEM((hidden, 128), BF16)
    field_held = pltpu.VMEM(field_shape.shape, BF16)
    raw_held = pltpu.VMEM(noisy_field.shape, BF16)
    maps = (skip_weights, lift_t, in_bias, out_weights)
    maps_held = [pltpu.VMEM(value.shape, value.dtype) for value in maps]
    pieces = quarter // (2 * YB)
    rows, field = pl.pallas_call(
        functools.partial(modes_kernel, (groups, quarters)),
        out_shape=[rows_shape, field_shape],
        in_specs=[anywhere] * 14,
        out_specs=[vmem, anywhere],
        scratch_shapes=[
            raw_held, held("to_rows"), held("to_x"), held("to_y"),
            pltpu.VMEM(weights.shape, BF16), held("from_y"), held("from_x"),
            held("turn"), held("to_z"), held("from_z"), *maps_held, field_held, field_held, lift_held,
            pltpu.VMEM((planes * channels, planes * channels), BF16), pltpu.VMEM(rows_shape.shape, BF16),
            pltpu.SemaphoreType.DMA((4 + pieces,)), pltpu.SemaphoreType.DMA((8 + layer_count,)),
            pltpu.SemaphoreType.DMA((1,)),
        ] + traffic * layer_count + signals * layer_count,
        compiler_params=pltpu.CompilerParams(
            collective_id=0, has_side_effects=True, vmem_limit_bytes=VMEM_LIMIT
        ),
        name="modes",
    )(
        noisy_field, tables["to_rows"], tables["to_x"], tables["to_y"], weights, tables["from_y"],
        tables["from_x"], tables["turn"], tables["to_z"], tables["from_z"], *maps,
    )
    return pl.pallas_call(
        functools.partial(last_kernel, layer_count - 1),
        out_shape=jax.ShapeDtypeStruct(noisy_field.shape, BF16),
        in_specs=[anywhere, pl.BlockSpec(memory_space=pl.ANY)] + [anywhere] * 6,
        out_specs=anywhere,
        scratch_shapes=[
            pltpu.VMEM(rows_shape.shape, BF16), held("from_x"), held("from_rows"), *maps_held,
            field_held, lift_held, raw_held, pltpu.SemaphoreType.DMA((7 + pieces,)),
            pltpu.SemaphoreType.DMA((pieces,)),
        ],
        compiler_params=pltpu.CompilerParams(vmem_limit_bytes=VMEM_LIMIT),
        name="last_layer",
    )(field, rows, tables["from_x"], tables["from_rows"], *maps)


def pick(noisy_field, spectral_weights, *rest):
    groups, quarters = lax.axis_size("gz"), lax.axis_size("gy")
    channels, planes, quarter, _ = noisy_field.shape
    fits = (
        KZ % groups == 0
        and spectral_weights.shape[2] == KZ // groups * KY * MX
        and spectral_weights.shape[2] <= 8 * 128 - 128
        and channels == 8 * quarters
        and planes == 2
        and quarter % (4 * YB) == 0
    )
    body = fast_device if fits else per_device
    return body(noisy_field, spectral_weights, *rest)


def solution(mesh):
    in_specs = (P(None, "gz", "gy", None), P(None, None, "gz", None, "gy"), P(), P(), P(), P())
    out_specs = P(None, "gz", "gy", None)
    return jax.shard_map(
        pick, mesh=mesh, in_specs=in_specs, out_specs=out_specs, check_vma=False
    )
```

```python
import functools
import math

import jax
import jax.numpy as jnp
from jax import lax
from jax.experimental import pallas as pl
from jax.experimental.pallas import tpu as pltpu
from jax.sharding import PartitionSpec as P
import ml_dtypes
import numpy as np

MX = 12
KY = 24
KZ = 24
KP = KY // 2
LANES = 128
ROWS = 32
F32 = jnp.float32
BF16 = jnp.bfloat16


def angles(number, positions, length, signed):
    kept = jnp.arange(number, dtype=jnp.int32)
    if signed:
        kept = jnp.where(kept < number // 2, kept, kept - number)
    phases = jnp.mod(kept[:, None] * positions[None, :], length)
    radians = 2.0 * math.pi / length * phases.astype(jnp.float32)
    return (jnp.cos(radians), jnp.sin(radians))


def forward_table(length):
    cosine, sine = angles(MX, jnp.arange(length, dtype=jnp.int32), length, False)
    part = jnp.concatenate([cosine, -sine, -sine, -cosine], 0)
    table = jnp.concatenate([part, part], 0).T.astype(BF16)
    return jnp.pad(table, ((0, 0), (0, LANES - 8 * MX)))


def inverse_table(length):
    cosine, sine = angles(MX, jnp.arange(length, dtype=jnp.int32), length, False)
    factor = jnp.where(jnp.arange(MX) == 0, F32(1.0), F32(2.0))[:, None]
    scale = 1.0 / math.sqrt(2.0 * KZ * KY * MX)
    half = jnp.concatenate([cosine * factor, -sine * factor], 0) * scale
    table = jnp.concatenate([half] * 4, 0).astype(BF16)
    return jnp.pad(table, ((0, LANES - 8 * MX), (0, 0)))


def y_weights(positions, length):
    cosine, sine = angles(KY, positions, length, True)
    both = jnp.stack([cosine, sine], -1).transpose(1, 0, 2)
    lanes = jnp.repeat(both.reshape(positions.shape[0], KP, 4), 2 * MX, axis=2)
    return jnp.pad(lanes, ((0, 0), (0, 0), (0, LANES - 8 * MX)))


def gelu(value):
    return 0.5 * value * (1.0 + lax.erf(value * F32(math.sqrt(0.5))))


def accumulate_modes(along, weight_ref, modes_ref):
    rows, channels = along.shape[0], along.shape[1]

    @pl.when(pl.program_id(1) == 0)
    def _():
        modes_ref[...] = jnp.zeros_like(modes_ref)

    for kp in range(KP):
        total = along[0] * weight_ref[0, kp : kp + 1, :]
        for y in range(1, rows):
            total = total + along[y] * weight_ref[y, kp : kp + 1, :]
        modes_ref[0, kp] += total


def forward_kernel(field_ref, weight_ref, table_ref, modes_ref):
    rows, channels, length = field_ref.shape
    flat = field_ref[...].reshape(rows * channels, length)
    along = jnp.dot(flat, table_ref[...], preferred_element_type=F32)
    accumulate_modes(along.reshape(rows, channels, LANES), weight_ref, modes_ref)


def layer_body(
    field_ref, planes_ref, weight_ref, inverse_ref, skip_ref, lift_ref, bias_ref, down_ref, out_ref
):
    rows, channels, length = field_ref.shape
    parts = []
    for y in range(rows):
        total = planes_ref[0, 0] * weight_ref[y, 0:1, :]
        for kp in range(1, KP):
            total = total + planes_ref[0, kp] * weight_ref[y, kp : kp + 1, :]
        parts.append(total.astype(BF16))
    stacked = jnp.concatenate(parts, 0)
    spatial = jnp.dot(stacked, inverse_ref[...], preferred_element_type=F32)
    wide_spatial = jnp.concatenate(
        [spatial[y * channels : (y + 1) * channels] for y in range(rows)], 1
    )
    wide_field = jnp.concatenate([field_ref[y] for y in range(rows)], 1)
    mixed = wide_spatial + jnp.dot(skip_ref[...], wide_field, preferred_element_type=F32)
    before = jnp.dot(lift_ref[...], mixed.astype(BF16), preferred_element_type=F32)
    hidden = gelu(before + bias_ref[...]).astype(BF16)
    result = mixed + jnp.dot(down_ref[...], hidden, preferred_element_type=F32)
    result = result.astype(BF16)
    for y in range(rows):
        out_ref[y] = result[:, y * length : (y + 1) * length]


def middle_kernel(
    field_ref, planes_ref, weight_ref, inverse_ref, skip_ref, lift_ref, bias_ref, down_ref,
    table_ref, out_ref, modes_ref,
):
    layer_body(
        field_ref, planes_ref, weight_ref, inverse_ref, skip_ref, lift_ref, bias_ref, down_ref,
        out_ref,
    )
    forward_kernel(out_ref, weight_ref, table_ref, modes_ref)


def whole(shape):
    return pl.BlockSpec(shape, lambda z, y: (0,) * len(shape))


def run_forward(field, weights_y, table, planes):
    total, channels, length = field.shape
    steps = total // planes // ROWS
    return pl.pallas_call(
        forward_kernel,
        grid=(planes, steps),
        in_specs=[
            pl.BlockSpec((ROWS, channels, length), lambda z, y: (z * steps + y, 0, 0)),
            pl.BlockSpec((ROWS, KP, LANES), lambda z, y: (y, 0, 0)),
            whole(table.shape),
        ],
        out_specs=pl.BlockSpec((1, KP, channels, LANES), lambda z, y: (z, 0, 0, 0)),
        out_shape=jax.ShapeDtypeStruct((planes, KP, channels, LANES), F32),
        name="forward_modes",
    )(field, weights_y, table)


def run_layer(field, plane_modes, weights_y, inverse, skip, lift, bias, down, table):
    total, channels, length = field.shape
    planes = plane_modes.shape[0]
    steps = total // planes // ROWS
    field_spec = pl.BlockSpec((ROWS, channels, length), lambda z, y: (z * steps + y, 0, 0))
    modes_spec = pl.BlockSpec((1, KP, channels, LANES), lambda z, y: (z, 0, 0, 0))
    field_shape = jax.ShapeDtypeStruct(field.shape, BF16)
    modes_shape = jax.ShapeDtypeStruct(plane_modes.shape, F32)
    args = [field, plane_modes, weights_y, inverse, skip, lift, bias, down]
    specs = [
        field_spec,
        modes_spec,
        pl.BlockSpec((ROWS, KP, LANES), lambda z, y: (y, 0, 0)),
        whole(inverse.shape),
        whole(skip.shape),
        whole(lift.shape),
        whole(bias.shape),
        whole(down.shape),
    ]
    if table is None:
        return pl.pallas_call(
            layer_body,
            grid=(planes, steps),
            in_specs=specs,
            out_specs=field_spec,
            out_shape=field_shape,
            name="last_layer",
        )(*args)
    return pl.pallas_call(
        middle_kernel,
        grid=(planes, steps),
        in_specs=specs + [whole(table.shape)],
        out_specs=[field_spec, modes_spec],
        out_shape=[field_shape, modes_shape],
        name="middle_layer",
    )(*args, table)


def fold_modes(modes, scale):
    planes, _, channels, _ = modes.shape
    split = modes[..., : 8 * MX].reshape(planes, KP, channels, 2, 2, 2, MX)
    folded = (split[:, :, :, :, 0] + split[:, :, :, :, 1]) * scale
    ordered = folded.transpose(0, 4, 2, 1, 3, 5)
    return ordered.reshape(planes * 2, channels, KY * MX)


def unfold_modes(rows, planes):
    channels = rows.shape[1]
    real, imag = (
        rows.astype(F32).reshape(planes, 2, channels, KP, 2, MX)[:, part] for part in range(2)
    )
    lanes = jnp.stack([real, imag, -imag, real], axis=4)
    lanes = lanes.transpose(0, 2, 1, 3, 4, 5).reshape(planes, KP, channels, 8 * MX)
    return jnp.pad(lanes, ((0, 0), (0, 0), (0, 0), (0, LANES - 8 * MX)))


def greet(axes):
    barrier = pltpu.get_barrier_semaphore()
    total = 0
    for axis, count in axes:
        me = lax.axis_index(axis)
        for step in range(1, count):
            pl.semaphore_signal(
                barrier,
                inc=1,
                device_id={axis: lax.rem(me + step, count)},
                device_id_type=pl.DeviceIdType.MESH,
            )
        total += count - 1
    pl.semaphore_wait(barrier, total)


def spread(axis, count, source, held, send_sem, recv_sem):
    me = lax.axis_index(axis)
    copies = []
    for step in range(1, count):
        peer = lax.rem(me + step, count)
        copy = pltpu.make_async_remote_copy(
            src_ref=source(peer),
            dst_ref=held.at[step],
            send_sem=send_sem.at[step],
            recv_sem=recv_sem.at[step],
            device_id={axis: peer},
            device_id_type=pl.DeviceIdType.MESH,
        )
        copy.start()
        copies.append(copy)
    return copies


def collect(axis, count, own, held, copies, out_ref):
    me = lax.axis_index(axis)
    out_ref[me] = own
    for step, copy in enumerate(copies, 1):
        copy.wait_recv()
        out_ref[lax.rem(me - step + count, count)] = held[step]


def z_and_y(groups, quarters, own_ref, matrix_ref, out_ref, held_z, all_z, stage, held_y, sems):
    send_z, recv_z, send_y, recv_y = sems
    first = spread("gz", groups, lambda peer: own_ref, held_z, send_z, recv_z)
    collect("gz", groups, own_ref[...], held_z, first, all_z)
    rows = all_z[...].reshape(-1, all_z.shape[-1]).astype(F32)
    stage[...] = jnp.dot(
        matrix_ref[...], rows, precision=lax.Precision.HIGHEST, preferred_element_type=F32
    ).astype(BF16)
    second = spread("gy", quarters, lambda peer: stage, held_y, send_y, recv_y)
    collect("gy", quarters, stage[...], held_y, second, out_ref)
    return first + second


def sum_kernel(
    groups, quarters, own_ref, matrix_ref, out_ref, held_sum, summed, held_z, all_z, stage, held_y,
    send_sum, recv_sum, *sems,
):
    greet((("gz", groups), ("gy", quarters)))
    copies = spread("gy", quarters, lambda peer: own_ref.at[peer], held_sum, send_sum, recv_sum)
    total = own_ref[lax.axis_index("gy")]
    for step, copy in enumerate(copies, 1):
        copy.wait_recv()
        total = total + held_sum[step]
    summed[...] = total.astype(BF16)
    copies += z_and_y(
        groups, quarters, summed, matrix_ref, out_ref, held_z, all_z, stage, held_y, sems
    )
    for copy in copies:
        copy.wait_send()


def spread_kernel(
    groups, quarters, own_ref, matrix_ref, out_ref, held_z, all_z, stage, held_y, *sems
):
    greet((("gz", groups), ("gy", quarters)))
    copies = z_and_y(
        groups, quarters, own_ref, matrix_ref, out_ref, held_z, all_z, stage, held_y, sems
    )
    for copy in copies:
        copy.wait_send()


def communicate(value, matrix, summing, number):
    groups, quarters = lax.axis_size("gz"), lax.axis_size("gy")
    block = value.shape[-2:]
    result = (matrix.shape[0], block[1])
    vmem = pl.BlockSpec(memory_space=pltpu.VMEM)
    scratch = [
        pltpu.VMEM((groups,) + block, BF16),
        pltpu.VMEM((groups,) + block, BF16),
        pltpu.VMEM(result, BF16),
        pltpu.VMEM((quarters,) + result, BF16),
    ]
    sems = [pltpu.SemaphoreType.DMA((count,)) for count in (groups, groups, quarters, quarters)]
    if summing:
        scratch = [pltpu.VMEM((quarters,) + block, F32), pltpu.VMEM(block, BF16)] + scratch
        sems = [pltpu.SemaphoreType.DMA((quarters,))] * 2 + sems
    return pl.pallas_call(
        functools.partial(sum_kernel if summing else spread_kernel, groups, quarters),
        out_shape=jax.ShapeDtypeStruct((quarters,) + result, BF16),
        in_specs=[vmem, vmem],
        out_specs=vmem,
        scratch_shapes=scratch + sems,
        compiler_params=pltpu.CompilerParams(collective_id=number, has_side_effects=True),
        name="exchange",
    )(value, matrix)


def z_matrix(cosine, sine, inverse):
    sign = -1.0 if inverse else 1.0
    return jnp.stack(
        [jnp.stack([cosine, sign * sine]), jnp.stack([-sign * sine, cosine])]
    )


def weigh(spectrum, coefficients):
    real, imag = spectrum[0], spectrum[1]

    def product(left, right):
        return jnp.einsum("zcq,zqco->zoq", left, right, preferred_element_type=F32)

    modal_real = product(real, coefficients[0]) - product(imag, coefficients[1])
    modal_imag = product(real, coefficients[1]) + product(imag, coefficients[0])
    return jnp.stack([modal_real, modal_imag]).astype(BF16)


def exchange(partial, local_weights, planes, full_z, number):
    highest = lax.Precision.HIGHEST
    channels = partial.shape[1]
    modes = KY * MX
    here_z = lax.axis_index("gz") * planes + jnp.arange(planes, dtype=jnp.int32)
    all_z = jnp.arange(full_z, dtype=jnp.int32)
    own_modes = local_weights.shape[1]
    groups = lax.axis_size("gz")
    if own_modes % modes == 0:
        own_kz = own_modes // modes
        cosine, sine = angles(KZ, all_z, full_z, True)
        first = lax.axis_index("gz") * own_kz
        cosine = lax.dynamic_slice_in_dim(cosine, first, own_kz, 0)
        sine = lax.dynamic_slice_in_dim(sine, first, own_kz, 0)
        forward = z_matrix(cosine, sine, False).transpose(0, 2, 3, 1)
        forward = forward.reshape(2 * own_kz, 2 * full_z)
        quarters = lax.axis_size("gy")
        share = channels // quarters
        split = partial.reshape(planes * 2, quarters, share, modes).transpose(1, 0, 2, 3)
        spectrum = communicate(
            split.reshape(quarters, planes * 2 * share, modes),
            jnp.kron(forward, jnp.eye(share, dtype=F32)),
            True,
            number,
        )
        spectrum = spectrum.reshape(quarters, 2, own_kz, share, modes).transpose(1, 2, 0, 3, 4)
        spectrum = spectrum.reshape(2, own_kz, channels, modes)
        coefficients = local_weights.reshape(2, own_kz, modes, channels, -1)
        modal = weigh(spectrum, coefficients)
        outputs = modal.shape[2]
        cosine, sine = angles(KZ, here_z, full_z, True)
        inverse = z_matrix(cosine, sine, True).reshape(2, 2, groups, own_kz, planes)
        inverse = inverse.transpose(4, 0, 2, 1, 3).reshape(planes * 2, groups * 2 * own_kz)
        rows = communicate(
            modal.reshape(2 * own_kz * outputs, modes),
            jnp.kron(inverse, jnp.eye(outputs, dtype=F32)),
            False,
            number + 1,
        )
        rows = rows.reshape(quarters, planes * 2, outputs, modes).transpose(1, 0, 2, 3)
        return rows.reshape(planes * 2, channels, modes)
    cosine, sine = angles(KZ, here_z, full_z, True)
    forward = z_matrix(cosine, sine, False).transpose(0, 2, 3, 1)
    sums = jnp.einsum(
        "akr,rcq->ackq", forward.reshape(2, KZ, planes * 2), partial, precision=highest
    ).reshape(2, channels, KZ * modes)
    sums = lax.psum_scatter(sums, "gz", scatter_dimension=2, tiled=True)
    spectrum = lax.psum(sums, "gy").astype(BF16)[:, None]
    coefficients = lax.all_gather(local_weights, "gy", axis=3, tiled=True)[:, None]
    modal = weigh(spectrum, coefficients)[:, 0]
    modal = lax.all_gather(modal, "gz", axis=2, tiled=True)
    modal = modal.astype(F32).reshape(2, channels, KZ, modes)
    inverse = z_matrix(cosine, sine, True)
    rows = jnp.einsum("abkz,bckq->zacq", inverse, modal, precision=highest)
    return rows.reshape(planes * 2, channels, modes)


def per_device(noisy_field, spectral_weights, skip_weights, in_weights, in_bias, out_weights):
    channels, planes, quarter, length_x = noisy_field.shape
    layer_count = spectral_weights.shape[0]
    full_y = quarter * lax.axis_size("gy")
    full_z = planes * lax.axis_size("gz")
    y_positions = lax.axis_index("gy") * quarter + jnp.arange(quarter, dtype=jnp.int32)
    weights_y = y_weights(y_positions, full_y)
    table = forward_table(length_x)
    inverse = inverse_table(length_x)
    scale = 1.0 / math.sqrt(length_x * full_y * full_z)
    field = noisy_field.transpose(1, 2, 0, 3).reshape(planes * quarter, channels, length_x)
    modes = run_forward(field, weights_y, table, planes)
    for layer in range(layer_count):
        rows = exchange(
            fold_modes(modes, scale), spectral_weights[layer], planes, full_z, 2 * layer
        )
        last = layer == layer_count - 1
        result = run_layer(
            field,
            unfold_modes(rows, planes),
            weights_y,
            inverse,
            skip_weights[layer],
            in_weights[layer],
            in_bias[layer][:, None],
            out_weights[layer],
            None if last else table,
        )
        if last:
            field = result
        else:
            field, modes = result
    return field.reshape(planes, quarter, channels, length_x).transpose(2, 0, 1, 3)


HALF = math.sqrt(0.5)
WIDE = 384
SUB = 32
YB = 8
HJ = 4
VMEM_LIMIT = 60 * 2**20


def np_angles(number, positions, length, signed):
    kept = np.arange(number)
    if signed:
        kept = np.where(kept < number // 2, kept, kept - number)
    phases = np.mod(kept[:, None] * np.asarray(positions)[None, :], length)
    radians = 2.0 * math.pi / length * phases
    return np.cos(radians), np.sin(radians)


def np_tables(groups, quarters, planes, quarter, length_x, channels):
    full_y, full_z = quarter * quarters, planes * groups
    share = channels // quarters
    own_kz = KZ // groups
    modes = KY * MX
    x_cos, x_sin = np_angles(MX, range(length_x), length_x, False)
    to_x = np.zeros((HJ, length_x, HJ, SUB))
    from_x = np.zeros((HJ, SUB, HJ, length_x))
    factor = np.where(np.arange(MX) == 0, 1.0, 2.0)[:, None] / math.sqrt(2.0 * KZ * KY * MX)
    for j in range(HJ):
        to_x[j, :, j, :MX] = x_cos.T
        to_x[j, :, j, MX : 2 * MX] = -x_sin.T
        from_x[j, :MX, j, :] = x_cos * factor
        from_x[j, MX : 2 * MX, j, :] = -x_sin * factor
    y_cos, y_sin = np_angles(KY, range(quarter), full_y, True)
    to_y = np.zeros((quarter, SUB, 2, WIDE))
    from_y = np.zeros((2, WIDE, quarter, SUB))
    scale = 1.0 / math.sqrt(length_x * full_y * full_z)
    for ky in range(KY):
        for kx in range(MX):
            at = ky * MX + kx
            cosine, sine = y_cos[ky], y_sin[ky]
            to_y[:, kx, 0, at] = cosine * scale
            to_y[:, MX + kx, 0, at] = sine * scale
            to_y[:, kx, 1, at] = -sine * scale
            to_y[:, MX + kx, 1, at] = cosine * scale
            from_y[0, at, :, kx] = cosine
            from_y[1, at, :, kx] = -sine
            from_y[0, at, :, MX + kx] = sine
            from_y[1, at, :, MX + kx] = cosine
    turn_cos, turn_sin = np_angles(KY, np.arange(quarters) * quarter, full_y, True)
    turn = np.zeros((quarters, 2, WIDE))
    turn[:, 0, :modes] = np.repeat(turn_cos.T, MX, axis=1)
    turn[:, 1, :modes] = np.repeat(turn_sin.T, MX, axis=1)
    z_cos, z_sin = np_angles(KZ, range(full_z), full_z, True)
    z_cos = z_cos.reshape(groups, own_kz, groups, planes)
    z_sin = z_sin.reshape(groups, own_kz, groups, planes)
    forward = np.zeros((groups, 2, own_kz, groups, planes, 2))
    forward[:, 0, :, :, :, 0] = z_cos
    forward[:, 0, :, :, :, 1] = z_sin
    forward[:, 1, :, :, :, 0] = -z_sin
    forward[:, 1, :, :, :, 1] = z_cos
    forward = forward.reshape(groups, 2 * own_kz, groups * planes * 2)
    back_cos = z_cos.transpose(0, 2, 3, 1)
    back_sin = z_sin.transpose(0, 2, 3, 1)
    inverse = np.zeros((groups, groups, planes, 2, own_kz, 2))
    inverse[:, :, :, 0, :, 0] = back_cos
    inverse[:, :, :, 0, :, 1] = -back_sin
    inverse[:, :, :, 1, :, 0] = back_sin
    inverse[:, :, :, 1, :, 1] = back_cos
    inverse = inverse.reshape(groups, groups * planes * 2, own_kz * 2)
    eye = np.eye(share)[None]
    to_rows = np.eye(channels * YB).reshape(channels, YB, -1).transpose(1, 0, 2)
    from_rows = np.eye(channels * YB).reshape(YB, channels, -1).transpose(1, 0, 2)

    def low(array):
        return array.astype(np.float32).astype(ml_dtypes.bfloat16)

    return dict(
        to_x=low(to_x.reshape(HJ * length_x, HJ * SUB)),
        from_x=low(from_x.reshape(HJ * SUB, HJ * length_x)),
        to_y=low(to_y.reshape(quarter * SUB, 2 * WIDE)),
        from_y=low(from_y.reshape(2 * WIDE, quarter * SUB)),
        turn=turn.astype(np.float32),
        to_rows=low(to_rows.reshape(channels * YB, channels * YB)),
        from_rows=low(from_rows.reshape(channels * YB, channels * YB)),
        to_z=low(np.kron(forward, eye)),
        from_z=low(np.kron(inverse, eye)),
    )


def pack(blocks):
    tail = blocks[0][:, 256:]
    for at, block in enumerate(blocks[1:], 1):
        tail = tail + pltpu.roll(block[:, 256:], at * 32, 1)
    firsts = [block[:, :128] for block in blocks]
    seconds = [block[:, 128:256] for block in blocks]
    return jnp.concatenate(firsts + seconds + [tail], 0)


def unpack(piece):
    tail = piece[64:72]
    blocks = []
    for at in range(4):
        rest = tail if at == 0 else pltpu.roll(tail, 128 - at * 32, 1)
        blocks.append(
            jnp.concatenate([piece[at * 8 : at * 8 + 8], piece[32 + at * 8 : 40 + at * 8], rest], 1)
        )
    return blocks


def send(axis, count, source, target, send_sem, recv_sem):
    me = lax.axis_index(axis)
    copies = []
    for step in range(1, count):
        peer = lax.rem(me + step, count)
        copy = pltpu.make_async_remote_copy(
            src_ref=source(peer),
            dst_ref=target(me, step),
            send_sem=send_sem.at[step],
            recv_sem=recv_sem.at[step],
            device_id={axis: peer},
            device_id_type=pl.DeviceIdType.MESH,
        )
        copy.start()
        copies.append(copy)
    return copies


def settle(copies, more):
    for copy in copies:
        copy.wait_send()
    return more


def along_x(field, first, count, to_x):
    rows = field.shape[1]
    depth, width = to_x.shape
    parts = []
    for b in range(first, first + count):
        for half in range(YB // HJ):
            parts.append(field[b, :, half * depth : (half + 1) * depth])
    along = jnp.dot(jnp.concatenate(parts, 0), to_x[...], preferred_element_type=F32).astype(BF16)
    return [along[at * rows : (at + 1) * rows] for at in range(len(parts))]


def weigh_modes(spec, weights, modal):
    share = 8
    length = weights.shape[-1]
    for start in range(0, length, 256):
        width = min(256, length - start)
        cols = slice(start, start + width)

        def group(cg, total, cols=cols, width=width):
            real, imag = total
            lines = spec[pl.ds(pl.multiple_of(cg * 16, 16), 16), cols]
            for t in range(share // 2):
                at = pl.ds(pl.multiple_of(cg * share * share + 16 * t, 16), 16)
                w_real = weights[0, at, cols].astype(F32)
                w_imag = weights[1, at, cols].astype(F32)
                parts = []
                for part in range(2):
                    rows = [
                        jnp.broadcast_to(lines[at_row : at_row + 1], (share, width))
                        for at_row in (part * share + 2 * t, part * share + 2 * t + 1)
                    ]
                    parts.append(jnp.concatenate(rows, 0))
                real = real + parts[0] * w_real - parts[1] * w_imag
                imag = imag + parts[0] * w_imag + parts[1] * w_real
            return real, imag

        zero = jnp.zeros((16, width), F32)
        real, imag = lax.fori_loop(0, spec.shape[0] // 16, group, (zero, zero), unroll=True)
        modal[:share, cols] = real[:share] + real[share:]
        modal[share:, cols] = imag[:share] + imag[share:]


def exchange_modes(spectrum, tables, weights, buffers, sems, ready):
    turn_ref, to_z, from_z, from_y = tables
    part, held_sum, all_z, all_c, spec, modal, out_z, held_z, all_o = buffers
    groups, quarters = all_z.shape[0], part.shape[0]
    share = 8
    planes = to_z.shape[2] // (2 * share * groups)
    channels = quarters * share
    kept = lax.broadcasted_iota(jnp.int32, (1, WIDE), 1) < KY * MX
    own_kz = to_z.shape[1] // (2 * share)
    g, q = lax.axis_index("gz"), lax.axis_index("gy")
    turn = turn_ref[q]
    cosine, sine = turn[0:1], turn[1:2]
    real, imag = spectrum[:, :WIDE], spectrum[:, WIDE:]
    real, imag = cosine * real + sine * imag, cosine * imag - sine * real
    for quarter in range(quarters):
        rows = []
        for z in range(planes):
            at = z * channels + quarter * share
            rows += [real[at : at + share], imag[at : at + share]]
        part[quarter] = pack(rows).astype(BF16)
    ready["greet"]()
    copies = send(
        "gy", quarters, lambda peer: part.at[peer], lambda me, step: held_sum.at[step], *sems[0]
    )
    ready["idle"]()
    total = part[q].astype(F32)
    for step, copy in enumerate(copies, 1):
        copy.wait_recv()
        total = total + held_sum[step].astype(F32)
    all_z[g] = total.astype(BF16)
    more = send("gz", groups, lambda peer: all_z.at[g], lambda me, step: all_z.at[me], *sems[1])
    copies = settle(copies, more)
    ready["to_z"]()
    for copy in more:
        copy.wait_recv()
    rows = []
    for group in range(groups):
        rows += unpack(all_z[group].astype(F32))
    rows = jnp.concatenate(rows, 0).astype(BF16)
    bins = jnp.where(kept, jnp.dot(to_z[g], rows, preferred_element_type=F32), 0.0)
    modes = KY * MX
    length = 8 * 128
    zero = jnp.zeros((share, length - WIDE), F32)
    halves = []
    for half in range(2):
        for kz in range(own_kz):
            at = (half * own_kz + kz) * share
            wide = jnp.concatenate([bins[at : at + share], zero], 1)
            if kz == 0:
                line = wide
            else:
                line = line + pltpu.roll(wide, kz * modes, 1)
        halves.append(line)
    all_c[q] = jnp.concatenate(halves, 0)[:, : all_c.shape[-1]].astype(BF16)
    more = send("gy", quarters, lambda peer: all_c.at[q], lambda me, step: all_c.at[me], *sems[2])
    copies = settle(copies, more)
    modal[...] = jnp.zeros_like(modal)
    ready["weights"]()
    for copy in more:
        copy.wait_recv()
    spec[...] = all_c[...].reshape(spec.shape).astype(F32)
    weigh_modes(spec, weights, modal)
    line = modal[...]
    rows = []
    for kz in range(own_kz):
        moved = line if kz == 0 else pltpu.roll(line, length - kz * modes, 1)
        rows.append(moved[:, :WIDE])
    rows = jnp.concatenate(rows, 0).astype(BF16)
    ready["from_z"]()
    back = jnp.dot(from_z[g], rows, preferred_element_type=F32)
    back = jnp.where(kept, back, 0.0)
    for group in range(groups):
        first = group * planes * 2 * share
        blocks = [back[first + at * share : first + (at + 1) * share] for at in range(2 * planes)]
        out_z[group] = pack(blocks).astype(BF16)
    more = send(
        "gz", groups, lambda peer: out_z.at[peer], lambda me, step: held_z.at[step], *sems[3]
    )
    copies = settle(copies, more)
    ready["from_y"]()
    total = out_z[g].astype(F32)
    for step, copy in enumerate(more, 1):
        copy.wait_recv()
        total = total + held_z[step].astype(F32)
    all_o[q] = total.astype(BF16)
    more = send("gy", quarters, lambda peer: all_o.at[q], lambda me, step: all_o.at[me], *sems[4])
    copies = settle(copies, more)
    for copy in more:
        copy.wait_recv()
    real, imag = [], []
    pieces = [unpack(all_o[quarter].astype(F32)) for quarter in range(quarters)]
    for z in range(planes):
        for piece in pieces:
            real.append(piece[2 * z])
            imag.append(piece[2 * z + 1])
    real, imag = jnp.concatenate(real, 0), jnp.concatenate(imag, 0)
    real, imag = cosine * real - sine * imag, sine * real + cosine * imag
    rows = jnp.concatenate([real, imag], 1).astype(BF16)
    result = jnp.dot(rows, from_y[...], preferred_element_type=F32).astype(BF16)
    return result, copies


def prepare_maps(skip, lift_t, bias, lift, planes):
    channels, hidden = lift_t.shape
    scaled = bias * F32(HALF)
    high = scaled.astype(BF16).astype(F32)
    middle = (scaled - high).astype(BF16).astype(F32)
    low = scaled - high - middle
    tail = jnp.zeros((128 - channels - 3, hidden), F32)
    tall = jnp.concatenate([lift_t.astype(F32), high, middle, low, tail], 0)
    lift[...] = tall.T.astype(BF16)
    blank = jnp.zeros((channels, channels), F32)
    skip = skip.astype(F32)
    block_rows = []
    for z in range(planes):
        block_rows.append(
            jnp.concatenate([skip if z == other else blank for other in range(planes)], 1)
        )
    return jnp.concatenate(block_rows, 0).astype(BF16)


def pointwise(current, rows_y, from_x, skip_all, lift, down):
    rows, length = current.shape
    channels = down.shape[0]
    planes = rows // channels
    ones = (lax.broadcasted_iota(jnp.int32, (16, planes * length), 0) < 3).astype(F32).astype(BF16)
    depth, width = from_x.shape
    halves = []
    for half in range(length // width):
        left = jnp.concatenate([rows_y[:, half * depth : (half + 1) * depth], skip_all], 1)
        right = jnp.concatenate([from_x[...], current[:, half * width : (half + 1) * width]], 0)
        halves.append(jnp.dot(left, right, preferred_element_type=F32))
    mixed = jnp.concatenate(halves, 1)
    lower = (mixed * F32(HALF)).astype(BF16)
    wide = jnp.concatenate([lower[z * channels : (z + 1) * channels] for z in range(planes)], 1)
    wide = jnp.concatenate([wide, ones], 0)
    value = jnp.dot(lift[:, : channels + 16], wide, preferred_element_type=F32)
    value = (value + value * lax.erf(value)).astype(BF16)
    change = jnp.dot(down, value, preferred_element_type=F32) * F32(HALF)
    return [
        (mixed[z * channels : (z + 1) * channels] + change[:, z * length : (z + 1) * length]).astype(BF16)
        for z in range(planes)
    ]


def meet(groups, quarters):
    barrier = pltpu.get_barrier_semaphore()
    for axis, count in (("gz", groups), ("gy", quarters)):
        me = lax.axis_index(axis)
        for step in range(1, count):
            pl.semaphore_signal(
                barrier,
                inc=1,
                device_id={axis: lax.rem(me + step, count)},
                device_id_type=pl.DeviceIdType.MESH,
            )
    return lambda: pl.semaphore_wait(barrier, groups + quarters - 2)


def loads(pairs, sem):
    copies = [
        pltpu.make_async_copy(source, target, sem.at[at])
        for at, (source, target) in enumerate(pairs)
    ]
    for copy in copies:
        copy.start()
    return copies


def modes_kernel(
    sizes, raw_hbm, to_rows_hbm, to_x_hbm, to_y_hbm, weights_hbm, from_y_hbm, from_x_hbm,
    turn_hbm, to_z_hbm, from_z_hbm, skip_hbm, lift_t_hbm, bias_hbm, down_hbm,
    rows_out, field_hbm, raw, to_rows, to_x, to_y, weights, from_y, from_x, turn, to_z, from_z,
    skip, lift_t, bias, down, field, later, lift, skip_all, rows_y, local_sem, late_sem, out_sem, *rest,
):
    groups, quarters = sizes
    layers = weights_hbm.shape[0]
    greeting = meet(groups, quarters)
    channels, planes, quarter, length_x = raw.shape
    lines = 2 * YB
    pieces = quarter // lines
    copies = loads(
        [(to_rows_hbm, to_rows)]
        + [
            (raw_hbm.at[:, :, pl.ds(at * lines, lines)], raw.at[:, :, pl.ds(at * lines, lines)])
            for at in range(pieces)
        ]
        + [(to_x_hbm, to_x), (to_y_hbm, to_y), (turn_hbm, turn)],
        local_sem,
    )
    copies[0].wait()
    along = []
    for at in range(pieces):
        copies[1 + at].wait()
        if at == 1:
            copies[1 + pieces].wait()
        for z in range(planes):
            block = raw[:, z, at * lines : (at + 1) * lines, :].astype(F32)
            for half in range(2):
                eight = block[:, half * YB : (half + 1) * YB].reshape(channels * YB, length_x)
                turned = jnp.dot(
                    to_rows[...], eight.astype(BF16), preferred_element_type=F32
                ).astype(BF16)
                for j in range(YB):
                    field[
                        at * 2 + half,
                        z * channels : (z + 1) * channels,
                        j * length_x : (j + 1) * length_x,
                    ] = turned[j * channels : (j + 1) * channels]
        if at > 0:
            along += along_x(field, 2 * at - 2, 2, to_x)
    along += along_x(field, 2 * pieces - 2, 2, to_x)
    for copy in copies[2 + pieces :]:
        copy.wait()
    waits = loads(
        [(to_z_hbm, to_z)]
        + [(weights_hbm.at[layer], weights.at[layer]) for layer in range(layers)]
        + [(from_z_hbm, from_z), (from_y_hbm, from_y), (from_x_hbm, from_x)]
        + [(skip_hbm, skip), (lift_t_hbm, lift_t), (bias_hbm, bias), (down_hbm, down)],
        late_sem,
    )
    current, sent = field, []
    for layer in range(layers):
        if layer > 0:
            along = []
            source, current = current, (later if layer % 2 else field)
            for first in range(0, quarter // YB, 2):
                parts = pointwise(
                    jnp.concatenate([source[b] for b in range(first, first + 2)], 1),
                    rows_y[:, first * YB * SUB : (first + 2) * YB * SUB], from_x, skip_all[...],
                    lift, down[layer - 1],
                )
                for z, part in enumerate(parts):
                    for b in range(2):
                        current[first + b, z * channels : (z + 1) * channels, :] = part[
                            :, b * YB * length_x : (b + 1) * YB * length_x
                        ]
                along += along_x(current, first, 2, to_x)
            if layer == layers - 1:
                leave = pltpu.make_async_copy(current, field_hbm, out_sem.at[0])
                leave.start()
        spectrum = jnp.dot(jnp.concatenate(along, 1), to_y[...], preferred_element_type=F32)
        buffers = rest[9 * layer : 9 * layer + 9]
        at = 9 * layers + 10 * layer
        sems = [(rest[at + 2 * phase], rest[at + 2 * phase + 1]) for phase in range(5)]
        nothing = lambda: None

        def idle(layer=layer, before=sent):
            for copy in before:
                copy.wait_send()
            if layer == 0:
                for copy in waits[layers + 3 :]:
                    copy.wait()
            if layer < layers - 1:
                skip_all[...] = prepare_maps(
                    skip[layer], lift_t[layer], bias[layer : layer + 1], lift, planes
                )

        ready = {
            "greet": nothing if layer else greeting,
            "idle": idle,
            "to_z": nothing if layer else waits[0].wait,
            "weights": waits[1 + layer].wait,
            "from_z": nothing if layer else waits[layers + 1].wait,
            "from_y": nothing if layer else waits[layers + 2].wait,
        }
        rows, sent = exchange_modes(
            spectrum, (turn, to_z, from_z, from_y), weights.at[layer], buffers, sems, ready
        )
        if layer == layers - 1:
            rows_out[...] = rows
        else:
            rows_y[...] = rows
    for copy in sent:
        copy.wait_send()
    leave.wait()


def last_kernel(
    layer, field_hbm, rows_hbm, from_x_hbm, from_rows_hbm, skip_hbm, lift_t_hbm, bias_hbm,
    down_hbm, out_hbm, rows_y, from_x, from_rows, skip, lift_t, bias, down, field, lift, result,
    in_sem, out_sem,
):
    blocks = field.shape[0]
    channels, planes, _, length_x = result.shape
    lines = 2 * YB
    steps = blocks // 2
    copies = loads(
        [
            (skip_hbm, skip), (lift_t_hbm, lift_t), (bias_hbm, bias), (down_hbm, down),
            (rows_hbm, rows_y), (from_x_hbm, from_x), (from_rows_hbm, from_rows),
        ]
        + [(field_hbm.at[pl.ds(2 * at, 2)], field.at[pl.ds(2 * at, 2)]) for at in range(steps)],
        in_sem,
    )
    for copy in copies[:7]:
        copy.wait()
    copies = copies[7:]
    skip_all = prepare_maps(skip[layer], lift_t[layer], bias[layer : layer + 1], lift, planes)
    outs = []
    for first in range(0, blocks, 4):
        for at in range(first // 2, (first + 4) // 2):
            copies[at].wait()
        group = range(first, first + 4)
        both = pointwise(
            jnp.concatenate([field[b] for b in group], 1),
            rows_y[:, first * YB * SUB : (first + 4) * YB * SUB], from_x, skip_all, lift,
            down[layer],
        )
        for at in range(first // 2, (first + 4) // 2):
            window = pl.ds(at * lines, lines)
            for z, part in enumerate(both):
                turned = []
                for b in (2 * at, 2 * at + 1):
                    rows = [
                        part[:, j * length_x : (j + 1) * length_x]
                        for j in range((b - first) * YB, (b - first + 1) * YB)
                    ]
                    tall = jnp.concatenate(rows, 0)
                    tall = jnp.dot(from_rows[...], tall, preferred_element_type=F32)
                    turned.append(tall.reshape(channels, YB, length_x))
                result[:, z, window, :] = jnp.concatenate(turned, 1).astype(BF16)
            copy = pltpu.make_async_copy(
                result.at[:, :, window], out_hbm.at[:, :, window], out_sem.at[at]
            )
            copy.start()
            outs.append(copy)
    for copy in outs:
        copy.wait()


def fast_device(noisy_field, spectral_weights, skip_weights, in_weights, in_bias, out_weights):
    channels, planes, quarter, length_x = noisy_field.shape
    layer_count = spectral_weights.shape[0]
    groups, quarters = lax.axis_size("gz"), lax.axis_size("gy")
    own_kz = KZ // groups
    own_modes = spectral_weights.shape[2]
    share = channels // quarters
    blocks = quarter // YB
    hidden = in_weights.shape[1]
    tables = np_tables(groups, quarters, planes, quarter, length_x, channels)
    tables = {name: jnp.asarray(value) for name, value in tables.items()}
    weights = spectral_weights.transpose(0, 1, 3, 4, 2)
    weights = weights.reshape(layer_count, 2, channels * share, own_modes)
    lift_t = in_weights.transpose(0, 2, 1)
    rows_shape = jax.ShapeDtypeStruct((planes * channels, quarter * SUB), BF16)
    field_shape = jax.ShapeDtypeStruct((blocks, planes * channels, YB * length_x), BF16)
    anywhere = pl.BlockSpec(memory_space=pltpu.HBM)
    vmem = pl.BlockSpec(memory_space=pltpu.VMEM)

    def held(name):
        return pltpu.VMEM(tables[name].shape, tables[name].dtype)

    full = -(-own_modes // 128) * 128
    block = (planes * 2 * share * 2 + share, 128)
    traffic = [
        pltpu.VMEM((quarters,) + block, BF16),
        pltpu.VMEM((quarters,) + block, BF16),
        pltpu.VMEM((groups,) + block, BF16),
        pltpu.VMEM((quarters, 2 * share, full), BF16),
        pltpu.VMEM((quarters * 2 * share, full), F32),
        pltpu.VMEM((2 * share, 8 * 128), F32),
        pltpu.VMEM((groups,) + block, BF16),
        pltpu.VMEM((groups,) + block, BF16),
        pltpu.VMEM((quarters,) + block, BF16),
    ]
    signals = []
    for count in (quarters, groups, quarters, groups, quarters):
        signals += [pltpu.SemaphoreType.DMA((count,))] * 2
    lift_held = pltpu.VMEM((hidden, 128), BF16)
    field_held = pltpu.VMEM(field_shape.shape, BF16)
    raw_held = pltpu.VMEM(noisy_field.shape, BF16)
    maps = (skip_weights, lift_t, in_bias, out_weights)
    maps_held = [pltpu.VMEM(value.shape, value.dtype) for value in maps]
    pieces = quarter // (2 * YB)
    rows, field = pl.pallas_call(
        functools.partial(modes_kernel, (groups, quarters)),
        out_shape=[rows_shape, field_shape],
        in_specs=[anywhere] * 14,
        out_specs=[vmem, anywhere],
        scratch_shapes=[
            raw_held, held("to_rows"), held("to_x"), held("to_y"),
            pltpu.VMEM(weights.shape, BF16), held("from_y"), held("from_x"),
            held("turn"), held("to_z"), held("from_z"), *maps_held, field_held, field_held, lift_held,
            pltpu.VMEM((planes * channels, planes * channels), BF16), pltpu.VMEM(rows_shape.shape, BF16),
            pltpu.SemaphoreType.DMA((4 + pieces,)), pltpu.SemaphoreType.DMA((8 + layer_count,)),
            pltpu.SemaphoreType.DMA((1,)),
        ] + traffic * layer_count + signals * layer_count,
        compiler_params=pltpu.CompilerParams(
            collective_id=0, has_side_effects=True, vmem_limit_bytes=VMEM_LIMIT
        ),
        name="modes",
    )(
        noisy_field, tables["to_rows"], tables["to_x"], tables["to_y"], weights, tables["from_y"],
        tables["from_x"], tables["turn"], tables["to_z"], tables["from_z"], *maps,
    )
    return pl.pallas_call(
        functools.partial(last_kernel, layer_count - 1),
        out_shape=jax.ShapeDtypeStruct(noisy_field.shape, BF16),
        in_specs=[anywhere, pl.BlockSpec(memory_space=pl.ANY)] + [anywhere] * 6,
        out_specs=anywhere,
        scratch_shapes=[
            pltpu.VMEM(rows_shape.shape, BF16), held("from_x"), held("from_rows"), *maps_held,
            field_held, lift_held, raw_held, pltpu.SemaphoreType.DMA((7 + pieces,)),
            pltpu.SemaphoreType.DMA((pieces,)),
        ],
        compiler_params=pltpu.CompilerParams(vmem_limit_bytes=VMEM_LIMIT),
        name="last_layer",
    )(field, rows, tables["from_x"], tables["from_rows"], *maps)


def pick(noisy_field, spectral_weights, *rest):
    groups, quarters = lax.axis_size("gz"), lax.axis_size("gy")
    channels, planes, quarter, _ = noisy_field.shape
    fits = (
        KZ % groups == 0
        and spectral_weights.shape[2] == KZ // groups * KY * MX
        and spectral_weights.shape[2] <= 8 * 128 - 128
        and channels == 8 * quarters
        and planes == 2
        and quarter % (4 * YB) == 0
    )
    body = fast_device if fits else per_device
    return body(noisy_field, spectral_weights, *rest)


def solution(mesh):
    in_specs = (P(None, "gz", "gy", None), P(None, None, "gz", None, "gy"), P(), P(), P(), P())
    out_specs = P(None, "gz", "gy", None)
    return jax.shard_map(
        pick, mesh=mesh, in_specs=in_specs, out_specs=out_specs, check_vma=False
    )
```
